32 devices in a mesh: parts: 2 (over y), wide: 4 (over z), narrow: 4 (over x, core).
Axes of the slice: x: 2, y: 2, z: 4, core: 2. Of those that a mesh axis runs over, the one named last changes fastest.
Arguments:
- embeddings: bfloat16 [8192, 1024], P(('parts', 'wide', 'narrow')), parts along dimension 0, may hold values from -6 to 6
- cluster_id: int32 [8192], P(('parts', 'wide', 'narrow')), parts along dimension 0, may hold values from 0 to 63, as said below
- order_index: int32 [8192], P(('parts', 'wide', 'narrow')), parts along dimension 0, may hold values from 0 to 2047, as said below
Outputs:
- nearest: float32 [8192], P(('parts', 'wide', 'narrow')), parts along dimension 0
The draws below stay inside these ranges and needn't reach their ends.
There are 2 independent parts, one for each index of `parts`. The reference program is written for one: setup_inputs(seed, part) draws one part's arguments, and reference() takes and returns one part's arrays. A program takes and returns all parts, laid end to end along the dimension named above; each array names one. Nothing has to cross between parts.
Inputs may be any that keep to these rules, and one draw needn't show every extreme that they name: `cluster_id`: cluster c belongs to owner c // 16 of wide; among the members held by one device at most 128 belong to clusters of one owner, and in every draw one owner gets exactly 128 from every device. `order_index`: the members of each cluster carry the distinct numbers 0, 1, 2, ... up to its size less one; in every draw some cluster holds 4 * 4 * 128 members.
All inputs are finite; a program needn't handle non-finite values.
Results may differ from the reference program's by a relative error of at most 0.00099.
Values may be sent and summed in bfloat16 or wider, within the bound.
A program may use at most 64 MiB of HBM per device.

```python
import math
import jax
import jax.numpy as jnp
from jax import lax

D = 1024
CPO = 16
M_DEV = 256
CAP = 128
MEMBERS = 4096
N_WIDE = 4
N_NARROW = 4


def members_layout(key):
    base = jax.random.fold_in(key, 11)
    k_full, k_perm, k_mix, k_first, k_second, k_turn, k_rank = jax.random.split(base, 7)
    devices = N_WIDE * N_NARROW
    slots = N_WIDE * CAP
    total = devices * M_DEV
    full_owner = jax.random.randint(k_full, (), 0, N_WIDE)
    slot_owner = jnp.arange(slots, dtype=jnp.int32) // CAP
    perms = jax.vmap(lambda k: jax.random.permutation(k, slots))(jax.random.split(k_perm, devices))
    score = perms.astype(jnp.int32) - jnp.where(slot_owner == full_owner, slots, 0).astype(jnp.int32)[None, :]
    chosen = jnp.argsort(score, axis=1)[:, :M_DEV]
    mixing = jax.vmap(lambda k: jax.random.permutation(k, M_DEV))(jax.random.split(k_mix, devices))
    chosen = jnp.take_along_axis(chosen, mixing, axis=1)
    owner = (chosen // CAP).reshape(total).astype(jnp.int32)
    first = jax.random.randint(k_first, (total,), 0, CPO)
    second = jax.random.randint(k_second, (total,), 0, CPO)
    turn = jax.random.randint(k_turn, (N_WIDE,), 0, CPO)
    spread = (first * second // CPO + turn[owner]) % CPO
    local = jnp.where(owner == full_owner, turn[owner], spread)
    cluster = (owner * CPO + local).astype(jnp.int32)
    ranks = jax.random.permutation(k_rank, total).astype(jnp.int32)
    sort_key = cluster * total + ranks
    index = jnp.argsort(sort_key)
    position = jnp.zeros((total,), jnp.int32).at[index].set(jnp.arange(total, dtype=jnp.int32))
    counts = jax.ops.segment_sum(jnp.ones((total,), jnp.int32), cluster, num_segments=N_WIDE * CPO)
    starts = jnp.cumsum(counts) - counts
    order = position - starts[cluster]
    return (cluster, order.astype(jnp.int32))


def draw_cluster_id(key, part):
    return members_layout(key)[0]


def draw_order_index(key, part):
    return members_layout(key)[1]


def block_scale(key, dims, shards, least, top_value):
    factor_of, own = 1.0, jax.random.fold_in(key, 6)
    for dim, parts in shards:
        heights = jnp.exp(jax.random.uniform(jax.random.fold_in(own, dim), (parts,), jnp.float32, least / len(shards), top_value / len(shards)))
        factor_of = factor_of * jnp.repeat(heights, dims[dim] // parts).reshape([-1 if axis == dim else 1 for axis in range(len(dims))])
    return factor_of


def gaussian(rng, dims, deviation, limit, pieces=(), kind=jnp.bfloat16):
    array = jax.random.normal(rng, dims, jnp.float32) * deviation
    if len(pieces) > 0:
        array = block_scale(rng, dims, pieces, -0.22, 0.18) * array
    return jnp.clip(array, min=-limit, max=limit).astype(kind)


def setup_inputs(seed: int = 0, part: int = 0) -> dict:
    splits = jax.random.split(jax.random.key(seed), 4)
    part_keys = jax.random.split(jax.random.fold_in(splits[3], part), 4)
    embeddings = gaussian(part_keys[0], (MEMBERS, D), 1.0, 6.0, ((0, 16),))
    cluster_id = draw_cluster_id(jax.random.fold_in(jax.random.fold_in(splits[3], part), 71), part)
    order_index = draw_order_index(jax.random.fold_in(jax.random.fold_in(splits[3], part), 71), part)
    return {"embeddings": embeddings, "cluster_id": cluster_id, "order_index": order_index}


def reference(embeddings, cluster_id, order_index):
    values = embeddings.astype(jnp.float32)
    unit = (values * lax.rsqrt(lax.optimization_barrier(jnp.sum(values * values, axis=1, keepdims=True)) + 1e-06)).astype(jnp.bfloat16)
    total = unit.shape[0]
    width = unit.shape[1]
    window = N_WIDE * N_NARROW * (2 * M_DEV // N_WIDE)
    block = math.gcd(total, 512)
    sort_key = cluster_id * total + order_index
    perm = jnp.argsort(sort_key).astype(jnp.int32)
    sorted_rows = unit[perm].astype(jnp.float32)
    sorted_cl = cluster_id[perm]
    sorted_or = order_index[perm]
    padded_rows = jnp.concatenate([jnp.zeros((window, width), jnp.float32), sorted_rows], axis=0)
    padded_cl = jnp.concatenate([jnp.full((window,), -1, jnp.int32), sorted_cl], axis=0)
    padded_or = jnp.concatenate([jnp.zeros((window,), jnp.int32), sorted_or], axis=0)

    def one_block(index):
        start = (index * block).astype(jnp.int32)
        query = lax.dynamic_slice_in_dim(sorted_rows, start, block, 0)
        query_cl = lax.dynamic_slice_in_dim(sorted_cl, start, block, 0)
        query_or = lax.dynamic_slice_in_dim(sorted_or, start, block, 0)
        keys = lax.dynamic_slice_in_dim(padded_rows, start, window + block, 0)
        keys_cl = lax.dynamic_slice_in_dim(padded_cl, start, window + block, 0)
        keys_or = lax.dynamic_slice_in_dim(padded_or, start, window + block, 0)
        inner = jnp.dot(query, keys.T, precision=lax.Precision.HIGHEST)
        allowed = (keys_cl[None, :] == query_cl[:, None]) & (keys_or[None, :] < query_or[:, None])
        return lax.optimization_barrier(jnp.max(jnp.where(allowed, inner, -1.0), axis=1))
    found = lax.map(one_block, jnp.arange(total // block, dtype=jnp.int32)).reshape(total)
    return jnp.zeros((total,), found.dtype).at[perm].set(found)
```

```python
import jax
import jax.numpy as jnp
from jax import lax
from jax.experimental import pallas as pl
from jax.experimental.pallas import tpu as pltpu
from jax.sharding import PartitionSpec as P

CPO = 16


def shifted(shard, axis, by):
    count = lax.axis_size(axis)
    return lax.ppermute(shard, axis, [(i, (i + by) % count) for i in range(count)])


def pair_inner(left, right):
    return lax.dot_general(
        left, right, (((1,), (1,)), ((), ())), preferred_element_type=jnp.float32
    )


def per_device(embeddings, cluster_id, order_index):
    wide_size = lax.axis_size("wide")
    rows = embeddings.shape[0]
    width = embeddings.shape[1]
    bucket = 2 * rows // wide_size
    values = embeddings.astype(jnp.float32)
    unit = (values * lax.rsqrt(jnp.sum(values * values, axis=1, keepdims=True) + 1e-06)).astype(
        jnp.bfloat16
    )
    owner = cluster_id // CPO
    here = jnp.arange(rows, dtype=jnp.int32)
    earlier = (owner[:, None] == owner[None, :]) & (here[None, :] < here[:, None])
    slot = jnp.sum(jnp.where(earlier, 1, 0), axis=1)
    target = owner * bucket + slot
    send_rows = jnp.zeros((wide_size * bucket, width), jnp.bfloat16).at[target].set(unit)
    meta_rows = jnp.stack([cluster_id, order_index], axis=1)
    send_meta = jnp.full((wide_size * bucket, 2), -1, jnp.int32).at[target].set(meta_rows)
    held, held_meta = (
        lax.all_to_all(send_rows, "wide", split_axis=0, concat_axis=0, tiled=True),
        lax.all_to_all(send_meta, "wide", split_axis=0, concat_axis=0, tiled=True),
    )
    held_cl = held_meta[:, 0]
    held_or = held_meta[:, 1]
    live = held_cl >= 0
    start_best = jnp.full((held.shape[0],), -1.0, jnp.float32)

    def row_best(inner, other_cl, other_or):
        allowed = (
            (other_cl[None, :] == held_cl[:, None])
            & (other_or[None, :] < held_or[:, None])
            & live[:, None]
        )
        return jnp.max(jnp.where(allowed, inner, -1.0), axis=1)

    narrow_size = lax.axis_size("narrow")
    best = jnp.maximum(start_best, row_best(pair_inner(held, held), held_cl, held_or))
    for distance in range(1, narrow_size // 2 + 1):
        other_rows, other_meta = shifted((held, held_meta), "narrow", distance)
        other_cl = other_meta[:, 0]
        other_or = other_meta[:, 1]
        inner = pair_inner(held, other_rows)
        best = jnp.maximum(best, row_best(inner, other_cl, other_or))
        column_ok = (
            (held_cl[:, None] == other_cl[None, :])
            & (held_or[:, None] < other_or[None, :])
            & (other_cl[None, :] >= 0)
        )
        column_best = jnp.max(jnp.where(column_ok, inner, -1.0), axis=0)
        returned = shifted(column_best, "narrow", -distance)
        best = jnp.maximum(best, returned)
    answers = lax.all_to_all(best, "wide", split_axis=0, concat_axis=0, tiled=True)
    return answers[target]


CHUNKS = 4
SIDE = 4
MESH = pl.DeviceIdType.MESH


def meet_kernel(emb_far, cl, od, out, emb, got, qraw, uq, acl, qod, pk, pm, kbuf, kmeta, target, racc, rres, cacc, cres, cfull,
                xs, xr, fs, fr, cs, cr, als, alr, ods, odr, zs, zr, zms, zmr, rs, rr, ts, tr):
    w = lax.axis_index("wide")
    n = lax.axis_index("narrow")
    near = n + 1 - 2 * lax.rem(n, 2)
    cross = lax.rem(n + 2, SIDE)
    far = lax.rem(near + 2, SIDE)
    peers = (near, cross, far)
    mate = w + 1 - 2 * lax.rem(w, 2)
    over = SIDE - 1 - w
    over_mate = over + 1 - 2 * lax.rem(over, 2)
    outer = (w == 0) | (w == SIDE - 1)
    inner = (w > 0) & (w < SIDE - 1)
    rows = emb.shape[0]
    half = rows // 2
    f32 = jnp.float32

    def send(s, d, ss, rs_, **who):
        return pltpu.make_async_remote_copy(s, d, ss, rs_, device_id=who, device_id_type=MESH)

    others = [(a, b) for a in range(SIDE) for b in range(SIDE) if a or b]
    barrier = pltpu.get_barrier_semaphore()
    for a, b in others:
        pl.semaphore_signal(
            barrier, inc=1, device_id={"wide": lax.rem(w + a, SIDE), "narrow": lax.rem(n + b, SIDE)}, device_id_type=MESH
        )
    take = pltpu.make_async_copy(emb_far, emb, got)
    take.start()
    pl.semaphore_wait(barrier, len(others))

    x_part = [pl.ds(c * (rows // CHUNKS), rows // CHUNKS) for c in range(CHUNKS)]
    z_part = [pl.ds(c * (half // CHUNKS), half // CHUNKS) for c in range(CHUNKS)]

    ids = [
        send(cl, acl.at[a * SIDE + b], als.at[a * SIDE + b], alr.at[a * SIDE + b],
             wide=lax.rem(w + a, SIDE), narrow=lax.rem(n + b, SIDE))
        for a, b in others
    ]
    orders = [send(od, qod.at[b - 1], ods.at[b - 1], odr.at[b - 1], narrow=lax.rem(n + b, SIDE)) for b in range(1, SIDE)]
    xc = [send(emb.at[p], qraw.at[1, p], xs.at[c], xr.at[c], narrow=cross) for c, p in enumerate(x_part)]
    cc = send(emb, qraw.at[0], cs, cr, narrow=near)
    fc = [send(qraw.at[1, p], qraw.at[2, p], fs.at[c], fr.at[c], narrow=near) for c, p in enumerate(x_part)]
    for c in ids[::-1] + orders:
        c.start()
    take.wait()
    for c in xc + [cc]:
        c.start()

    def normed(ref):
        values = ref[...].astype(f32)
        return (values * lax.rsqrt(jnp.sum(values * values, axis=1, keepdims=True) + 1e-06)).astype(jnp.bfloat16)

    def tall(row, across):
        return jnp.broadcast_to(row, (across, row.shape[1])).T

    def asked(j):
        if j == 0:
            return cl[...].astype(f32), od[...].astype(f32)
        if j == 2:
            return acl[2].astype(f32), qod[1].astype(f32)
        even = lax.rem(n, 2) == 0
        low, high = (3, 1) if j == 1 else (1, 3)
        slot = jnp.where(even, low, high)
        return acl[slot].astype(f32), qod[slot - 1].astype(f32)

    uq[0] = normed(emb)
    own_cl = tall(cl[...].astype(f32), rows)
    own_od = tall(od[...].astype(f32), rows)

    def own_part(j):
        q_cl, q_od = asked(j)
        ok = (own_cl == q_cl) & (own_od < q_od)
        racc[j] = jnp.max(jnp.where(ok, pair_inner(uq[0], uq[j]), -1.0), axis=0, keepdims=True)

    own_part(0)
    acl[0] = cl[...]
    for c in ids + orders:
        c.wait_recv()

    all_cl = acl[...].astype(f32)
    full = jnp.zeros((1, 1), f32)
    for o in range(SIDE)[::-1]:
        mine = (all_cl >= o * CPO) & (all_cl < (o + 1) * CPO)
        count = jnp.sum(jnp.where(mine, 1.0, 0.0), axis=2, keepdims=True)
        good = jnp.min(jnp.where(count == half, 1.0, 0.0), axis=0)
        full = jnp.where(good > 0.5, jnp.float32(o), full)
    id_row = cl[...].astype(f32)
    od_row = od[...].astype(f32)
    heavy = jnp.where((id_row >= full * CPO) & (id_row < (full + 1.0) * CPO), 1.0, 0.0)
    away = jnp.where(w < SIDE // 2, heavy, 1.0 - heavy)
    deep = lax.broadcasted_iota(jnp.int32, (rows, rows), 0)
    long = lax.broadcasted_iota(jnp.int32, (rows, rows), 1)
    tri = jnp.where(deep < long, 1.0, 0.0).astype(jnp.bfloat16)
    rank = jnp.dot(jnp.broadcast_to(away, (16, rows)).astype(jnp.bfloat16), tri, preferred_element_type=f32)[0:1]
    lane = lax.broadcasted_iota(jnp.int32, (1, rows), 1).astype(f32)
    place = jnp.where(away > 0.5, rank, half + lane - rank)
    target[...] = place
    pick = jnp.where(deep.astype(f32) == place, 1.0, 0.0).astype(jnp.bfloat16)
    od_high = jnp.floor(od_row * (1.0 / 128))
    od_low = od_row - od_high * 128
    tags = [jnp.broadcast_to(r, (16, rows)).astype(jnp.bfloat16) for r in (id_row, od_high, od_low)]
    tagged = [pair_inner(t, pick)[0:1] for t in tags]
    moved = jnp.concatenate([tagged[0], tagged[1] * 128 + tagged[2]], axis=0)
    pm[0] = moved[:, :half]
    pm[1] = moved[:, half:]
    for s in range(2):
        pk[s] = jnp.dot(pick[s * half:(s + 1) * half], uq[0], preferred_element_type=f32).astype(jnp.bfloat16)

    def row_of(src, dst, ss, slot, who):
        return [send(src.at[p], kbuf.at[dst, p], zs.at[ss, c], zr.at[slot, c], wide=who) for c, p in enumerate(z_part)]

    out_away = row_of(pk.at[0], 2, 0, 2, mate)
    out_home = row_of(pk.at[1], 3, 1, 3, mate)
    in_away = row_of(pk.at[0], 0, 0, 0, over)
    in_next = row_of(kbuf.at[2], 1, 1, 1, over)
    on_near = row_of(kbuf.at[0], 0, 2, 0, mate)
    on_far = row_of(kbuf.at[1], 1, 3, 1, mate)

    def tag_of(src, dst, ss, who):
        return send(src, kmeta.at[dst], zms.at[ss], zmr.at[dst], wide=who)

    t_out_away = tag_of(pm.at[0], 2, 0, mate)
    t_out_home = tag_of(pm.at[1], 3, 1, mate)
    t_in_away = tag_of(pm.at[0], 0, 0, over)
    t_in_next = tag_of(kmeta.at[2], 1, 1, over)
    t_on_near = tag_of(kmeta.at[0], 0, 2, mate)
    t_on_far = tag_of(kmeta.at[1], 1, 3, mate)

    @pl.when(outer)
    def _():
        t_out_away.start()
        t_out_home.start()
        for c in out_away + out_home:
            c.start()

    @pl.when(inner)
    def _():
        t_in_away.start()
        for c in in_away:
            c.start()

    cc.wait_recv()
    uq[1] = normed(qraw.at[0])
    own_part(1)

    @pl.when(inner)
    def _():
        t_out_away.wait_recv()
        t_in_next.start()
        t_in_away.wait_recv()
        t_on_near.start()

    for c in range(CHUNKS):
        xc[c].wait_recv()
        fc[c].start()

        @pl.when(inner)
        def _():
            out_away[c].wait_recv()
            in_next[c].start()
            in_away[c].wait_recv()
            on_near[c].start()

    uq[2] = normed(qraw.at[1])
    own_part(2)

    @pl.when(inner)
    def _():
        t_in_next.wait_recv()
        t_on_far.start()
        in_next[0].wait_recv()
        on_far[0].start()

    for c in fc:
        c.wait_recv()
    uq[3] = normed(qraw.at[2])
    own_part(3)

    def met_by(slot, ready=None):
        k_cl = tall(kmeta[slot][0:1], rows)
        k_od = tall(kmeta[slot][1:2], rows)
        quarter = half // 2
        cols = []
        for b in range(2):
            if ready is not None:
                for c in ready[b * CHUNKS // 2:(b + 1) * CHUNKS // 2]:
                    c.wait_recv()
            span = slice(b * quarter, (b + 1) * quarter)
            keys = kbuf[slot, span]
            col = jnp.full((quarter, rows), -1.0, f32)
            for j in range(4):
                q_cl, q_od = asked(j)
                same = jnp.where(k_cl[span] == q_cl, pair_inner(keys, uq[j]), -1.0)
                before = k_od[span] < q_od
                racc[j] = jnp.maximum(racc[j], jnp.max(jnp.where(before, same, -1.0), axis=0, keepdims=True))
                col = jnp.maximum(col, jnp.where(before, -1.0, same))
            cols.append(col)
        cacc[slot] = jnp.max(jnp.concatenate(cols, axis=0).T, axis=0, keepdims=True)

    def back(slot, dst, who):
        return send(cacc.at[slot], cres.at[dst], ts.at[slot], tr.at[dst], wide=who)

    b_in = [back(0, 0, over), back(1, 0, over_mate), back(2, 2, mate), back(3, 3, mate)]
    b_out = [back(0, 1, over_mate), back(1, 1, over)]

    @pl.when(inner)
    def _():
        in_next[1].wait_recv()
        on_far[1].start()
        met_by(0)
        b_in[0].start()
        for c in range(2, CHUNKS):
            in_next[c].wait_recv()
            on_far[c].start()
        met_by(1)
        b_in[1].start()
        t_out_home.wait_recv()
        for c in out_home:
            c.wait_recv()
        met_by(2)
        b_in[2].start()
        met_by(3)
        b_in[3].start()

    @pl.when(outer)
    def _():
        t_on_near.wait_recv()
        for c in on_near:
            c.wait_recv()
        met_by(0)
        b_out[0].start()
        t_on_far.wait_recv()
        met_by(1, on_far)
        b_out[1].start()

    rowb = [send(racc.at[j + 1], rres.at[j], rs.at[j], rr.at[j], narrow=peers[j]) for j in range(3)]
    for c in rowb:
        c.start()
    for c in rowb:
        c.wait_recv()
    b_in[0].wait_recv()
    b_out[0].wait_recv()
    cfull[:, :half] = jnp.maximum(cres[0], cres[1])
    cfull[:, half:] = jnp.full((1, half), -1.0, f32)

    @pl.when(outer)
    def _():
        b_in[2].wait_recv()
        b_in[3].wait_recv()
        cfull[:, :half] = jnp.maximum(cfull[:, :half], cres[2])
        cfull[:, half:] = cres[3]

    mine = jnp.where(deep.astype(f32) == target[...], tall(cfull[...], rows), -1.0)
    best = jnp.maximum(jnp.maximum(racc[0], rres[0]), jnp.maximum(rres[1], rres[2]))
    out[...] = jnp.maximum(best, jnp.max(mine, axis=0, keepdims=True))

    @pl.when(outer)
    def _():
        for c in [t_out_away, t_out_home] + out_away + out_home + b_out:
            c.wait_send()

    @pl.when(inner)
    def _():
        for c in [t_in_away, t_in_next, t_on_near, t_on_far] + in_away + in_next + on_near + on_far + b_in:
            c.wait_send()

    for c in ids + orders + xc + [cc] + fc + rowb:
        c.wait_send()


def per_device_meet(embeddings, cluster_id, order_index):
    rows, width = embeddings.shape
    half = rows // 2
    dma = pltpu.SemaphoreType.DMA
    vmem = pl.BlockSpec(memory_space=pltpu.VMEM)
    line = lambda k, m: pltpu.VMEM((k, 1, m), jnp.float32)
    block = lambda k, m: pltpu.VMEM((k, m, width), jnp.bfloat16)
    found = pl.pallas_call(
        meet_kernel,
        out_shape=jax.ShapeDtypeStruct((1, rows), jnp.float32),
        in_specs=[pl.BlockSpec(memory_space=pl.ANY), vmem, vmem],
        out_specs=vmem,
        scratch_shapes=[
            pltpu.VMEM((rows, width), jnp.bfloat16), dma, block(3, rows), block(4, rows),
            pltpu.VMEM((SIDE * SIDE, 1, rows), jnp.int32), pltpu.VMEM((3, 1, rows), jnp.int32),
            block(2, half), pltpu.VMEM((2, 2, half), jnp.float32),
            block(4, half), pltpu.VMEM((4, 2, half), jnp.float32),
            pltpu.VMEM((1, rows), jnp.float32),
            line(4, rows), line(3, rows), line(4, half), line(4, half), pltpu.VMEM((1, rows), jnp.float32),
            dma((CHUNKS,)), dma((CHUNKS,)), dma((CHUNKS,)), dma((CHUNKS,)), dma, dma,
            dma((SIDE * SIDE,)), dma((SIDE * SIDE,)), dma((3,)), dma((3,)),
            dma((4, CHUNKS)), dma((4, CHUNKS)), dma((4,)), dma((4,)),
            dma((3,)), dma((3,)), dma((4,)), dma((4,)),
        ],
        compiler_params=pltpu.CompilerParams(collective_id=0, has_side_effects=True),
    )(embeddings, cluster_id.reshape(1, rows), order_index.reshape(1, rows))
    return jnp.maximum(found.reshape(rows), -1.0)


def solution(mesh):
    meet = mesh.shape["wide"] == SIDE and mesh.shape["narrow"] == SIDE
    return jax.shard_map(
        per_device_meet if meet else per_device,
        mesh=mesh,
        in_specs=(
            P(("parts", "wide", "narrow"), None),
            P(("parts", "wide", "narrow")),
            P(("parts", "wide", "narrow")),
        ),
        out_specs=P(("parts", "wide", "narrow")),
        check_vma=False,
    )
```

```python
import jax
import jax.numpy as jnp
from jax import lax
from jax.experimental import pallas as pl
from jax.experimental.pallas import tpu as pltpu
from jax.sharding import PartitionSpec as P

CPO = 16


def shifted(shard, axis, by):
    count = lax.axis_size(axis)
    return lax.ppermute(shard, axis, [(i, (i + by) % count) for i in range(count)])


def pair_inner(left, right):
    return lax.dot_general(
        left, right, (((1,), (1,)), ((), ())), preferred_element_type=jnp.float32
    )


def per_device(embeddings, cluster_id, order_index):
    wide_size = lax.axis_size("wide")
    rows = embeddings.shape[0]
    width = embeddings.shape[1]
    bucket = 2 * rows // wide_size
    values = embeddings.astype(jnp.float32)
    unit = (values * lax.rsqrt(jnp.sum(values * values, axis=1, keepdims=True) + 1e-06)).astype(
        jnp.bfloat16
    )
    owner = cluster_id // CPO
    here = jnp.arange(rows, dtype=jnp.int32)
    earlier = (owner[:, None] == owner[None, :]) & (here[None, :] < here[:, None])
    slot = jnp.sum(jnp.where(earlier, 1, 0), axis=1)
    target = owner * bucket + slot
    send_rows = jnp.zeros((wide_size * bucket, width), jnp.bfloat16).at[target].set(unit)
    meta_rows = jnp.stack([cluster_id, order_index], axis=1)
    send_meta = jnp.full((wide_size * bucket, 2), -1, jnp.int32).at[target].set(meta_rows)
    held, held_meta = (
        lax.all_to_all(send_rows, "wide", split_axis=0, concat_axis=0, tiled=True),
        lax.all_to_all(send_meta, "wide", split_axis=0, concat_axis=0, tiled=True),
    )
    held_cl = held_meta[:, 0]
    held_or = held_meta[:, 1]
    live = held_cl >= 0
    start_best = jnp.full((held.shape[0],), -1.0, jnp.float32)

    def row_best(inner, other_cl, other_or):
        allowed = (
            (other_cl[None, :] == held_cl[:, None])
            & (other_or[None, :] < held_or[:, None])
            & live[:, None]
        )
        return jnp.max(jnp.where(allowed, inner, -1.0), axis=1)

    narrow_size = lax.axis_size("narrow")
    best = jnp.maximum(start_best, row_best(pair_inner(held, held), held_cl, held_or))
    for distance in range(1, narrow_size // 2 + 1):
        other_rows, other_meta = shifted((held, held_meta), "narrow", distance)
        other_cl = other_meta[:, 0]
        other_or = other_meta[:, 1]
        inner = pair_inner(held, other_rows)
        best = jnp.maximum(best, row_best(inner, other_cl, other_or))
        column_ok = (
            (held_cl[:, None] == other_cl[None, :])
            & (held_or[:, None] < other_or[None, :])
            & (other_cl[None, :] >= 0)
        )
        column_best = jnp.max(jnp.where(column_ok, inner, -1.0), axis=0)
        returned = shifted(column_best, "narrow", -distance)
        best = jnp.maximum(best, returned)
    answers = lax.all_to_all(best, "wide", split_axis=0, concat_axis=0, tiled=True)
    return answers[target]


CHUNKS = 4
SIDE = 4
MESH = pl.DeviceIdType.MESH
NEXT, MATE_AWAY, LAST, MATE_HOME = range(4)


def meet_kernel(emb_far, cl, od, out, emb, got, qraw, uq, tags, cand, pq, pk, pm, kbuf, kmeta, ktall, colacc, target,
                racc, rsend, rres, cacc, cres, cfull, late,
                xs, xr, fs, fr, cs, cr, tgs, tgr, cas, car, zs, zr, zms, zmr, rs, rr, ts, tr):
    w = lax.axis_index("wide")
    n = lax.axis_index("narrow")
    near = n + 1 - 2 * lax.rem(n, 2)
    cross = lax.rem(n + 2, SIDE)
    far = lax.rem(near + 2, SIDE)
    peers = (near, cross, far)
    mate = w + 1 - 2 * lax.rem(w, 2)
    over = SIDE - 1 - w
    over_mate = over + 1 - 2 * lax.rem(over, 2)
    outer = (w == 0) | (w == SIDE - 1)
    inner = (w > 0) & (w < SIDE - 1)
    rows = emb.shape[0]
    half = rows // 2
    f32 = jnp.float32

    def send(s, d, ss, rs_, **who):
        return pltpu.make_async_remote_copy(s, d, ss, rs_, device_id=who, device_id_type=MESH)

    take = pltpu.make_async_copy(emb_far, emb, got)
    take.start()
    others = [(a, b) for a in range(SIDE) for b in range(SIDE) if a or b]
    barrier = pltpu.get_barrier_semaphore()

    def greet(a, b):
        pl.semaphore_signal(
            barrier, inc=1, device_id={"wide": lax.rem(w + a, SIDE), "narrow": lax.rem(n + b, SIDE)}, device_id_type=MESH
        )

    for a, b in others:
        if a != 1:
            greet(a, b)

    @pl.when(w != SIDE - 1)
    def _():
        for b in range(SIDE):
            greet(1, b)

    id_row = cl[...].astype(f32)
    od_row = od[...].astype(f32)
    tags[0] = jnp.concatenate([id_row, od_row], axis=0)
    spot = lax.broadcasted_iota(jnp.int32, (1, 128), 1).astype(f32)
    fits = jnp.zeros((1, 128), f32)
    for o in range(SIDE):
        mine = jnp.where((id_row >= o * CPO) & (id_row < (o + 1) * CPO), 1.0, 0.0)
        fits = jnp.where((spot == o) & (jnp.sum(mine, axis=1, keepdims=True) == half), 1.0, fits)
    cand[0] = fits

    def lowest(mask):
        return jnp.min(jnp.where(mask > 0.5, spot, jnp.float32(SIDE)), axis=1, keepdims=True)

    @pl.when(w == 0)
    def _():
        pl.semaphore_wait(barrier, len(others) - SIDE)

    @pl.when(w != 0)
    def _():
        pl.semaphore_wait(barrier, len(others))

    @pl.when(w == SIDE - 1)
    def _():
        for b in range(SIDE):
            pl.semaphore_signal(late, inc=1, device_id={"wide": 0, "narrow": b}, device_id_type=MESH)

    x_part = [pl.ds(c * (rows // CHUNKS), rows // CHUNKS) for c in range(CHUNKS)]
    z_part = [pl.ds(c * (half // CHUNKS), half // CHUNKS) for c in range(CHUNKS)]
    votes = {
        (a, b): send(cand.at[0], cand.at[a * SIDE + b], cas.at[a * SIDE + b], car.at[a * SIDE + b],
                     wide=lax.rem(w + a, SIDE), narrow=lax.rem(n + b, SIDE))
        for a, b in others
    }
    names = [send(tags.at[0], tags.at[j + 1], tgs.at[j], tgr.at[j], narrow=peers[j]) for j in range(3)]
    xc = [send(emb.at[p], qraw.at[1, p], xs.at[c], xr.at[c], narrow=cross) for c, p in enumerate(x_part)]
    cc = send(emb, qraw.at[0], cs, cr, narrow=near)
    fc = [send(qraw.at[1, p], qraw.at[2, p], fs.at[c], fr.at[c], narrow=near) for c, p in enumerate(x_part)]
    for (a, b), c in votes.items():
        if a != SIDE - 1:
            c.start()

    @pl.when(w != 0)
    def _():
        for b in range(SIDE):
            votes[SIDE - 1, b].start()

    for c in names:
        c.start()
    take.wait()
    for c in xc + [cc]:
        c.start()

    def normed(values):
        values = values.astype(f32)
        return (values * lax.rsqrt(jnp.sum(values * values, axis=1, keepdims=True) + 1e-06)).astype(jnp.bfloat16)

    def tall(row, across):
        return jnp.broadcast_to(row, (across, row.shape[1])).T

    uq[0] = normed(emb[...])
    local = lowest(fits)
    first = jnp.where((id_row >= local * CPO) & (id_row < (local + 1.0) * CPO), 1.0, 0.0)
    deep = lax.broadcasted_iota(jnp.int32, (rows, rows), 0)
    long = lax.broadcasted_iota(jnp.int32, (rows, rows), 1)
    tri = jnp.where(deep < long, 1.0, 0.0).astype(jnp.bfloat16)
    rank = jnp.dot(jnp.broadcast_to(first, (16, rows)).astype(jnp.bfloat16), tri, preferred_element_type=f32)[0:1]
    lane = lax.broadcasted_iota(jnp.int32, (1, rows), 1).astype(f32)
    place = jnp.where(first > 0.5, rank, half + lane - rank)
    pick = jnp.where(deep.astype(f32) == place, 1.0, 0.0).astype(jnp.bfloat16)
    for s in range(2):
        pq[s] = jnp.dot(pick[s * half:(s + 1) * half], uq[0], preferred_element_type=f32).astype(jnp.bfloat16)
    od_high = jnp.floor(od_row * (1.0 / 128))
    od_low = od_row - od_high * 128
    marks = [jnp.broadcast_to(r, (16, rows)).astype(jnp.bfloat16) for r in (id_row, od_high, od_low)]
    marked = [pair_inner(t, pick)[0:1] for t in marks]
    moved = jnp.concatenate([marked[0], marked[1] * 128 + marked[2]], axis=0)

    @pl.when(w == 0)
    def _():
        pl.semaphore_wait(late, SIDE)
        for b in range(SIDE):
            votes[SIDE - 1, b].start()

    for c in votes.values():
        c.wait_recv()
    agreed = jnp.where(lowest(jnp.min(cand[...], axis=0)) == local, 1.0, 0.0)
    swap = jnp.where(w < SIDE // 2, 1.0 - agreed, agreed)
    pm[0] = jnp.where(swap > 0.5, moved[:, half:], moved[:, :half])
    pm[1] = jnp.where(swap > 0.5, moved[:, :half], moved[:, half:])

    def row_of(src, dst, ss, who):
        return [send(src.at[p], kbuf.at[dst, p], zs.at[ss, c], zr.at[dst, c], wide=who) for c, p in enumerate(z_part)]

    def tag_of(src, dst, ss, who):
        return send(src, kmeta.at[dst], zms.at[ss], zmr.at[dst], wide=who)

    def way(src, msrc, dst, ss, who):
        return tag_of(msrc, dst, ss, who), row_of(src, dst, ss, who)

    t_out_away, out_away = way(pk.at[0], pm.at[0], MATE_AWAY, 0, mate)
    t_out_home, out_home = way(pk.at[1], pm.at[1], MATE_HOME, 1, mate)
    t_in_away, in_away = way(pk.at[0], pm.at[0], NEXT, 0, over)
    t_in_next, in_next = way(kbuf.at[MATE_AWAY], kmeta.at[MATE_AWAY], LAST, 1, over)
    t_on_near, on_near = way(kbuf.at[NEXT], kmeta.at[NEXT], NEXT, 2, mate)
    t_on_far, on_far = way(kbuf.at[LAST], kmeta.at[LAST], LAST, 3, mate)

    def chosen(s, p):
        pk[s, p] = jnp.where(swap > 0.5, pq[1 - s, p].astype(f32), pq[s, p].astype(f32)).astype(jnp.bfloat16)

    for c, p in enumerate(z_part):
        chosen(0, p)

        @pl.when(outer)
        def _():
            if c == 0:
                t_out_away.start()
                t_out_home.start()
            out_away[c].start()

        @pl.when(inner)
        def _():
            if c == 0:
                t_in_away.start()
            in_away[c].start()

    target[...] = jnp.where(swap > 0.5, jnp.where(place < half, place + half, place - half), place)

    own_cl = tall(id_row, rows)
    own_od = tall(od_row, rows)

    def asked(j):
        if j < 2:
            return tags[j, 0:1], tags[j, 1:2]
        span = slice((j - 2) * half, (j - 1) * half)
        both = [jnp.concatenate([tags[2, r:r + 1, span], tags[3, r:r + 1, span]], axis=1) for r in range(2)]
        return both[0], both[1]

    def own_part(j):
        q_cl, q_od = asked(j)
        ok = (own_cl == q_cl) & (own_od < q_od)
        racc[j] = jnp.max(jnp.where(ok, pair_inner(uq[0], uq[j]), -1.0), axis=0, keepdims=True)

    own_part(0)
    for c in names:
        c.wait_recv()
    cc.wait_recv()
    uq[1] = normed(qraw[0])
    own_part(1)
    step = rows // CHUNKS

    def crossed(c):
        xc[c].wait_recv()
        fc[c].start()
        at = (c % 2) * step
        uq[2 + c // 2, at:at + step] = normed(qraw[1, c * step:(c + 1) * step])

    def turned(c):
        fc[c].wait_recv()
        at = half + (c % 2) * step
        uq[2 + c // 2, at:at + step] = normed(qraw[2, c * step:(c + 1) * step])

    def relay_near(c):
        @pl.when(inner)
        def _():
            if c == 0:
                t_out_away.wait_recv()
                t_in_next.start()
                t_in_away.wait_recv()
                t_on_near.start()
            out_away[c].wait_recv()
            in_next[c].start()
            in_away[c].wait_recv()
            on_near[c].start()

    def relay_far(c):
        if c == 0:
            t_in_next.wait_recv()
            t_on_far.start()
        in_next[c].wait_recv()
        on_far[c].start()

    def home(c):
        chosen(1, z_part[c])
        out_home[c].start()

    crossed(0)
    relay_near(0)
    relay_near(1)
    crossed(1)

    @pl.when(outer)
    def _():
        home(0)
        home(1)

    relay_near(2)
    turned(0)
    turned(1)
    own_part(2)
    relay_near(3)

    def learn(slot):
        ktall[slot, 0] = tall(kmeta[slot, 0:1], 128)
        ktall[slot, 1] = tall(kmeta[slot, 1:2], 128)

    started = set()

    def met(pieces, js):
        def stack(parts):
            return parts[0] if len(parts) == 1 else jnp.concatenate(parts, axis=0)

        keys = stack([kbuf[s, lo:hi] for s, lo, hi in pieces])
        k_cl, k_od = (
            stack([jnp.concatenate([ktall[s, r, lo:hi]] * (rows // 128), axis=1) for s, lo, hi in pieces]) for r in range(2)
        )
        col = jnp.full((keys.shape[0], 128), -1.0, f32)
        for j in js:
            q_cl, q_od = asked(j)
            same = jnp.where(k_cl == q_cl, pair_inner(keys, uq[j]), -1.0)
            before = k_od < q_od
            racc[j] = jnp.maximum(racc[j], jnp.max(jnp.where(before, same, -1.0), axis=0, keepdims=True))
            after = jnp.where(before, -1.0, same)
            for k in range(rows // 128):
                col = jnp.maximum(col, after[:, k * 128:(k + 1) * 128])
        at = 0
        for s, lo, hi in pieces:
            part = col[at:at + hi - lo]
            at += hi - lo
            if (s, lo) in started:
                part = jnp.maximum(part, colacc[s, lo:hi])
            started.add((s, lo))
            colacc[s, lo:hi] = part

    def back(slot, dst, who):
        return send(cacc.at[slot], cres.at[dst], ts.at[slot], tr.at[dst], wide=who)

    b_in = [back(NEXT, 0, over), back(MATE_AWAY, 2, mate), back(LAST, 0, over_mate), back(MATE_HOME, 3, mate)]
    b_out = {NEXT: back(NEXT, 1, over_mate), LAST: back(LAST, 1, over)}

    def give(slot, copies):
        cacc[slot] = jnp.max(colacc[slot].T, axis=0, keepdims=True)
        copies[slot].start()

    quarter = half // 2

    @pl.when(inner)
    def _():
        learn(NEXT)
        learn(MATE_AWAY)
        met([(NEXT, 0, half)], (0, 1, 2))
        crossed(2)
        relay_far(0)
        met([(MATE_AWAY, 0, half)], (0, 1, 2))
        relay_far(1)
        t_out_home.wait_recv()
        out_home[0].wait_recv()
        out_home[1].wait_recv()
        learn(LAST)
        learn(MATE_HOME)
        met([(LAST, 0, quarter), (MATE_HOME, 0, quarter)], (0, 1, 2))
        crossed(3)
        relay_far(2)
        turned(2)
        turned(3)
        own_part(3)
        met([(NEXT, 0, half), (MATE_AWAY, 0, half)], (3,))
        relay_far(3)
        give(MATE_AWAY, b_in)
        give(NEXT, b_in)
        met([(LAST, 0, quarter), (MATE_HOME, 0, quarter)], (3,))
        out_home[2].wait_recv()
        out_home[3].wait_recv()
        met([(LAST, quarter, half), (MATE_HOME, quarter, half)], (0, 1, 2, 3))
        give(MATE_HOME, b_in)
        give(LAST, b_in)

    started.clear()

    @pl.when(outer)
    def _():
        crossed(2)
        home(2)
        home(3)
        t_on_near.wait_recv()
        learn(NEXT)
        for c in on_near:
            c.wait_recv()
        met([(NEXT, 0, half)], (0, 1, 2))
        crossed(3)
        t_on_far.wait_recv()
        learn(LAST)
        turned(2)
        turned(3)
        own_part(3)
        met([(NEXT, 0, half)], (3,))
        give(NEXT, b_out)
        on_far[0].wait_recv()
        on_far[1].wait_recv()
        met([(LAST, 0, quarter)], (0, 1, 2, 3))
        on_far[2].wait_recv()
        on_far[3].wait_recv()
        met([(LAST, quarter, half)], (0, 1, 2, 3))
        give(LAST, b_out)

    rsend[0] = racc[1]
    rsend[1, :, :half] = racc[2, :, :half]
    rsend[1, :, half:] = racc[3, :, :half]
    rsend[2, :, :half] = racc[2, :, half:]
    rsend[2, :, half:] = racc[3, :, half:]
    rowb = [send(rsend.at[j], rres.at[j], rs.at[j], rr.at[j], narrow=peers[j]) for j in range(3)]
    for c in rowb[::-1]:
        c.start()
    b_in[NEXT].wait_recv()
    b_out[NEXT].wait_recv()
    cfull[:, :half] = jnp.maximum(cres[0], cres[1])
    cfull[:, half:] = jnp.full((1, half), -1.0, f32)

    @pl.when(outer)
    def _():
        b_in[MATE_AWAY].wait_recv()
        b_in[MATE_HOME].wait_recv()
        cfull[:, :half] = jnp.maximum(cfull[:, :half], cres[2])
        cfull[:, half:] = cres[3]

    mine = jnp.where(deep.astype(f32) == target[...], tall(cfull[...], rows), -1.0)
    mine = jnp.maximum(racc[0], jnp.max(mine, axis=0, keepdims=True))
    for c in rowb:
        c.wait_recv()
    out[...] = jnp.maximum(jnp.maximum(mine, rres[0]), jnp.maximum(rres[1], rres[2]))

    @pl.when(outer)
    def _():
        for c in [t_out_away, t_out_home] + out_away + out_home + list(b_out.values()):
            c.wait_send()

    @pl.when(inner)
    def _():
        for c in [t_in_away, t_in_next, t_on_near, t_on_far] + in_away + in_next + on_near + on_far + b_in:
            c.wait_send()

    for c in list(votes.values()) + names + xc + [cc] + fc + rowb:
        c.wait_send()


def per_device_meet(embeddings, cluster_id, order_index):
    rows, width = embeddings.shape
    half = rows // 2
    dma = pltpu.SemaphoreType.DMA
    vmem = pl.BlockSpec(memory_space=pltpu.VMEM)
    line = lambda k, m: pltpu.VMEM((k, 1, m), jnp.float32)
    block = lambda k, m: pltpu.VMEM((k, m, width), jnp.bfloat16)
    found = pl.pallas_call(
        meet_kernel,
        out_shape=jax.ShapeDtypeStruct((1, rows), jnp.float32),
        in_specs=[pl.BlockSpec(memory_space=pl.ANY), vmem, vmem],
        out_specs=vmem,
        scratch_shapes=[
            pltpu.VMEM((rows, width), jnp.bfloat16), dma, block(3, rows), block(4, rows),
            pltpu.VMEM((4, 2, rows), jnp.float32), line(SIDE * SIDE, 128),
            block(2, half), block(2, half), pltpu.VMEM((2, 2, half), jnp.float32),
            block(4, half), pltpu.VMEM((4, 2, half), jnp.float32),
            pltpu.VMEM((4, 2, half, 128), jnp.float32), pltpu.VMEM((4, half, 128), jnp.float32),
            pltpu.VMEM((1, rows), jnp.float32),
            line(4, rows), line(3, rows), line(3, rows), line(4, half), line(4, half), pltpu.VMEM((1, rows), jnp.float32),
            pltpu.SemaphoreType.REGULAR,
            dma((CHUNKS,)), dma((CHUNKS,)), dma((CHUNKS,)), dma((CHUNKS,)), dma, dma,
            dma((3,)), dma((3,)), dma((SIDE * SIDE,)), dma((SIDE * SIDE,)),
            dma((4, CHUNKS)), dma((4, CHUNKS)), dma((4,)), dma((4,)),
            dma((3,)), dma((3,)), dma((4,)), dma((4,)),
        ],
        compiler_params=pltpu.CompilerParams(collective_id=0, has_side_effects=True),
    )(embeddings, cluster_id.reshape(1, rows), order_index.reshape(1, rows))
    return jnp.maximum(found.reshape(rows), -1.0)


def solution(mesh):
    meet = mesh.shape["wide"] == SIDE and mesh.shape["narrow"] == SIDE
    return jax.shard_map(
        per_device_meet if meet else per_device,
        mesh=mesh,
        in_specs=(
            P(("parts", "wide", "narrow"), None),
            P(("parts", "wide", "narrow")),
            P(("parts", "wide", "narrow")),
        ),
        out_specs=P(("parts", "wide", "narrow")),
        check_vma=False,
    )
```

```python
import jax
import jax.numpy as jnp
from jax import lax
from jax.experimental import pallas as pl
from jax.experimental.pallas import tpu as pltpu
from jax.sharding import PartitionSpec as P

CPO = 16


def shifted(shard, axis, by):
    count = lax.axis_size(axis)
    return lax.ppermute(shard, axis, [(i, (i + by) % count) for i in range(count)])


def pair_inner(left, right):
    return lax.dot_general(
        left, right, (((1,), (1,)), ((), ())), preferred_element_type=jnp.float32
    )


def per_device(embeddings, cluster_id, order_index):
    wide_size = lax.axis_size("wide")
    rows = embeddings.shape[0]
    width = embeddings.shape[1]
    bucket = 2 * rows // wide_size
    values = embeddings.astype(jnp.float32)
    unit = (values * lax.rsqrt(jnp.sum(values * values, axis=1, keepdims=True) + 1e-06)).astype(
        jnp.bfloat16
    )
    owner = cluster_id // CPO
    here = jnp.arange(rows, dtype=jnp.int32)
    earlier = (owner[:, None] == owner[None, :]) & (here[None, :] < here[:, None])
    slot = jnp.sum(jnp.where(earlier, 1, 0), axis=1)
    target = owner * bucket + slot
    send_rows = jnp.zeros((wide_size * bucket, width), jnp.bfloat16).at[target].set(unit)
    meta_rows = jnp.stack([cluster_id, order_index], axis=1)
    send_meta = jnp.full((wide_size * bucket, 2), -1, jnp.int32).at[target].set(meta_rows)
    held, held_meta = (
        lax.all_to_all(send_rows, "wide", split_axis=0, concat_axis=0, tiled=True),
        lax.all_to_all(send_meta, "wide", split_axis=0, concat_axis=0, tiled=True),
    )
    held_cl = held_meta[:, 0]
    held_or = held_meta[:, 1]
    live = held_cl >= 0
    start_best = jnp.full((held.shape[0],), -1.0, jnp.float32)

    def row_best(inner, other_cl, other_or):
        allowed = (
            (other_cl[None, :] == held_cl[:, None])
            & (other_or[None, :] < held_or[:, None])
            & live[:, None]
        )
        return jnp.max(jnp.where(allowed, inner, -1.0), axis=1)

    narrow_size = lax.axis_size("narrow")
    best = jnp.maximum(start_best, row_best(pair_inner(held, held), held_cl, held_or))
    for distance in range(1, narrow_size // 2 + 1):
        other_rows, other_meta = shifted((held, held_meta), "narrow", distance)
        other_cl = other_meta[:, 0]
        other_or = other_meta[:, 1]
        inner = pair_inner(held, other_rows)
        best = jnp.maximum(best, row_best(inner, other_cl, other_or))
        column_ok = (
            (held_cl[:, None] == other_cl[None, :])
            & (held_or[:, None] < other_or[None, :])
            & (other_cl[None, :] >= 0)
        )
        column_best = jnp.max(jnp.where(column_ok, inner, -1.0), axis=0)
        returned = shifted(column_best, "narrow", -distance)
        best = jnp.maximum(best, returned)
    answers = lax.all_to_all(best, "wide", split_axis=0, concat_axis=0, tiled=True)
    return answers[target]


CHUNKS = 4
PIECES = 8
SIDE = 4
MESH = pl.DeviceIdType.MESH
NEXT, MATE_AWAY, LAST, MATE_HOME = range(4)


def meet_kernel(emb_far, cl_far, od_far, out, emb, cl, od, got, qraw, uq, tags, cand, pq, pk, pm, gotpq, gotpm, hm, kbuf, kmeta,
                ktall, colacc, target, racc, rsend, rres, cacc, cres, hsend, hres, cfull, late,
                xs, xr, fs, fr, cs, cr, tgs, tgr, cas, car, ps, pr, qs, qr, qms, qmr, zs, zr, zms, zmr,
                hxs, hxr, hfs, hfr, hns, hnr, hms, hmr, rs, rr, ts, tr, os, orr):
    w = lax.axis_index("wide")
    n = lax.axis_index("narrow")

    def flipped(v, k):
        return (v, v + 1 - 2 * lax.rem(v, 2), lax.rem(v + 2, SIDE), SIDE - 1 - v)[k]

    near, cross, far = (flipped(n, k) for k in (1, 2, 3))
    peers = (near, cross, far)
    mate, over_mate, over = (flipped(w, k) for k in (1, 2, 3))
    early = w < SIDE // 2
    outer = (w == 0) | (w == SIDE - 1)
    inner = (w > 0) & (w < SIDE - 1)
    rows = emb.shape[0]
    half = rows // 2
    f32 = jnp.float32

    def send(s, d, ss, rs_, **who):
        return pltpu.make_async_remote_copy(s, d, ss, rs_, device_id=who, device_id_type=MESH)

    take = [pltpu.make_async_copy(s, d, got.at[k]) for k, (s, d) in enumerate([(cl_far, cl), (od_far, od), (emb_far, emb)])]
    for c in take:
        c.start()
    same_side = [(0, b) for b in range(1, SIDE)] + [(1, b) for b in range(SIDE)]
    far_side = [(a, b) for a in (2, 3) for b in range(SIDE)]
    barrier = pltpu.get_barrier_semaphore()

    def greet(a, b):
        pl.semaphore_signal(barrier, inc=1, device_id={"wide": flipped(w, a), "narrow": flipped(n, b)}, device_id_type=MESH)

    for a, b in same_side:
        greet(a, b)

    @pl.when(early)
    def _():
        for a, b in far_side:
            greet(a, b)

    take[0].wait()
    take[1].wait()
    id_row = cl[...].astype(f32)
    od_row = od[...].astype(f32)
    tags[0] = jnp.concatenate([id_row, od_row], axis=0)
    spot = lax.broadcasted_iota(jnp.int32, (1, 128), 1).astype(f32)
    fits = jnp.zeros((1, 128), f32)
    for o in range(SIDE):
        mine = jnp.where((id_row >= o * CPO) & (id_row < (o + 1) * CPO), 1.0, 0.0)
        fits = jnp.where((spot == o) & (jnp.sum(mine, axis=1, keepdims=True) == half), 1.0, fits)
    cand[0] = fits

    def lowest(mask):
        return jnp.min(jnp.where(mask > 0.5, spot, jnp.float32(SIDE)), axis=1, keepdims=True)

    @pl.when(early)
    def _():
        pl.semaphore_wait(barrier, len(same_side))

    @pl.when(w >= SIDE // 2)
    def _():
        pl.semaphore_wait(barrier, len(same_side) + len(far_side))
        pl.semaphore_signal(late, inc=1, device_id={"wide": 1}, device_id_type=MESH)

    x_part = [pl.ds(c * (rows // CHUNKS), rows // CHUNKS) for c in range(CHUNKS)]
    z_part = [pl.ds(c * (half // PIECES), half // PIECES) for c in range(PIECES)]
    votes = {
        (a, b): send(cand.at[0], cand.at[a * SIDE + b], cas.at[a * SIDE + b], car.at[a * SIDE + b],
                     wide=flipped(w, a), narrow=flipped(n, b))
        for a, b in same_side + far_side
    }
    sums = [send(cand.at[SIDE * SIDE], cand.at[SIDE * SIDE + 1], ps.at[k], pr, wide=who) for k, who in enumerate((over, over_mate))]
    names = [send(tags.at[0], tags.at[j + 1], tgs.at[j], tgr.at[j], narrow=peers[j]) for j in range(3)]
    xc = [send(emb.at[p], qraw.at[1, p], xs.at[c], xr.at[c], narrow=cross) for c, p in enumerate(x_part)]
    cc = send(emb, qraw.at[0], cs, cr, narrow=near)
    fc = [send(qraw.at[1, p], qraw.at[2, p], fs.at[c], fr.at[c], narrow=near) for c, p in enumerate(x_part)]
    for k in same_side:
        votes[k].start()

    @pl.when(w >= SIDE // 2)
    def _():
        for k in far_side:
            votes[k].start()

    for c in names:
        c.start()
    take[2].wait()
    for c in xc + [cc]:
        c.start()

    def normed(values):
        values = values.astype(f32)
        return (values * lax.rsqrt(jnp.sum(values * values, axis=1, keepdims=True) + 1e-06)).astype(jnp.bfloat16)

    def tall(row, across):
        return jnp.broadcast_to(row, (across, row.shape[1])).T

    uq[0] = normed(emb[...])
    local = lowest(fits)
    first = jnp.where((id_row >= local * CPO) & (id_row < (local + 1.0) * CPO), 1.0, 0.0)
    deep = lax.broadcasted_iota(jnp.int32, (rows, rows), 0)
    long = lax.broadcasted_iota(jnp.int32, (rows, rows), 1)
    tri = jnp.where(deep < long, 1.0, 0.0).astype(jnp.bfloat16)
    rank = jnp.dot(jnp.broadcast_to(first, (16, rows)).astype(jnp.bfloat16), tri, preferred_element_type=f32)[0:1]
    lane = lax.broadcasted_iota(jnp.int32, (1, rows), 1).astype(f32)
    place = jnp.where(first > 0.5, rank, half + lane - rank)
    pick = jnp.where(deep.astype(f32) == place, 1.0, 0.0).astype(jnp.bfloat16)
    for s in range(2):
        pq[s] = jnp.dot(pick[s * half:(s + 1) * half], uq[0], preferred_element_type=f32).astype(jnp.bfloat16)
    od_high = jnp.floor(od_row * (1.0 / 128))
    od_low = od_row - od_high * 128
    marks = [jnp.broadcast_to(r, (16, rows)).astype(jnp.bfloat16) for r in (id_row, od_high, od_low)]
    marked = [pair_inner(t, pick)[0:1] for t in marks]
    moved = jnp.concatenate([marked[0], marked[1] * 128 + marked[2]], axis=0)

    pm[0] = moved

    pq_out = [[send(pq.at[k, p], gotpq.at[k, p], qs.at[k, c], qr.at[k, c], wide=mate) for c, p in enumerate(z_part)] for k in range(2)]
    pm_out = send(pm.at[0], gotpm, qms, qmr, wide=mate)

    @pl.when(outer)
    def _():
        pm_out.start()
        for k in range(2):
            for c in pq_out[k]:
                c.start()

    for k in same_side:
        votes[k].wait_recv()
    cand[SIDE * SIDE] = jnp.min(cand[0:2 * SIDE], axis=0)

    @pl.when(w == 1)
    def _():
        pl.semaphore_wait(late, 2)
        for c in sums:
            c.start()

    @pl.when(early)
    def _():
        for k in far_side:
            votes[k].wait_recv()
        cand[SIDE * SIDE + 2] = jnp.min(cand[2 * SIDE:4 * SIDE], axis=0)

    @pl.when(w >= SIDE // 2)
    def _():
        sums[0].wait_recv()
        cand[SIDE * SIDE + 2] = cand[SIDE * SIDE + 1]

    shared = jnp.minimum(cand[SIDE * SIDE], cand[SIDE * SIDE + 2])

    def turn(fit):
        agreed = jnp.where(lowest(shared) == lowest(fit), 1.0, 0.0)
        return jnp.where(early, 1.0 - agreed, agreed)

    swap = turn(fits)
    pm[1, :, :half] = jnp.where(swap > 0.5, moved[:, half:], moved[:, :half])

    def way(src, msrc, dst, ss):
        row = [send(src.at[p], kbuf.at[dst, p], zs.at[ss, c], zr.at[dst, c], wide=over) for c, p in enumerate(z_part)]
        return send(msrc, kmeta.at[dst], zms.at[ss], zmr.at[dst], wide=over), row

    t_in_away, in_away = way(pk, pm.at[1, :, pl.ds(0, half)], NEXT, 0)
    t_in_next, in_next = way(kbuf.at[MATE_AWAY], kmeta.at[MATE_AWAY], LAST, 1)

    def choose(flag, a, b):
        return jnp.where(flag > 0.5, b.astype(f32), a.astype(f32)).astype(jnp.bfloat16)

    @pl.when(inner)
    def _():
        t_in_away.start()
        for c, p in enumerate(z_part):
            pk[p] = choose(swap, pq[0, p], pq[1, p])
            in_away[c].start()

    target[...] = jnp.where(swap > 0.5, jnp.where(place < half, place + half, place - half), place)

    own_cl = tall(id_row, rows)
    own_od = tall(od_row, rows)

    def asked(j):
        if j < 2:
            return tags[j, 0:1], tags[j, 1:2]
        if j > 3:
            pair = [jnp.concatenate([hm[2 * j - 8, r:r + 1], hm[2 * j - 7, r:r + 1]], axis=1) for r in range(2)]
            return pair[0], pair[1]
        span = slice((j - 2) * half, (j - 1) * half)
        both = [jnp.concatenate([tags[2, r:r + 1, span], tags[3, r:r + 1, span]], axis=1) for r in range(2)]
        return both[0], both[1]

    def own_part(j):
        q_cl, q_od = asked(j)
        ok = (own_cl == q_cl) & (own_od < q_od)
        racc[j] = jnp.max(jnp.where(ok, pair_inner(uq[0], uq[j]), -1.0), axis=0, keepdims=True)

    own_part(0)
    for c in names:
        c.wait_recv()
    cc.wait_recv()
    uq[1] = normed(qraw[0])
    own_part(1)
    step = rows // CHUNKS

    def crossed(c):
        xc[c].wait_recv()
        fc[c].start()
        at = (c % 2) * step
        uq[2 + c // 2, at:at + step] = normed(qraw[1, c * step:(c + 1) * step])

    def turned(c):
        fc[c].wait_recv()
        at = half + (c % 2) * step
        uq[2 + c // 2, at:at + step] = normed(qraw[2, c * step:(c + 1) * step])

    def part(c):
        return slice(c * (half // PIECES), (c + 1) * (half // PIECES))

    hx = [send(uq.at[4, p], uq.at[5, p], hxs.at[c], hxr.at[c], narrow=cross) for c, p in enumerate(z_part)]
    hn = send(uq.at[4, pl.ds(0, half)], uq.at[4, pl.ds(half, half)], hns, hnr, narrow=near)
    hf = [
        send(uq.at[5, p], uq.at[5, pl.ds(half + c * (half // PIECES), half // PIECES)], hfs.at[c], hfr.at[c], narrow=near)
        for c, p in enumerate(z_part)
    ]
    hnames = [send(hm.at[0], hm.at[j + 1], hms.at[j], hmr.at[j], narrow=peers[j]) for j in range(3)]

    crossed(0)
    crossed(1)
    turned(0)
    turned(1)
    own_part(2)

    def learn(slot):
        ktall[slot, 0] = tall(kmeta[slot, 0:1], 128)
        ktall[slot, 1] = tall(kmeta[slot, 1:2], 128)

    started = set()

    def met(pieces, js):
        def stack(parts):
            return parts[0] if len(parts) == 1 else jnp.concatenate(parts, axis=0)

        keys = stack([uq[4, lo:hi] if s == MATE_HOME else kbuf[s, lo:hi] for s, lo, hi in pieces])
        k_cl, k_od = (
            stack([jnp.concatenate([ktall[s, r, lo:hi]] * (rows // 128), axis=1) for s, lo, hi in pieces]) for r in range(2)
        )
        col = jnp.full((keys.shape[0], 128), -1.0, f32)
        for j in js:
            q_cl, q_od = asked(j)
            same = jnp.where(k_cl == q_cl, pair_inner(keys, uq[j]), -1.0)
            before = k_od < q_od
            racc[j] = jnp.maximum(racc[j], jnp.max(jnp.where(before, same, -1.0), axis=0, keepdims=True))
            after = jnp.where(before, -1.0, same)
            for k in range(rows // 128):
                col = jnp.maximum(col, after[:, k * 128:(k + 1) * 128])
        at = 0
        for s, lo, hi in pieces:
            part = col[at:at + hi - lo]
            at += hi - lo
            if (s, lo) in started:
                part = jnp.maximum(part, colacc[s, lo:hi])
            started.add((s, lo))
            colacc[s, lo:hi] = part

    def back(slot, dst, who):
        return send(cacc.at[slot], cres.at[dst], ts.at[slot], tr.at[dst], wide=who)

    b_in = [back(NEXT, 0, over), back(MATE_AWAY, 2, mate), back(LAST, 0, over_mate), back(MATE_HOME, 3, mate)]
    h_in = [
        send(hsend.at[k], hres.at[k], os.at[k], orr.at[k], wide=mate, narrow=(n, near, cross, far)[k]) for k in range(SIDE)
    ]
    rowb = [send(rsend.at[j], rres.at[j], rs.at[j], rr.at[j], narrow=peers[j]) for j in range(3)]

    def give(slot):
        cacc[slot] = jnp.max(colacc[slot].T, axis=0, keepdims=True)
        b_in[slot].start()

    def share():
        rsend[0] = racc[1]
        rsend[1, :, :half] = racc[2, :, :half]
        rsend[1, :, half:] = racc[3, :, :half]
        rsend[2, :, :half] = racc[2, :, half:]
        rsend[2, :, half:] = racc[3, :, half:]
        for c in rowb[::-1]:
            c.start()

    def home(j):
        hsend[2 * j - 8] = racc[j, :, :half]
        hsend[2 * j - 7] = racc[j, :, half:]
        h_in[2 * j - 7].start()
        h_in[2 * j - 8].start()

    def last_block():
        crossed(3)
        turned(2)
        turned(3)
        own_part(3)

    quarter = half // 2

    @pl.when(inner)
    def _():
        racc[4] = jnp.full((1, rows), -1.0, f32)
        racc[5] = jnp.full((1, rows), -1.0, f32)
        mate_swap = turn(cand[SIDE])
        pm_out.wait_recv()
        got_tags = gotpm[...]
        kmeta[MATE_AWAY] = jnp.where(mate_swap > 0.5, got_tags[:, half:], got_tags[:, :half])
        hm[0] = jnp.where(mate_swap > 0.5, got_tags[:, :half], got_tags[:, half:])
        kmeta[MATE_HOME] = hm[0]
        t_in_next.start()
        for c in hnames:
            c.start()

        def settle(c):
            pq_out[0][c].wait_recv()
            pq_out[1][c].wait_recv()
            p = part(c)
            kbuf[MATE_AWAY, p] = choose(mate_swap, gotpq[0, p], gotpq[1, p])
            in_next[c].start()
            uq[4, p] = choose(mate_swap, gotpq[1, p], gotpq[0, p])
            hx[c].start()

        def passed(c):
            hx[c].wait_recv()
            hf[c].start()

        t_in_away.wait_recv()
        learn(NEXT)
        learn(MATE_AWAY)
        learn(MATE_HOME)
        settle(0)
        settle(1)
        crossed(2)
        for c in range(2, 6):
            settle(c)
        for c in in_away:
            c.wait_recv()
        met([(NEXT, 0, half)], (0,))
        settle(6)
        met([(NEXT, 0, half)], (1,))
        settle(7)
        hn.start()
        last_block()
        passed(0)
        met([(NEXT, 0, half)], (2, 3))
        passed(1)
        mates = [(MATE_AWAY, 0, half), (MATE_HOME, 0, half)]
        met(mates, (0,))
        passed(2)
        met(mates, (1,))
        passed(3)
        met(mates, (2,))
        passed(4)
        met(mates, (3,))
        passed(5)
        for c in hnames:
            c.wait_recv()
        hn.wait_recv()
        met([(NEXT, 0, half)], (4,))
        t_in_next.wait_recv()
        learn(LAST)
        for c in in_next[:PIECES // 2]:
            c.wait_recv()
        passed(6)
        met([(LAST, 0, quarter)], (0, 1, 2, 3, 4))
        passed(7)
        for c in in_next[PIECES // 2:]:
            c.wait_recv()
        met([(LAST, quarter, half)], (0, 1, 2, 3, 4))
        home(4)
        share()
        for c in hf:
            c.wait_recv()
        met([(NEXT, 0, half), (LAST, 0, quarter), (LAST, quarter, half)], (5,))
        home(5)
        give(MATE_HOME)
        give(MATE_AWAY)
        give(LAST)
        give(NEXT)

    @pl.when(outer)
    def _():
        crossed(2)
        last_block()
        share()

    b_in[NEXT].wait_recv()
    cfull[:, :half] = cres[0]
    cfull[:, half:] = jnp.full((1, half), -1.0, f32)

    @pl.when(outer)
    def _():
        b_in[MATE_AWAY].wait_recv()
        b_in[MATE_HOME].wait_recv()
        for c in h_in:
            c.wait_recv()
        cfull[:, :half] = jnp.maximum(cres[0], cres[2])
        cfull[:, half:] = jnp.maximum(jnp.maximum(cres[3], jnp.maximum(hres[0], hres[1])), jnp.maximum(hres[2], hres[3]))

    mine = jnp.where(deep.astype(f32) == target[...], tall(cfull[...], rows), -1.0)
    mine = jnp.maximum(racc[0], jnp.max(mine, axis=0, keepdims=True))
    for c in rowb:
        c.wait_recv()
    out[...] = jnp.maximum(jnp.maximum(mine, rres[0]), jnp.maximum(rres[1], rres[2]))

    @pl.when(outer)
    def _():
        for c in [pm_out] + pq_out[0] + pq_out[1]:
            c.wait_send()

    @pl.when(inner)
    def _():
        for c in [t_in_away, t_in_next, hn] + in_away + in_next + hx + hf + hnames + b_in + h_in:
            c.wait_send()

    @pl.when(w == 1)
    def _():
        for c in sums:
            c.wait_send()

    @pl.when(w >= SIDE // 2)
    def _():
        for k in far_side:
            votes[k].wait_send()

    for c in [votes[k] for k in same_side] + names + xc + [cc] + fc + rowb:
        c.wait_send()


def per_device_meet(embeddings, cluster_id, order_index):
    rows, width = embeddings.shape
    half = rows // 2
    dma = pltpu.SemaphoreType.DMA
    vmem = pl.BlockSpec(memory_space=pltpu.VMEM)
    line = lambda k, m: pltpu.VMEM((k, 1, m), jnp.float32)
    block = lambda k, m: pltpu.VMEM((k, m, width), jnp.bfloat16)
    found = pl.pallas_call(
        meet_kernel,
        out_shape=jax.ShapeDtypeStruct((1, rows), jnp.float32),
        in_specs=[pl.BlockSpec(memory_space=pl.ANY)] * 3,
        out_specs=vmem,
        scratch_shapes=[
            pltpu.VMEM((rows, width), jnp.bfloat16), pltpu.VMEM((1, rows), jnp.int32), pltpu.VMEM((1, rows), jnp.int32),
            dma((3,)), block(3, rows), block(6, rows),
            pltpu.VMEM((4, 2, rows), jnp.float32), line(SIDE * SIDE + 3, 128),
            block(2, half), pltpu.VMEM((half, width), jnp.bfloat16), pltpu.VMEM((2, 2, rows), jnp.float32),
            block(2, half), pltpu.VMEM((2, rows), jnp.float32), pltpu.VMEM((4, 2, half), jnp.float32),
            block(3, half), pltpu.VMEM((4, 2, half), jnp.float32),
            pltpu.VMEM((4, 2, half, 128), jnp.float32), pltpu.VMEM((4, half, 128), jnp.float32),
            pltpu.VMEM((1, rows), jnp.float32),
            line(6, rows), line(3, rows), line(3, rows), line(4, half), line(4, half), line(4, half), line(4, half),
            pltpu.VMEM((1, rows), jnp.float32), pltpu.SemaphoreType.REGULAR,
            dma((CHUNKS,)), dma((CHUNKS,)), dma((CHUNKS,)), dma((CHUNKS,)), dma, dma,
            dma((3,)), dma((3,)), dma((SIDE * SIDE,)), dma((SIDE * SIDE,)), dma((2,)), dma,
            dma((2, PIECES)), dma((2, PIECES)), dma, dma,
            dma((2, PIECES)), dma((3, PIECES)), dma((2,)), dma((3,)),
            dma((PIECES,)), dma((PIECES,)), dma((PIECES,)), dma((PIECES,)), dma, dma, dma((3,)), dma((3,)),
            dma((3,)), dma((3,)), dma((4,)), dma((4,)), dma((4,)), dma((4,)),
        ],
        compiler_params=pltpu.CompilerParams(collective_id=0, has_side_effects=True),
    )(embeddings, cluster_id.reshape(1, rows), order_index.reshape(1, rows))
    return jnp.maximum(found.reshape(rows), -1.0)


def solution(mesh):
    meet = mesh.shape["wide"] == SIDE and mesh.shape["narrow"] == SIDE
    return jax.shard_map(
        per_device_meet if meet else per_device,
        mesh=mesh,
        in_specs=(
            P(("parts", "wide", "narrow"), None),
            P(("parts", "wide", "narrow")),
            P(("parts", "wide", "narrow")),
        ),
        out_specs=P(("parts", "wide", "narrow")),
        check_vma=False,
    )
```

```python
import jax
import jax.numpy as jnp
from jax import lax
from jax.experimental import pallas as pl
from jax.experimental.pallas import tpu as pltpu
from jax.sharding import PartitionSpec as P

CPO = 16


def shifted(shard, axis, by):
    count = lax.axis_size(axis)
    return lax.ppermute(shard, axis, [(i, (i + by) % count) for i in range(count)])


def pair_inner(left, right):
    return lax.dot_general(
        left, right, (((1,), (1,)), ((), ())), preferred_element_type=jnp.float32
    )


def per_device(embeddings, cluster_id, order_index):
    wide_size = lax.axis_size("wide")
    rows = embeddings.shape[0]
    width = embeddings.shape[1]
    bucket = 2 * rows // wide_size
    values = embeddings.astype(jnp.float32)
    unit = (values * lax.rsqrt(jnp.sum(values * values, axis=1, keepdims=True) + 1e-06)).astype(
        jnp.bfloat16
    )
    owner = cluster_id // CPO
    here = jnp.arange(rows, dtype=jnp.int32)
    earlier = (owner[:, None] == owner[None, :]) & (here[None, :] < here[:, None])
    slot = jnp.sum(jnp.where(earlier, 1, 0), axis=1)
    target = owner * bucket + slot
    send_rows = jnp.zeros((wide_size * bucket, width), jnp.bfloat16).at[target].set(unit)
    meta_rows = jnp.stack([cluster_id, order_index], axis=1)
    send_meta = jnp.full((wide_size * bucket, 2), -1, jnp.int32).at[target].set(meta_rows)
    held, held_meta = (
        lax.all_to_all(send_rows, "wide", split_axis=0, concat_axis=0, tiled=True),
        lax.all_to_all(send_meta, "wide", split_axis=0, concat_axis=0, tiled=True),
    )
    held_cl = held_meta[:, 0]
    held_or = held_meta[:, 1]
    live = held_cl >= 0
    start_best = jnp.full((held.shape[0],), -1.0, jnp.float32)

    def row_best(inner, other_cl, other_or):
        allowed = (
            (other_cl[None, :] == held_cl[:, None])
            & (other_or[None, :] < held_or[:, None])
            & live[:, None]
        )
        return jnp.max(jnp.where(allowed, inner, -1.0), axis=1)

    narrow_size = lax.axis_size("narrow")
    best = jnp.maximum(start_best, row_best(pair_inner(held, held), held_cl, held_or))
    for distance in range(1, narrow_size // 2 + 1):
        other_rows, other_meta = shifted((held, held_meta), "narrow", distance)
        other_cl = other_meta[:, 0]
        other_or = other_meta[:, 1]
        inner = pair_inner(held, other_rows)
        best = jnp.maximum(best, row_best(inner, other_cl, other_or))
        column_ok = (
            (held_cl[:, None] == other_cl[None, :])
            & (held_or[:, None] < other_or[None, :])
            & (other_cl[None, :] >= 0)
        )
        column_best = jnp.max(jnp.where(column_ok, inner, -1.0), axis=0)
        returned = shifted(column_best, "narrow", -distance)
        best = jnp.maximum(best, returned)
    answers = lax.all_to_all(best, "wide", split_axis=0, concat_axis=0, tiled=True)
    return answers[target]


PIECES = 8
SIDE = 4
MESH = pl.DeviceIdType.MESH
NEXT, LAST, RELAY = range(3)


def meet_kernel(emb_far, cl_far, od_far, out, emb, cl, od, got, own, uq, marks, cand, pq, pk, gotpq, kbuf, kmeta, asked, ktall,
                colacc, target, racc, gave, res, cacc, cres, cfull, late,
                cas, car, ps, pr, mks, mkr, qs, qr, zs, zr, zms, zmr, ms, mr, xs, xr, fs, fr, ns, nr, rs, rr, ts, tr):
    w = lax.axis_index("wide")
    n = lax.axis_index("narrow")

    def flipped(v, k):
        return (v, v + 1 - 2 * lax.rem(v, 2), lax.rem(v + 2, SIDE), SIDE - 1 - v)[k]

    near, cross, far = (flipped(n, k) for k in (1, 2, 3))
    peers = (near, cross, far)
    mate, over_mate, over = (flipped(w, k) for k in (1, 2, 3))
    early = w < SIDE // 2
    outer = (w == 0) | (w == SIDE - 1)
    inner = (w > 0) & (w < SIDE - 1)
    rows = emb.shape[0]
    half = rows // 2
    f32 = jnp.float32

    def send(s, d, ss, rs_, **who):
        return pltpu.make_async_remote_copy(s, d, ss, rs_, device_id=who, device_id_type=MESH)

    take = [pltpu.make_async_copy(s, d, got.at[k]) for k, (s, d) in enumerate([(cl_far, cl), (od_far, od), (emb_far, emb)])]
    for c in take:
        c.start()
    same_side = [(0, b) for b in range(1, SIDE)] + [(1, b) for b in range(SIDE)]
    far_side = [(a, b) for a in (2, 3) for b in range(SIDE)]
    barrier = pltpu.get_barrier_semaphore()

    def greet(a, b):
        pl.semaphore_signal(barrier, inc=1, device_id={"wide": flipped(w, a), "narrow": flipped(n, b)}, device_id_type=MESH)

    for a, b in same_side:
        greet(a, b)

    @pl.when(early)
    def _():
        for a, b in far_side:
            greet(a, b)

    take[0].wait()
    take[1].wait()
    id_row = cl[...].astype(f32)
    od_row = od[...].astype(f32)
    spot = lax.broadcasted_iota(jnp.int32, (1, 128), 1).astype(f32)
    fits = jnp.zeros((1, 128), f32)
    for o in range(SIDE):
        mine = jnp.where((id_row >= o * CPO) & (id_row < (o + 1) * CPO), 1.0, 0.0)
        fits = jnp.where((spot == o) & (jnp.sum(mine, axis=1, keepdims=True) == half), 1.0, fits)
    cand[0] = fits

    def lowest(mask):
        return jnp.min(jnp.where(mask > 0.5, spot, jnp.float32(SIDE)), axis=1, keepdims=True)

    @pl.when(early)
    def _():
        pl.semaphore_wait(barrier, len(same_side))

    @pl.when(w >= SIDE // 2)
    def _():
        pl.semaphore_wait(barrier, len(same_side) + len(far_side))
        pl.semaphore_signal(late, inc=1, device_id={"wide": 1}, device_id_type=MESH)

    z_part = [pl.ds(c * (half // PIECES), half // PIECES) for c in range(PIECES)]
    votes = {
        (a, b): send(cand.at[0], cand.at[a * SIDE + b], cas.at[a * SIDE + b], car.at[a * SIDE + b],
                     wide=flipped(w, a), narrow=flipped(n, b))
        for a, b in same_side + far_side
    }
    sums = [send(cand.at[SIDE * SIDE], cand.at[SIDE * SIDE + 1], ps.at[k], pr, wide=who) for k, who in enumerate((over, over_mate))]
    for k in same_side:
        votes[k].start()

    @pl.when(w >= SIDE // 2)
    def _():
        for k in far_side:
            votes[k].start()

    take[2].wait()

    def normed(values):
        values = values.astype(f32)
        return (values * lax.rsqrt(jnp.sum(values * values, axis=1, keepdims=True) + 1e-06)).astype(jnp.bfloat16)

    own[...] = normed(emb[...])
    local = lowest(fits)
    first = jnp.where((id_row >= local * CPO) & (id_row < (local + 1.0) * CPO), 1.0, 0.0)
    deep = lax.broadcasted_iota(jnp.int32, (rows, rows), 0)
    long = lax.broadcasted_iota(jnp.int32, (rows, rows), 1)
    tri = jnp.where(deep < long, 1.0, 0.0).astype(jnp.bfloat16)
    rank = jnp.dot(jnp.broadcast_to(first, (16, rows)).astype(jnp.bfloat16), tri, preferred_element_type=f32)[0:1]
    lane = lax.broadcasted_iota(jnp.int32, (1, rows), 1).astype(f32)
    place = jnp.where(first > 0.5, rank, half + lane - rank)
    pick = jnp.where(deep.astype(f32) == place, 1.0, 0.0).astype(jnp.bfloat16)
    od_high = jnp.floor(od_row * (1.0 / 128))
    od_low = od_row - od_high * 128
    digits = [jnp.broadcast_to(r, (16, rows)).astype(jnp.bfloat16) for r in (id_row, od_high, od_low)]
    marked = [pair_inner(t, pick)[0:1] for t in digits]
    marks[0] = jnp.concatenate([marked[0], marked[1] * 128 + marked[2]], axis=0)
    tells = {
        (a, b): send(marks.at[0], marks.at[a * SIDE + b], mks.at[a * SIDE + b], mkr.at[a * SIDE + b],
                     wide=flipped(w, a), narrow=flipped(n, b))
        for a, b in same_side
    }
    for c in tells.values():
        c.start()
    pq_out = [[send(pq.at[k, p], gotpq.at[k, p], qs.at[k, c], qr.at[k, c], wide=mate) for c, p in enumerate(z_part)] for k in range(2)]
    for k in range(2):
        pq[k] = jnp.dot(pick[k * half:(k + 1) * half], own[...], preferred_element_type=f32).astype(jnp.bfloat16)

        @pl.when(outer)
        def _():
            for c in pq_out[k]:
                c.start()

    for k in same_side:
        votes[k].wait_recv()
    cand[SIDE * SIDE] = jnp.min(cand[0:2 * SIDE], axis=0)

    @pl.when(w == 1)
    def _():
        pl.semaphore_wait(late, 2)
        for c in sums:
            c.start()

    @pl.when(early)
    def _():
        for k in far_side:
            votes[k].wait_recv()
        cand[SIDE * SIDE + 2] = jnp.min(cand[2 * SIDE:4 * SIDE], axis=0)

    @pl.when(w >= SIDE // 2)
    def _():
        sums[0].wait_recv()
        cand[SIDE * SIDE + 2] = cand[SIDE * SIDE + 1]

    shared = jnp.minimum(cand[SIDE * SIDE], cand[SIDE * SIDE + 2])

    def turn(fit):
        agreed = jnp.where(lowest(shared) == lowest(fit), 1.0, 0.0)
        return jnp.where(early, 1.0 - agreed, agreed)

    swap = turn(fits)
    mate_swap = turn(cand[SIDE])

    def choose(flag, a, b):
        return jnp.where(flag > 0.5, b.astype(f32), a.astype(f32)).astype(jnp.bfloat16)

    def way(src, msrc, dst, ss):
        row = [send(src.at[p], kbuf.at[dst, p], zs.at[ss, c], zr.at[dst, c], wide=over) for c, p in enumerate(z_part)]
        return send(msrc, kmeta.at[dst], zms.at[ss], zmr.at[dst], wide=over), row

    t_in_away, in_away = way(pk, kmeta.at[2], NEXT, 0)
    t_in_next, in_next = way(kbuf.at[RELAY], kmeta.at[3], LAST, 1)
    to_mate = [send(pk.at[p], uq.at[1, p], ms.at[c], mr.at[c], wide=mate) for c, p in enumerate(z_part)]
    behind = [pl.ds(half + c * (half // PIECES), half // PIECES) for c in range(PIECES)]
    x_out = [[send(uq.at[k, p], uq.at[2 + k, p], xs.at[k, c], xr.at[k, c], narrow=cross) for c, p in enumerate(z_part)] for k in range(2)]
    x_on = [
        [send(uq.at[2 + k, p], uq.at[2 + k, behind[c]], fs.at[k, c], fr.at[k, c], narrow=near) for c, p in enumerate(z_part)]
        for k in range(2)
    ]
    beside = [send(uq.at[k, pl.ds(0, half)], uq.at[k, pl.ds(half, half)], ns.at[k], nr.at[k], narrow=near) for k in range(2)]

    def tag_half(slot, flag):
        return jnp.where(flag > 0.5, marks[slot, :, half:], marks[slot, :, :half])

    tells[1, 0].wait_recv()

    @pl.when(inner)
    def _():
        kmeta[2] = tag_half(0, swap)
        kmeta[3] = tag_half(SIDE, mate_swap)
        t_in_away.start()
        t_in_next.start()
        for c, p in enumerate(z_part):
            pk[p] = choose(swap, pq[0, p], pq[1, p])
            in_away[c].start()

    hub = jnp.where(inner, 1.0 - swap, swap)
    for c, p in enumerate(z_part):
        uq[0, p] = choose(hub, pq[0, p], pq[1, p])
        x_out[0][c].start()
    beside[0].start()

    @pl.when(inner)
    def _():
        for c in to_mate:
            c.start()

    target[...] = jnp.where(swap > 0.5, jnp.where(place < half, place + half, place - half), place)
    for k in same_side:
        if k != (1, 0):
            tells[k].wait_recv()
    for j in range(4):
        for k in range(2):
            slot = (j % 2) * SIDE + (j // 2) * 2 + k
            flag = turn(cand[slot])
            asked[j, :, k * half:(k + 1) * half] = tag_half(slot, jnp.where(inner, 1.0 - flag, flag))

    def tall(row):
        return jnp.broadcast_to(row, (128, row.shape[1])).T

    for k in range(2):
        for r in range(2):
            ktall[k, r] = tall(asked[k, r:r + 1, :half])

    def stack(parts):
        return parts[0] if len(parts) == 1 else jnp.concatenate(parts, axis=0)

    def tag_of(pieces, r):
        return stack([jnp.concatenate([ktall[s, r, lo:hi]] * (rows // 128), axis=1) for s, lo, hi in pieces])

    def own_part(js):
        pieces = [(0, 0, half), (1, 0, half)]
        keys = stack([uq[0, :half], uq[1, :half]])
        k_cl, k_od = tag_of(pieces, 0), tag_of(pieces, 1)
        for j in js:
            ok = (k_cl == asked[j, 0:1]) & (k_od < asked[j, 1:2])
            racc[j] = jnp.maximum(racc[j], jnp.max(jnp.where(ok, pair_inner(keys, uq[j]), -1.0), axis=0, keepdims=True))

    started = set()

    def met(pieces, js):
        keys = stack([kbuf[s, lo:hi] for s, lo, hi in pieces])
        slots = [(s + 2, lo, hi) for s, lo, hi in pieces]
        k_cl, k_od = tag_of(slots, 0), tag_of(slots, 1)
        col = jnp.full((keys.shape[0], 128), -1.0, f32)
        for j in js:
            same = jnp.where(k_cl == asked[j, 0:1], pair_inner(keys, uq[j]), -1.0)
            before = k_od < asked[j, 1:2]
            racc[j] = jnp.maximum(racc[j], jnp.max(jnp.where(before, same, -1.0), axis=0, keepdims=True))
            after = jnp.where(before, -1.0, same)
            for k in range(rows // 128):
                col = jnp.maximum(col, after[:, k * 128:(k + 1) * 128])
        at = 0
        for s, lo, hi in pieces:
            part = col[at:at + hi - lo]
            at += hi - lo
            if (s, lo) in started:
                part = jnp.maximum(part, colacc[s, lo:hi])
            started.add((s, lo))
            colacc[s, lo:hi] = part

    for j in range(4):
        racc[j] = jnp.full((1, rows), -1.0, f32)
    answers = {
        (a, b): send(gave.at[a * SIDE + b], res.at[a * SIDE + b], rs.at[a * SIDE + b], rr.at[a * SIDE + b],
                     wide=flipped(w, a), narrow=flipped(n, b))
        for a, b in same_side
    }
    backs = [send(cacc.at[s], cres, ts.at[s], tr, wide=who) for s, who in enumerate((over, over_mate))]

    def give(slot):
        cacc[slot] = jnp.max(colacc[slot].T, axis=0, keepdims=True)
        backs[slot].start()

    def answer(j):
        for k in range(2)[::-1]:
            key = (j % 2, (j // 2) * 2 + k)
            gave[key[0] * SIDE + key[1]] = racc[j, :, k * half:(k + 1) * half]
            if key in answers:
                answers[key].start()

    def passed(k, c):
        x_out[k][c].wait_recv()
        x_on[k][c].start()

    def part(c):
        return slice(c * (half // PIECES), (c + 1) * (half // PIECES))

    quarter = half // 2

    @pl.when(inner)
    def _():
        def settle(c):
            pq_out[0][c].wait_recv()
            pq_out[1][c].wait_recv()
            p = part(c)
            kbuf[RELAY, p] = choose(mate_swap, gotpq[0, p], gotpq[1, p])
            in_next[c].start()
            uq[1, p] = choose(mate_swap, gotpq[1, p], gotpq[0, p])
            x_out[1][c].start()

        for c in range(PIECES):
            passed(0, c)
            settle(c)
        beside[1].start()
        t_in_away.wait_recv()
        t_in_next.wait_recv()
        for s in range(2):
            for r in range(2):
                ktall[s + 2, r] = tall(kmeta[s, r:r + 1])
        beside[0].wait_recv()
        own_part((0,))
        passed(1, 0)
        for c in in_away:
            c.wait_recv()
        met([(NEXT, 0, half)], (0,))
        passed(1, 1)
        for c in x_on[0]:
            c.wait_recv()
        own_part((2,))
        met([(NEXT, 0, half)], (2,))
        passed(1, 2)
        beside[1].wait_recv()
        own_part((1,))
        met([(NEXT, 0, half)], (1,))
        passed(1, 3)
        for c in in_next[:PIECES // 2]:
            c.wait_recv()
        passed(1, 4)
        met([(LAST, 0, quarter)], (0, 1, 2))
        passed(1, 5)
        passed(1, 6)
        for c in in_next[PIECES // 2:]:
            c.wait_recv()
        passed(1, 7)
        met([(LAST, quarter, half)], (0, 1, 2))
        answer(1)
        for c in x_on[1]:
            c.wait_recv()
        met([(LAST, 0, quarter), (LAST, quarter, half), (NEXT, 0, half)], (3,))
        give(LAST)
        own_part((3,))
        answer(3)
        answer(2)
        answer(0)
        give(NEXT)

    @pl.when(outer)
    def _():
        def settle(c):
            to_mate[c].wait_recv()
            x_out[1][c].start()

        for c in range(PIECES):
            passed(0, c)
            settle(c)
        beside[1].start()
        beside[0].wait_recv()
        own_part((0,))
        for c in x_on[0]:
            c.wait_recv()
        own_part((2,))
        beside[1].wait_recv()
        own_part((1,))
        for c in range(PIECES):
            passed(1, c)
        for c in x_on[1]:
            c.wait_recv()
        own_part((3,))
        for j in (3, 2, 1, 0):
            answer(j)

    for c in answers.values():
        c.wait_recv()
    hub_best = jnp.maximum(jnp.maximum(gave[0], res[1]), jnp.maximum(res[2], res[3]))
    other_best = jnp.maximum(jnp.maximum(res[4], res[5]), jnp.maximum(res[6], res[7]))
    backs[0].wait_recv()
    cfull[:, :half] = jnp.maximum(jnp.where(inner, other_best, hub_best), cres[...])
    cfull[:, half:] = jnp.where(inner, hub_best, other_best)
    spread = jnp.broadcast_to(cfull[...], (128, rows)).T
    mine = jnp.where(deep.astype(f32) == target[...], jnp.concatenate([spread] * (rows // 128), axis=1), -1.0)
    out[...] = jnp.max(mine, axis=0, keepdims=True)

    @pl.when(outer)
    def _():
        for c in pq_out[0] + pq_out[1]:
            c.wait_send()

    @pl.when(inner)
    def _():
        for c in [t_in_away, t_in_next] + in_away + in_next + to_mate + backs:
            c.wait_send()

    @pl.when(w == 1)
    def _():
        for c in sums:
            c.wait_send()

    @pl.when(w >= SIDE // 2)
    def _():
        for k in far_side:
            votes[k].wait_send()

    for c in [votes[k] for k in same_side] + list(tells.values()) + x_out[0] + x_out[1] + x_on[0] + x_on[1] + beside:
        c.wait_send()
    for c in answers.values():
        c.wait_send()


def per_device_meet(embeddings, cluster_id, order_index):
    rows, width = embeddings.shape
    half = rows // 2
    dma = pltpu.SemaphoreType.DMA
    vmem = pl.BlockSpec(memory_space=pltpu.VMEM)
    line = lambda k, m: pltpu.VMEM((k, 1, m), jnp.float32)
    block = lambda k, m: pltpu.VMEM((k, m, width), jnp.bfloat16)
    found = pl.pallas_call(
        meet_kernel,
        out_shape=jax.ShapeDtypeStruct((1, rows), jnp.float32),
        in_specs=[pl.BlockSpec(memory_space=pl.ANY)] * 3,
        out_specs=vmem,
        scratch_shapes=[
            pltpu.VMEM((rows, width), jnp.bfloat16), pltpu.VMEM((1, rows), jnp.int32), pltpu.VMEM((1, rows), jnp.int32),
            dma((3,)), pltpu.VMEM((rows, width), jnp.bfloat16), block(4, rows),
            pltpu.VMEM((2 * SIDE, 2, rows), jnp.float32), line(SIDE * SIDE + 3, 128),
            block(2, half), pltpu.VMEM((half, width), jnp.bfloat16), block(2, half),
            block(3, half), pltpu.VMEM((4, 2, half), jnp.float32), pltpu.VMEM((4, 2, rows), jnp.float32),
            pltpu.VMEM((4, 2, half, 128), jnp.float32), pltpu.VMEM((2, half, 128), jnp.float32),
            pltpu.VMEM((1, rows), jnp.float32),
            line(4, rows), line(2 * SIDE, half), line(2 * SIDE, half), line(2, half), pltpu.VMEM((1, half), jnp.float32),
            pltpu.VMEM((1, rows), jnp.float32), pltpu.SemaphoreType.REGULAR,
            dma((SIDE * SIDE,)), dma((SIDE * SIDE,)), dma((2,)), dma, dma((2 * SIDE,)), dma((2 * SIDE,)),
            dma((2, PIECES)), dma((2, PIECES)), dma((2, PIECES)), dma((2, PIECES)), dma((2,)), dma((2,)),
            dma((PIECES,)), dma((PIECES,)), dma((2, PIECES)), dma((2, PIECES)), dma((2, PIECES)), dma((2, PIECES)),
            dma((2,)), dma((2,)), dma((2 * SIDE,)), dma((2 * SIDE,)), dma((2,)), dma,
        ],
        compiler_params=pltpu.CompilerParams(collective_id=0, has_side_effects=True),
    )(embeddings, cluster_id.reshape(1, rows), order_index.reshape(1, rows))
    return jnp.maximum(found.reshape(rows), -1.0)


def solution(mesh):
    meet = mesh.shape["wide"] == SIDE and mesh.shape["narrow"] == SIDE
    return jax.shard_map(
        per_device_meet if meet else per_device,
        mesh=mesh,
        in_specs=(
            P(("parts", "wide", "narrow"), None),
            P(("parts", "wide", "narrow")),
            P(("parts", "wide", "narrow")),
        ),
        out_specs=P(("parts", "wide", "narrow")),
        check_vma=False,
    )
```

```python
import jax
import jax.numpy as jnp
from jax import lax
from jax.experimental import pallas as pl
from jax.experimental.pallas import tpu as pltpu
from jax.sharding import PartitionSpec as P

CPO = 16


def shifted(shard, axis, by):
    count = lax.axis_size(axis)
    return lax.ppermute(shard, axis, [(i, (i + by) % count) for i in range(count)])


def pair_inner(left, right):
    return lax.dot_general(
        left, right, (((1,), (1,)), ((), ())), preferred_element_type=jnp.float32
    )


def per_device(embeddings, cluster_id, order_index):
    wide_size = lax.axis_size("wide")
    rows = embeddings.shape[0]
    width = embeddings.shape[1]
    bucket = 2 * rows // wide_size
    values = embeddings.astype(jnp.float32)
    unit = (values * lax.rsqrt(jnp.sum(values * values, axis=1, keepdims=True) + 1e-06)).astype(
        jnp.bfloat16
    )
    owner = cluster_id // CPO
    here = jnp.arange(rows, dtype=jnp.int32)
    earlier = (owner[:, None] == owner[None, :]) & (here[None, :] < here[:, None])
    slot = jnp.sum(jnp.where(earlier, 1, 0), axis=1)
    target = owner * bucket + slot
    send_rows = jnp.zeros((wide_size * bucket, width), jnp.bfloat16).at[target].set(unit)
    meta_rows = jnp.stack([cluster_id, order_index], axis=1)
    send_meta = jnp.full((wide_size * bucket, 2), -1, jnp.int32).at[target].set(meta_rows)
    held, held_meta = (
        lax.all_to_all(send_rows, "wide", split_axis=0, concat_axis=0, tiled=True),
        lax.all_to_all(send_meta, "wide", split_axis=0, concat_axis=0, tiled=True),
    )
    held_cl = held_meta[:, 0]
    held_or = held_meta[:, 1]
    live = held_cl >= 0
    start_best = jnp.full((held.shape[0],), -1.0, jnp.float32)

    def row_best(inner, other_cl, other_or):
        allowed = (
            (other_cl[None, :] == held_cl[:, None])
            & (other_or[None, :] < held_or[:, None])
            & live[:, None]
        )
        return jnp.max(jnp.where(allowed, inner, -1.0), axis=1)

    narrow_size = lax.axis_size("narrow")
    best = jnp.maximum(start_best, row_best(pair_inner(held, held), held_cl, held_or))
    for distance in range(1, narrow_size // 2 + 1):
        other_rows, other_meta = shifted((held, held_meta), "narrow", distance)
        other_cl = other_meta[:, 0]
        other_or = other_meta[:, 1]
        inner = pair_inner(held, other_rows)
        best = jnp.maximum(best, row_best(inner, other_cl, other_or))
        column_ok = (
            (held_cl[:, None] == other_cl[None, :])
            & (held_or[:, None] < other_or[None, :])
            & (other_cl[None, :] >= 0)
        )
        column_best = jnp.max(jnp.where(column_ok, inner, -1.0), axis=0)
        returned = shifted(column_best, "narrow", -distance)
        best = jnp.maximum(best, returned)
    answers = lax.all_to_all(best, "wide", split_axis=0, concat_axis=0, tiled=True)
    return answers[target]


PIECES = 8
AHEAD = 1
SIDE = 4
MESH = pl.DeviceIdType.MESH
NEXT, LAST, RELAY = range(3)


def meet_kernel(emb_far, cl_far, od_far, out, emb, cl, od, got, own, uq, marks, cand, pq, pk, gotpq, gotx, gotz, kbuf, kmeta, asked, ktall,
                colacc, target, racc, gave, res, cacc, cres, cfull, late,
                cas, car, ps, pr, mks, mkr, qs, qr, axs, axr, azs, azr, zs, zr, zms, zmr, ms, mr, xs, xr, fs, fr, ns, nr, rs, rr, ts, tr):
    w = lax.axis_index("wide")
    n = lax.axis_index("narrow")

    def flipped(v, k):
        return (v, v + 1 - 2 * lax.rem(v, 2), lax.rem(v + 2, SIDE), SIDE - 1 - v)[k]

    near, cross, far = (flipped(n, k) for k in (1, 2, 3))
    peers = (near, cross, far)
    mate, over_mate, over = (flipped(w, k) for k in (1, 2, 3))
    early = w < SIDE // 2
    outer = (w == 0) | (w == SIDE - 1)
    inner = (w > 0) & (w < SIDE - 1)
    rows = emb.shape[0]
    half = rows // 2
    f32 = jnp.float32

    def send(s, d, ss, rs_, **who):
        return pltpu.make_async_remote_copy(s, d, ss, rs_, device_id=who, device_id_type=MESH)

    take = [pltpu.make_async_copy(s, d, got.at[k]) for k, (s, d) in enumerate([(cl_far, cl), (od_far, od), (emb_far, emb)])]
    for c in take:
        c.start()
    same_side = [(0, b) for b in range(1, SIDE)] + [(1, b) for b in range(SIDE)]
    far_side = [(a, b) for a in (2, 3) for b in range(SIDE)]
    barrier = pltpu.get_barrier_semaphore()

    def greet(a, b):
        pl.semaphore_signal(barrier, inc=1, device_id={"wide": flipped(w, a), "narrow": flipped(n, b)}, device_id_type=MESH)

    for a, b in same_side:
        if a == 0:
            greet(a, b)

    @pl.when(w != SIDE - 1)
    def _():
        for b in range(SIDE):
            greet(1, b)

    @pl.when(early)
    def _():
        for a, b in far_side:
            greet(a, b)

    take[0].wait()
    take[1].wait()
    id_row = cl[...].astype(f32)
    od_row = od[...].astype(f32)
    spot = lax.broadcasted_iota(jnp.int32, (1, 128), 1).astype(f32)
    fits = jnp.zeros((1, 128), f32)
    for o in range(SIDE):
        mine = jnp.where((id_row >= o * CPO) & (id_row < (o + 1) * CPO), 1.0, 0.0)
        fits = jnp.where((spot == o) & (jnp.sum(mine, axis=1, keepdims=True) == half), 1.0, fits)
    cand[0] = fits

    def lowest(mask):
        return jnp.min(jnp.where(mask > 0.5, spot, jnp.float32(SIDE)), axis=1, keepdims=True)

    @pl.when(early)
    def _():
        pl.semaphore_wait(barrier, len(same_side))

    @pl.when(w == SIDE // 2)
    def _():
        pl.semaphore_wait(barrier, len(same_side) + len(far_side) - SIDE)
        pl.semaphore_signal(late.at[0], inc=1, device_id={"wide": 1}, device_id_type=MESH)

    @pl.when(w == SIDE - 1)
    def _():
        pl.semaphore_wait(barrier, len(same_side) + len(far_side))
        pl.semaphore_signal(late.at[1], inc=1, device_id={"wide": 1}, device_id_type=MESH)
        for b in range(SIDE):
            pl.semaphore_signal(late.at[2], inc=1, device_id={"wide": 2, "narrow": b}, device_id_type=MESH)

    z_part = [pl.ds(c * (half // PIECES), half // PIECES) for c in range(PIECES)]
    votes = {
        (a, b): send(cand.at[0], cand.at[a * SIDE + b], cas.at[a * SIDE + b], car.at[a * SIDE + b],
                     wide=flipped(w, a), narrow=flipped(n, b))
        for a, b in same_side + far_side
    }
    sums = [send(cand.at[SIDE * SIDE], cand.at[SIDE * SIDE + 1], ps.at[k], pr, wide=who) for k, who in enumerate((over, over_mate))]
    @pl.when(w >= SIDE // 2)
    def _():
        for k in far_side:
            votes[k].start()

    for k in same_side:
        if k[0] == 0:
            votes[k].start()

    @pl.when(w != SIDE // 2)
    def _():
        for b in range(SIDE):
            votes[1, b].start()

    take[2].wait()

    def normed(values):
        values = values.astype(f32)
        return (values * lax.rsqrt(jnp.sum(values * values, axis=1, keepdims=True) + 1e-06)).astype(jnp.bfloat16)

    own[...] = normed(emb[...])
    local = lowest(fits)
    first = jnp.where((id_row >= local * CPO) & (id_row < (local + 1.0) * CPO), 1.0, 0.0)
    deep = lax.broadcasted_iota(jnp.int32, (rows, rows), 0)
    long = lax.broadcasted_iota(jnp.int32, (rows, rows), 1)
    tri = jnp.where(deep < long, 1.0, 0.0).astype(jnp.bfloat16)
    rank = jnp.dot(jnp.broadcast_to(first, (16, rows)).astype(jnp.bfloat16), tri, preferred_element_type=f32)[0:1]
    lane = lax.broadcasted_iota(jnp.int32, (1, rows), 1).astype(f32)
    place = jnp.where(first > 0.5, rank, half + lane - rank)
    pick = jnp.where(deep.astype(f32) == place, 1.0, 0.0).astype(jnp.bfloat16)
    pq_out = [[send(pq.at[k, p], gotpq.at[k, p], qs.at[k, c], qr.at[k, c], wide=mate) for c, p in enumerate(z_part)] for k in range(2)]
    ahead = 2
    pq[0] = jnp.dot(pick[:half], own[...], preferred_element_type=f32).astype(jnp.bfloat16)

    @pl.when(outer)
    def _():
        for c in pq_out[0][:ahead]:
            c.start()

    od_high = jnp.floor(od_row * (1.0 / 128))
    od_low = od_row - od_high * 128
    digits = [jnp.broadcast_to(r, (16, rows)).astype(jnp.bfloat16) for r in (id_row, od_high, od_low)]
    marked = [pair_inner(t, pick)[0:1] for t in digits]
    marks[0] = jnp.concatenate([marked[0], marked[1] * 128 + marked[2]], axis=0)
    tells = {
        (a, b): send(marks.at[0], marks.at[a * SIDE + b], mks.at[a * SIDE + b], mkr.at[a * SIDE + b],
                     wide=flipped(w, a), narrow=flipped(n, b))
        for a, b in same_side
    }

    @pl.when(w == SIDE // 2)
    def _():
        pl.semaphore_wait(late.at[2], SIDE)
        for b in range(SIDE):
            votes[1, b].start()

    for c in tells.values():
        c.start()

    @pl.when(outer)
    def _():
        for c in pq_out[0][ahead:]:
            c.start()

    pq[1] = jnp.dot(pick[half:], own[...], preferred_element_type=f32).astype(jnp.bfloat16)

    @pl.when(outer)
    def _():
        for c in pq_out[1]:
            c.start()

    def both(dst, ss, sr, **who):
        return [[send(pq.at[k, p], dst.at[k, p], ss.at[k, c], sr.at[k, c], **who) for c, p in enumerate(z_part[:AHEAD])] for k in range(2)]

    x_ahead = both(gotx, axs, axr, narrow=cross)
    z_ahead = both(gotz, azs, azr, wide=over)
    for c in x_ahead[0] + x_ahead[1]:
        c.start()

    @pl.when(w == SIDE // 2)
    def _():
        for c in z_ahead[0] + z_ahead[1]:
            c.start()

    for k in same_side:
        votes[k].wait_recv()
    cand[SIDE * SIDE] = jnp.min(cand[0:2 * SIDE], axis=0)

    @pl.when(w == 1)
    def _():
        for k, c in enumerate(sums):
            pl.semaphore_wait(late.at[k], 1)
            c.start()
        for c in z_ahead[0] + z_ahead[1]:
            c.start()

    @pl.when(early)
    def _():
        for k in far_side:
            votes[k].wait_recv()
        cand[SIDE * SIDE + 2] = jnp.min(cand[2 * SIDE:4 * SIDE], axis=0)

    @pl.when(w >= SIDE // 2)
    def _():
        sums[0].wait_recv()
        cand[SIDE * SIDE + 2] = cand[SIDE * SIDE + 1]

    shared = jnp.minimum(cand[SIDE * SIDE], cand[SIDE * SIDE + 2])

    def turn(fit):
        agreed = jnp.where(lowest(shared) == lowest(fit), 1.0, 0.0)
        return jnp.where(early, 1.0 - agreed, agreed)

    swap = turn(fits)
    mate_swap = turn(cand[SIDE])

    def choose(flag, a, b):
        return jnp.where(flag > 0.5, b.astype(f32), a.astype(f32)).astype(jnp.bfloat16)

    def way(src, msrc, dst, ss):
        row = [send(src.at[p], kbuf.at[dst, p], zs.at[ss, c], zr.at[dst, c], wide=over) for c, p in enumerate(z_part)]
        return send(msrc, kmeta.at[dst], zms.at[ss], zmr.at[dst], wide=over), row

    t_in_away, in_away = way(pk, kmeta.at[2], NEXT, 0)
    t_in_next, in_next = way(kbuf.at[RELAY], kmeta.at[3], LAST, 1)
    to_mate = [send(pk.at[p], uq.at[1, p], ms.at[c], mr.at[c], wide=mate) for c, p in enumerate(z_part)]
    behind = [pl.ds(half + c * (half // PIECES), half // PIECES) for c in range(PIECES)]
    x_out = [[send(uq.at[k, p], uq.at[2 + k, p], xs.at[k, c], xr.at[k, c], narrow=cross) for c, p in enumerate(z_part)] for k in range(2)]
    x_on = [
        [send(uq.at[2 + k, p], uq.at[2 + k, behind[c]], fs.at[k, c], fr.at[k, c], narrow=near) for c, p in enumerate(z_part)]
        for k in range(2)
    ]
    beside = [send(uq.at[k, pl.ds(0, half)], uq.at[k, pl.ds(half, half)], ns.at[k], nr.at[k], narrow=near) for k in range(2)]

    def tag_half(slot, flag):
        return jnp.where(flag > 0.5, marks[slot, :, half:], marks[slot, :, :half])

    @pl.when(inner)
    def _():
        kmeta[2, 0:2] = tag_half(0, swap)
        kmeta[2, 2:3] = jnp.broadcast_to(swap, (1, half))
        t_in_away.start()

    hub = jnp.where(inner, 1.0 - swap, swap)
    for c, p in list(enumerate(z_part))[AHEAD:] + list(enumerate(z_part))[:AHEAD]:
        @pl.when(inner)
        def _():
            pk[p] = choose(swap, pq[0, p], pq[1, p])
            if c >= AHEAD:
                in_away[c].start()

        uq[0, p] = choose(hub, pq[0, p], pq[1, p])
        if c >= AHEAD:
            x_out[0][c].start()
    beside[0].start()

    @pl.when(inner)
    def _():
        for c in to_mate:
            c.start()
        tells[1, 0].wait_recv()
        kmeta[3, 0:2] = tag_half(SIDE, mate_swap)
        kmeta[3, 2:3] = jnp.broadcast_to(mate_swap, (1, half))
        t_in_next.start()

    @pl.when(outer)
    def _():
        tells[1, 0].wait_recv()

    target[...] = jnp.where(swap > 0.5, jnp.where(place < half, place + half, place - half), place)
    for k in same_side:
        if k != (1, 0):
            tells[k].wait_recv()
    for j in range(4):
        for k in range(2):
            slot = (j % 2) * SIDE + (j // 2) * 2 + k
            flag = turn(cand[slot])
            asked[j, :, k * half:(k + 1) * half] = tag_half(slot, jnp.where(inner, 1.0 - flag, flag))

    def tall(row):
        return jnp.broadcast_to(row, (128, row.shape[1])).T

    for k in range(2):
        for r in range(2):
            ktall[k, r] = tall(asked[k, r:r + 1, :half])

    def stack(parts):
        return parts[0] if len(parts) == 1 else jnp.concatenate(parts, axis=0)

    def tag_of(pieces, r):
        return stack([jnp.concatenate([ktall[s, r, lo:hi]] * (rows // 128), axis=1) for s, lo, hi in pieces])

    def own_part(js):
        pieces = [(0, 0, half), (1, 0, half)]
        keys = stack([uq[0, :half], uq[1, :half]])
        k_cl, k_od = tag_of(pieces, 0), tag_of(pieces, 1)
        for j in js:
            ok = (k_cl == asked[j, 0:1]) & (k_od < asked[j, 1:2])
            racc[j] = jnp.maximum(racc[j], jnp.max(jnp.where(ok, pair_inner(keys, uq[j]), -1.0), axis=0, keepdims=True))

    started = set()

    def met(pieces, js):
        keys = stack([kbuf[s, lo:hi] for s, lo, hi in pieces])
        slots = [(s + 2, lo, hi) for s, lo, hi in pieces]
        k_cl, k_od = tag_of(slots, 0), tag_of(slots, 1)
        col = jnp.full((keys.shape[0], 128), -1.0, f32)
        for j in js:
            same = jnp.where(k_cl == asked[j, 0:1], pair_inner(keys, uq[j]), -1.0)
            before = k_od < asked[j, 1:2]
            racc[j] = jnp.maximum(racc[j], jnp.max(jnp.where(before, same, -1.0), axis=0, keepdims=True))
            after = jnp.where(before, -1.0, same)
            for k in range(rows // 128):
                col = jnp.maximum(col, after[:, k * 128:(k + 1) * 128])
        at = 0
        for s, lo, hi in pieces:
            part = col[at:at + hi - lo]
            at += hi - lo
            if (s, lo) in started:
                part = jnp.maximum(part, colacc[s, lo:hi])
            started.add((s, lo))
            colacc[s, lo:hi] = part

    for j in range(4):
        racc[j] = jnp.full((1, rows), -1.0, f32)
    answers = {
        (a, b): send(gave.at[a * SIDE + b], res.at[a * SIDE + b], rs.at[a * SIDE + b], rr.at[a * SIDE + b],
                     wide=flipped(w, a), narrow=flipped(n, b))
        for a, b in same_side
    }
    backs = [send(cacc.at[s], cres, ts.at[s], tr, wide=who) for s, who in enumerate((over, over_mate))]

    def give(slot):
        cacc[slot] = jnp.max(colacc[slot].T, axis=0, keepdims=True)
        backs[slot].start()

    def answer(j):
        for k in range(2)[::-1]:
            key = (j % 2, (j // 2) * 2 + k)
            gave[key[0] * SIDE + key[1]] = racc[j, :, k * half:(k + 1) * half]
            if key in answers:
                answers[key].start()

    cross_flag = turn(cand[2])
    cross_hub = jnp.where(inner, 1.0 - cross_flag, cross_flag)

    def passed(k, c):
        if k == 0 and c < AHEAD:
            p = part(c)
            x_ahead[0][c].wait_recv()
            x_ahead[1][c].wait_recv()
            uq[2, p] = choose(cross_hub, gotx[0, p], gotx[1, p])
        else:
            x_out[k][c].wait_recv()
        x_on[k][c].start()

    def part(c):
        return slice(c * (half // PIECES), (c + 1) * (half // PIECES))

    quarter = half // 2

    @pl.when(inner)
    def _():
        def settle(c):
            pq_out[0][c].wait_recv()
            pq_out[1][c].wait_recv()
            p = part(c)
            kbuf[RELAY, p] = choose(mate_swap, gotpq[0, p], gotpq[1, p])
            in_next[c].start()
            uq[1, p] = choose(mate_swap, gotpq[1, p], gotpq[0, p])
            x_out[1][c].start()

        for c in range(PIECES):
            passed(0, c)
            settle(c)
        beside[1].start()
        t_in_away.wait_recv()
        t_in_next.wait_recv()
        for s in range(2):
            for r in range(2):
                ktall[s + 2, r] = tall(kmeta[s, r:r + 1])
        beside[0].wait_recv()
        own_part((0,))
        passed(1, 0)
        over_flag = kmeta[NEXT, 2:3, 0:1]
        for c in range(AHEAD):
            z_ahead[0][c].wait_recv()
            z_ahead[1][c].wait_recv()
            kbuf[NEXT, part(c)] = choose(over_flag, gotz[0, part(c)], gotz[1, part(c)])
        for c in in_away[AHEAD:]:
            c.wait_recv()
        met([(NEXT, 0, half)], (0,))
        passed(1, 1)
        for c in x_on[0]:
            c.wait_recv()
        own_part((2,))
        met([(NEXT, 0, half)], (2,))
        passed(1, 2)
        beside[1].wait_recv()
        own_part((1,))
        met([(NEXT, 0, half)], (1,))
        passed(1, 3)
        for c in in_next[:PIECES // 2]:
            c.wait_recv()
        passed(1, 4)
        met([(LAST, 0, quarter)], (0, 1, 2))
        passed(1, 5)
        passed(1, 6)
        for c in in_next[PIECES // 2:]:
            c.wait_recv()
        passed(1, 7)
        met([(LAST, quarter, half)], (0, 1, 2))
        answer(1)
        for c in x_on[1]:
            c.wait_recv()
        met([(LAST, 0, quarter), (LAST, quarter, half), (NEXT, 0, half)], (3,))
        give(LAST)
        own_part((3,))
        answer(3)
        answer(2)
        answer(0)
        give(NEXT)

    @pl.when(outer)
    def _():
        def settle(c):
            to_mate[c].wait_recv()
            x_out[1][c].start()

        for c in range(PIECES):
            passed(0, c)
            settle(c)
        beside[1].start()
        beside[0].wait_recv()
        own_part((0,))
        for c in x_on[0]:
            c.wait_recv()
        own_part((2,))
        beside[1].wait_recv()
        own_part((1,))
        for c in range(PIECES):
            passed(1, c)
        for c in x_on[1]:
            c.wait_recv()
        own_part((3,))
        for j in (3, 2, 1, 0):
            answer(j)

    for c in answers.values():
        c.wait_recv()
    hub_best = jnp.maximum(jnp.maximum(gave[0], res[1]), jnp.maximum(res[2], res[3]))
    other_best = jnp.maximum(jnp.maximum(res[4], res[5]), jnp.maximum(res[6], res[7]))
    backs[0].wait_recv()
    cfull[:, :half] = jnp.maximum(jnp.where(inner, other_best, hub_best), cres[...])
    cfull[:, half:] = jnp.where(inner, hub_best, other_best)
    spread = jnp.broadcast_to(cfull[...], (128, rows)).T
    mine = jnp.where(deep.astype(f32) == target[...], jnp.concatenate([spread] * (rows // 128), axis=1), -1.0)
    out[...] = jnp.max(mine, axis=0, keepdims=True)

    @pl.when(outer)
    def _():
        for c in pq_out[0] + pq_out[1]:
            c.wait_send()

    @pl.when(inner)
    def _():
        for c in [t_in_away, t_in_next] + in_away[AHEAD:] + in_next + to_mate + backs + z_ahead[0] + z_ahead[1]:
            c.wait_send()

    @pl.when(w == 1)
    def _():
        for c in sums:
            c.wait_send()

    @pl.when(w >= SIDE // 2)
    def _():
        for k in far_side:
            votes[k].wait_send()

    for c in [votes[k] for k in same_side] + list(tells.values()) + x_ahead[0] + x_ahead[1] + x_out[0][AHEAD:] + x_out[1] + x_on[0] + x_on[1] + beside:
        c.wait_send()
    for c in answers.values():
        c.wait_send()


def per_device_meet(embeddings, cluster_id, order_index):
    rows, width = embeddings.shape
    half = rows // 2
    dma = pltpu.SemaphoreType.DMA
    vmem = pl.BlockSpec(memory_space=pltpu.VMEM)
    line = lambda k, m: pltpu.VMEM((k, 1, m), jnp.float32)
    block = lambda k, m: pltpu.VMEM((k, m, width), jnp.bfloat16)
    found = pl.pallas_call(
        meet_kernel,
        out_shape=jax.ShapeDtypeStruct((1, rows), jnp.float32),
        in_specs=[pl.BlockSpec(memory_space=pl.ANY)] * 3,
        out_specs=vmem,
        scratch_shapes=[
            pltpu.VMEM((rows, width), jnp.bfloat16), pltpu.VMEM((1, rows), jnp.int32), pltpu.VMEM((1, rows), jnp.int32),
            dma((3,)), pltpu.VMEM((rows, width), jnp.bfloat16), block(4, rows),
            pltpu.VMEM((2 * SIDE, 2, rows), jnp.float32), line(SIDE * SIDE + 3, 128),
            block(2, half), pltpu.VMEM((half, width), jnp.bfloat16), block(2, half), block(2, AHEAD * half // PIECES), block(2, AHEAD * half // PIECES),
            block(3, half), pltpu.VMEM((4, 3, half), jnp.float32), pltpu.VMEM((4, 2, rows), jnp.float32),
            pltpu.VMEM((4, 2, half, 128), jnp.float32), pltpu.VMEM((2, half, 128), jnp.float32),
            pltpu.VMEM((1, rows), jnp.float32),
            line(4, rows), line(2 * SIDE, half), line(2 * SIDE, half), line(2, half), pltpu.VMEM((1, half), jnp.float32),
            pltpu.VMEM((1, rows), jnp.float32), pltpu.SemaphoreType.REGULAR((3,)),
            dma((SIDE * SIDE,)), dma((SIDE * SIDE,)), dma((2,)), dma, dma((2 * SIDE,)), dma((2 * SIDE,)),
            dma((2, PIECES)), dma((2, PIECES)), dma((2, AHEAD)), dma((2, AHEAD)), dma((2, AHEAD)), dma((2, AHEAD)),
            dma((2, PIECES)), dma((2, PIECES)), dma((2,)), dma((2,)),
            dma((PIECES,)), dma((PIECES,)), dma((2, PIECES)), dma((2, PIECES)), dma((2, PIECES)), dma((2, PIECES)),
            dma((2,)), dma((2,)), dma((2 * SIDE,)), dma((2 * SIDE,)), dma((2,)), dma,
        ],
        compiler_params=pltpu.CompilerParams(collective_id=0, has_side_effects=True),
    )(embeddings, cluster_id.reshape(1, rows), order_index.reshape(1, rows))
    return jnp.maximum(found.reshape(rows), -1.0)


def solution(mesh):
    meet = mesh.shape["wide"] == SIDE and mesh.shape["narrow"] == SIDE
    return jax.shard_map(
        per_device_meet if meet else per_device,
        mesh=mesh,
        in_specs=(
            P(("parts", "wide", "narrow"), None),
            P(("parts", "wide", "narrow")),
            P(("parts", "wide", "narrow")),
        ),
        out_specs=P(("parts", "wide", "narrow")),
        check_vma=False,
    )
```

```python
import jax
import jax.numpy as jnp
from jax import lax
from jax.experimental import pallas as pl
from jax.experimental.pallas import tpu as pltpu
from jax.sharding import PartitionSpec as P

CPO = 16


def shifted(shard, axis, by):
    count = lax.axis_size(axis)
    return lax.ppermute(shard, axis, [(i, (i + by) % count) for i in range(count)])


def pair_inner(left, right):
    return lax.dot_general(
        left, right, (((1,), (1,)), ((), ())), preferred_element_type=jnp.float32
    )


def per_device(embeddings, cluster_id, order_index):
    wide_size = lax.axis_size("wide")
    rows = embeddings.shape[0]
    width = embeddings.shape[1]
    bucket = 2 * rows // wide_size
    values = embeddings.astype(jnp.float32)
    unit = (values * lax.rsqrt(jnp.sum(values * values, axis=1, keepdims=True) + 1e-06)).astype(
        jnp.bfloat16
    )
    owner = cluster_id // CPO
    here = jnp.arange(rows, dtype=jnp.int32)
    earlier = (owner[:, None] == owner[None, :]) & (here[None, :] < here[:, None])
    slot = jnp.sum(jnp.where(earlier, 1, 0), axis=1)
    target = owner * bucket + slot
    send_rows = jnp.zeros((wide_size * bucket, width), jnp.bfloat16).at[target].set(unit)
    meta_rows = jnp.stack([cluster_id, order_index], axis=1)
    send_meta = jnp.full((wide_size * bucket, 2), -1, jnp.int32).at[target].set(meta_rows)
    held, held_meta = (
        lax.all_to_all(send_rows, "wide", split_axis=0, concat_axis=0, tiled=True),
        lax.all_to_all(send_meta, "wide", split_axis=0, concat_axis=0, tiled=True),
    )
    held_cl = held_meta[:, 0]
    held_or = held_meta[:, 1]
    live = held_cl >= 0
    start_best = jnp.full((held.shape[0],), -1.0, jnp.float32)

    def row_best(inner, other_cl, other_or):
        allowed = (
            (other_cl[None, :] == held_cl[:, None])
            & (other_or[None, :] < held_or[:, None])
            & live[:, None]
        )
        return jnp.max(jnp.where(allowed, inner, -1.0), axis=1)

    narrow_size = lax.axis_size("narrow")
    best = jnp.maximum(start_best, row_best(pair_inner(held, held), held_cl, held_or))
    for distance in range(1, narrow_size // 2 + 1):
        other_rows, other_meta = shifted((held, held_meta), "narrow", distance)
        other_cl = other_meta[:, 0]
        other_or = other_meta[:, 1]
        inner = pair_inner(held, other_rows)
        best = jnp.maximum(best, row_best(inner, other_cl, other_or))
        column_ok = (
            (held_cl[:, None] == other_cl[None, :])
            & (held_or[:, None] < other_or[None, :])
            & (other_cl[None, :] >= 0)
        )
        column_best = jnp.max(jnp.where(column_ok, inner, -1.0), axis=0)
        returned = shifted(column_best, "narrow", -distance)
        best = jnp.maximum(best, returned)
    answers = lax.all_to_all(best, "wide", split_axis=0, concat_axis=0, tiled=True)
    return answers[target]


PIECES = 8
AHEAD = 1
SIDE = 4
MESH = pl.DeviceIdType.MESH
NEXT, LAST, RELAY = range(3)


def meet_kernel(emb_far, cl_far, od_far, out, emb, cl, od, got, own, uq, marks, cand, pq, pk, gotpq, gotx, gotz, kbuf, kmeta, asked, ktall,
                colacc, target, racc, gave, res, cacc, cres, cfull, late,
                cas, car, ps, pr, mks, mkr, qs, qr, axs, axr, azs, azr, zs, zr, zms, zmr, ms, mr, xs, xr, fs, fr, ns, nr, rs, rr, ts, tr):
    w = lax.axis_index("wide")
    n = lax.axis_index("narrow")

    def flipped(v, k):
        return (v, v + 1 - 2 * lax.rem(v, 2), lax.rem(v + 2, SIDE), SIDE - 1 - v)[k]

    near, cross, far = (flipped(n, k) for k in (1, 2, 3))
    peers = (near, cross, far)
    mate, over_mate, over = (flipped(w, k) for k in (1, 2, 3))
    early = w < SIDE // 2
    outer = (w == 0) | (w == SIDE - 1)
    inner = (w > 0) & (w < SIDE - 1)
    rows = emb.shape[0]
    half = rows // 2
    f32 = jnp.float32

    def send(s, d, ss, rs_, **who):
        return pltpu.make_async_remote_copy(s, d, ss, rs_, device_id=who, device_id_type=MESH)

    take = [pltpu.make_async_copy(s, d, got.at[k]) for k, (s, d) in enumerate([(cl_far, cl), (od_far, od), (emb_far, emb)])]
    for c in take:
        c.start()
    same_side = [(0, b) for b in range(1, SIDE)] + [(1, b) for b in range(SIDE)]
    far_side = [(a, b) for a in (2, 3) for b in range(SIDE)]
    barrier = pltpu.get_barrier_semaphore()

    def greet(a, b):
        pl.semaphore_signal(barrier, inc=1, device_id={"wide": flipped(w, a), "narrow": flipped(n, b)}, device_id_type=MESH)

    for a, b in same_side:
        if a == 0:
            greet(a, b)

    @pl.when(w != SIDE - 1)
    def _():
        for b in range(SIDE):
            greet(1, b)

    @pl.when(early)
    def _():
        for a, b in far_side:
            greet(a, b)

    take[0].wait()
    take[1].wait()
    id_row = cl[...].astype(f32)
    od_row = od[...].astype(f32)
    spot = lax.broadcasted_iota(jnp.int32, (1, 128), 1).astype(f32)
    fits = jnp.zeros((1, 128), f32)
    for o in range(SIDE):
        mine = jnp.where((id_row >= o * CPO) & (id_row < (o + 1) * CPO), 1.0, 0.0)
        fits = jnp.where((spot == o) & (jnp.sum(mine, axis=1, keepdims=True) == half), 1.0, fits)
    cand[0] = fits

    def lowest(mask):
        return jnp.min(jnp.where(mask > 0.5, spot, jnp.float32(SIDE)), axis=1, keepdims=True)

    @pl.when(early)
    def _():
        pl.semaphore_wait(barrier, len(same_side))

    @pl.when(w == SIDE // 2)
    def _():
        pl.semaphore_wait(barrier, len(same_side) + len(far_side) - SIDE)
        pl.semaphore_signal(late.at[0], inc=1, device_id={"wide": 1}, device_id_type=MESH)

    @pl.when(w == SIDE - 1)
    def _():
        pl.semaphore_wait(barrier, len(same_side) + len(far_side))
        pl.semaphore_signal(late.at[1], inc=1, device_id={"wide": 1}, device_id_type=MESH)
        for b in range(SIDE):
            pl.semaphore_signal(late.at[2], inc=1, device_id={"wide": 2, "narrow": b}, device_id_type=MESH)

    z_part = [pl.ds(c * (half // PIECES), half // PIECES) for c in range(PIECES)]
    votes = {
        (a, b): send(cand.at[0], cand.at[a * SIDE + b], cas.at[a * SIDE + b], car.at[a * SIDE + b],
                     wide=flipped(w, a), narrow=flipped(n, b))
        for a, b in same_side + far_side
    }
    sums = [send(cand.at[SIDE * SIDE], cand.at[SIDE * SIDE + 1], ps.at[k], pr, wide=who) for k, who in enumerate((over, over_mate))]
    @pl.when(w >= SIDE // 2)
    def _():
        for k in far_side:
            votes[k].start()

    for k in same_side:
        if k[0] == 0:
            votes[k].start()

    @pl.when(w != SIDE // 2)
    def _():
        for b in range(SIDE):
            votes[1, b].start()

    take[2].wait()

    def normed(values):
        values = values.astype(f32)
        return (values * lax.rsqrt(jnp.sum(values * values, axis=1, keepdims=True) + 1e-06)).astype(jnp.bfloat16)

    own[...] = normed(emb[...])
    local = lowest(fits)
    first = jnp.where((id_row >= local * CPO) & (id_row < (local + 1.0) * CPO), 1.0, 0.0)
    deep = lax.broadcasted_iota(jnp.int32, (rows, rows), 0)
    long = lax.broadcasted_iota(jnp.int32, (rows, rows), 1)
    tri = jnp.where(deep < long, 1.0, 0.0).astype(jnp.bfloat16)
    rank = jnp.dot(jnp.broadcast_to(first, (16, rows)).astype(jnp.bfloat16), tri, preferred_element_type=f32)[0:1]
    lane = lax.broadcasted_iota(jnp.int32, (1, rows), 1).astype(f32)
    place = jnp.where(first > 0.5, rank, half + lane - rank)
    pick = jnp.where(deep.astype(f32) == place, 1.0, 0.0).astype(jnp.bfloat16)
    pq_out = [[send(pq.at[k, p], gotpq.at[k, p], qs.at[k, c], qr.at[k, c], wide=mate) for c, p in enumerate(z_part)] for k in range(2)]
    ahead = 2
    pq[0] = jnp.dot(pick[:half], own[...], preferred_element_type=f32).astype(jnp.bfloat16)

    @pl.when(outer)
    def _():
        for c in pq_out[0][:ahead]:
            c.start()

    od_high = jnp.floor(od_row * (1.0 / 128))
    od_low = od_row - od_high * 128
    digits = [jnp.broadcast_to(r, (16, rows)).astype(jnp.bfloat16) for r in (id_row, od_high, od_low)]
    marked = [pair_inner(t, pick)[0:1] for t in digits]
    marks[0] = jnp.concatenate([marked[0], marked[1] * 128 + marked[2]], axis=0)
    tells = {
        (a, b): send(marks.at[0], marks.at[a * SIDE + b], mks.at[a * SIDE + b], mkr.at[a * SIDE + b],
                     wide=flipped(w, a), narrow=flipped(n, b))
        for a, b in same_side
    }

    @pl.when(w == SIDE // 2)
    def _():
        pl.semaphore_wait(late.at[2], SIDE)
        for b in range(SIDE):
            votes[1, b].start()

    for c in tells.values():
        c.start()

    @pl.when(outer)
    def _():
        for c in pq_out[0][ahead:]:
            c.start()

    pq[1] = jnp.dot(pick[half:], own[...], preferred_element_type=f32).astype(jnp.bfloat16)

    @pl.when(outer)
    def _():
        for c in pq_out[1]:
            c.start()

    def both(dst, ss, sr, **who):
        return [[send(pq.at[k, p], dst.at[k, p], ss.at[k, c], sr.at[k, c], **who) for c, p in enumerate(z_part[:AHEAD])] for k in range(2)]

    x_ahead = both(gotx, axs, axr, narrow=cross)
    z_ahead = both(gotz, azs, azr, wide=over)
    for c in x_ahead[0] + x_ahead[1]:
        c.start()

    @pl.when(w == SIDE // 2)
    def _():
        for c in z_ahead[0] + z_ahead[1]:
            c.start()

    for k in same_side:
        votes[k].wait_recv()
    cand[SIDE * SIDE] = jnp.min(cand[0:2 * SIDE], axis=0)

    @pl.when(w == 1)
    def _():
        for k, c in enumerate(sums):
            pl.semaphore_wait(late.at[k], 1)
            c.start()
        for c in z_ahead[0] + z_ahead[1]:
            c.start()

    @pl.when(early)
    def _():
        for k in far_side:
            votes[k].wait_recv()
        cand[SIDE * SIDE + 2] = jnp.min(cand[2 * SIDE:4 * SIDE], axis=0)

    @pl.when(w >= SIDE // 2)
    def _():
        sums[0].wait_recv()
        cand[SIDE * SIDE + 2] = cand[SIDE * SIDE + 1]

    shared = jnp.minimum(cand[SIDE * SIDE], cand[SIDE * SIDE + 2])

    def turn(fit):
        agreed = jnp.where(lowest(shared) == lowest(fit), 1.0, 0.0)
        return jnp.where(early, 1.0 - agreed, agreed)

    swap = turn(fits)
    mate_swap = turn(cand[SIDE])

    def choose(flag, a, b):
        return jnp.where(flag > 0.5, b.astype(f32), a.astype(f32)).astype(jnp.bfloat16)

    def way(src, msrc, dst, ss):
        row = [send(src.at[p], kbuf.at[dst, p], zs.at[ss, c], zr.at[dst, c], wide=over) for c, p in enumerate(z_part)]
        return send(msrc, kmeta.at[dst], zms.at[ss], zmr.at[dst], wide=over), row

    t_in_away, in_away = way(pk, kmeta.at[2], NEXT, 0)
    t_in_next, in_next = way(kbuf.at[RELAY], kmeta.at[3], LAST, 1)
    to_mate = [send(pk.at[p], uq.at[1, p], ms.at[c], mr.at[c], wide=mate) for c, p in enumerate(z_part)]
    behind = [pl.ds(half + c * (half // PIECES), half // PIECES) for c in range(PIECES)]
    x_out = [[send(uq.at[k, p], uq.at[2 + k, p], xs.at[k, c], xr.at[k, c], narrow=cross) for c, p in enumerate(z_part)] for k in range(2)]
    x_on = [
        [send(uq.at[2 + k, p], uq.at[2 + k, behind[c]], fs.at[k, c], fr.at[k, c], narrow=near) for c, p in enumerate(z_part)]
        for k in range(2)
    ]
    beside = [send(uq.at[k, pl.ds(0, half)], uq.at[k, pl.ds(half, half)], ns.at[k], nr.at[k], narrow=near) for k in range(2)]

    def tag_half(slot, flag):
        return jnp.where(flag > 0.5, marks[slot, :, half:], marks[slot, :, :half])

    @pl.when(inner)
    def _():
        kmeta[2, 0:2] = tag_half(0, swap)
        kmeta[2, 2:3] = jnp.broadcast_to(swap, (1, half))
        t_in_away.start()

    hub = jnp.where(inner, 1.0 - swap, swap)
    for c, p in list(enumerate(z_part))[AHEAD:] + list(enumerate(z_part))[:AHEAD]:
        @pl.when(inner)
        def _():
            pk[p] = choose(swap, pq[0, p], pq[1, p])
            if c >= AHEAD:
                in_away[c].start()

        uq[0, p] = choose(hub, pq[0, p], pq[1, p])
        if c >= AHEAD:
            x_out[0][c].start()
    beside[0].start()

    @pl.when(inner)
    def _():
        for c in to_mate:
            c.start()
        tells[1, 0].wait_recv()
        kmeta[3, 0:2] = tag_half(SIDE, mate_swap)
        kmeta[3, 2:3] = jnp.broadcast_to(mate_swap, (1, half))
        t_in_next.start()

    @pl.when(outer)
    def _():
        tells[1, 0].wait_recv()

    target[...] = jnp.where(swap > 0.5, jnp.where(place < half, place + half, place - half), place)
    for k in same_side:
        if k != (1, 0):
            tells[k].wait_recv()
    for j in range(4):
        for k in range(2):
            slot = (j % 2) * SIDE + (j // 2) * 2 + k
            flag = turn(cand[slot])
            asked[j, :, k * half:(k + 1) * half] = tag_half(slot, jnp.where(inner, 1.0 - flag, flag))

    def tall(row):
        return jnp.broadcast_to(row, (128, row.shape[1])).T

    for k in range(2):
        for r in range(2):
            ktall[k, r] = tall(asked[k, r:r + 1, :half])

    def stack(parts):
        return parts[0] if len(parts) == 1 else jnp.concatenate(parts, axis=0)

    def tag_of(pieces, r):
        return stack([jnp.concatenate([ktall[s, r, lo:hi]] * (rows // 128), axis=1) for s, lo, hi in pieces])

    def own_part(js):
        pieces = [(0, 0, half), (1, 0, half)]
        keys = stack([uq[0, :half], uq[1, :half]])
        k_cl, k_od = tag_of(pieces, 0), tag_of(pieces, 1)
        for j in js:
            ok = (k_cl == asked[j, 0:1]) & (k_od < asked[j, 1:2])
            racc[j] = jnp.maximum(racc[j], jnp.max(jnp.where(ok, pair_inner(keys, uq[j]), -1.0), axis=0, keepdims=True))

    started = set()

    def met(pieces, js):
        keys = stack([kbuf[s, lo:hi] for s, lo, hi in pieces])
        slots = [(s + 2, lo, hi) for s, lo, hi in pieces]
        k_cl, k_od = tag_of(slots, 0), tag_of(slots, 1)
        col = jnp.full((keys.shape[0], 128), -1.0, f32)
        for j in js:
            same = jnp.where(k_cl == asked[j, 0:1], pair_inner(keys, uq[j]), -1.0)
            before = k_od < asked[j, 1:2]
            racc[j] = jnp.maximum(racc[j], jnp.max(jnp.where(before, same, -1.0), axis=0, keepdims=True))
            after = jnp.where(before, -1.0, same)
            for k in range(rows // 128):
                col = jnp.maximum(col, after[:, k * 128:(k + 1) * 128])
        at = 0
        for s, lo, hi in pieces:
            part = col[at:at + hi - lo]
            at += hi - lo
            if (s, lo) in started:
                part = jnp.maximum(part, colacc[s, lo:hi])
            started.add((s, lo))
            colacc[s, lo:hi] = part

    def final():
        pieces = [(s, 0, half) for s in (2 + LAST, 2 + NEXT, 0, 1)]
        keys = stack([kbuf[LAST], kbuf[NEXT], uq[0, :half], uq[1, :half]])
        k_cl, k_od = tag_of(pieces, 0), tag_of(pieces, 1)
        same = jnp.where(k_cl == asked[3, 0:1], pair_inner(keys, uq[3]), -1.0)
        before = k_od < asked[3, 1:2]
        after = jnp.where(before[:rows], -1.0, same[:rows])
        for k in range(rows // 128):
            for s, lo in ((LAST, 0), (NEXT, half)):
                colacc[s] = jnp.maximum(colacc[s], after[lo:lo + half, k * 128:(k + 1) * 128])
        racc[3] = jnp.max(jnp.where(before, same, -1.0), axis=0, keepdims=True)

    for j in range(4):
        racc[j] = jnp.full((1, rows), -1.0, f32)
    answers = {
        (a, b): send(gave.at[a * SIDE + b], res.at[a * SIDE + b], rs.at[a * SIDE + b], rr.at[a * SIDE + b],
                     wide=flipped(w, a), narrow=flipped(n, b))
        for a, b in same_side
    }
    backs = [send(cacc.at[s], cres, ts.at[s], tr, wide=who) for s, who in enumerate((over, over_mate))]

    def give(slot):
        cacc[slot] = jnp.max(colacc[slot].T, axis=0, keepdims=True)
        backs[slot].start()

    def answer(j):
        for k in range(2)[::-1]:
            key = (j % 2, (j // 2) * 2 + k)
            gave[key[0] * SIDE + key[1]] = racc[j, :, k * half:(k + 1) * half]
            if key in answers:
                answers[key].start()

    cross_flag = turn(cand[2])
    cross_hub = jnp.where(inner, 1.0 - cross_flag, cross_flag)

    def passed(k, c):
        if k == 0 and c < AHEAD:
            p = part(c)
            x_ahead[0][c].wait_recv()
            x_ahead[1][c].wait_recv()
            uq[2, p] = choose(cross_hub, gotx[0, p], gotx[1, p])
        else:
            x_out[k][c].wait_recv()
        x_on[k][c].start()

    def part(c):
        return slice(c * (half // PIECES), (c + 1) * (half // PIECES))

    quarter = half // 2

    @pl.when(inner)
    def _():
        def settle(c):
            pq_out[0][c].wait_recv()
            pq_out[1][c].wait_recv()
            p = part(c)
            kbuf[RELAY, p] = choose(mate_swap, gotpq[0, p], gotpq[1, p])
            in_next[c].start()
            uq[1, p] = choose(mate_swap, gotpq[1, p], gotpq[0, p])
            x_out[1][c].start()

        for c in range(PIECES):
            settle(c)
            passed(0, c)
        beside[1].start()
        passed(1, 0)
        passed(1, 1)
        t_in_away.wait_recv()
        t_in_next.wait_recv()
        for s in range(2):
            for r in range(2):
                ktall[s + 2, r] = tall(kmeta[s, r:r + 1])
        beside[0].wait_recv()
        own_part((0,))
        over_flag = kmeta[NEXT, 2:3, 0:1]
        for c in range(AHEAD):
            z_ahead[0][c].wait_recv()
            z_ahead[1][c].wait_recv()
            kbuf[NEXT, part(c)] = choose(over_flag, gotz[0, part(c)], gotz[1, part(c)])
        for c in in_away[AHEAD:]:
            c.wait_recv()
        met([(NEXT, 0, half)], (0,))
        for c in x_on[0]:
            c.wait_recv()
        own_part((2,))
        met([(NEXT, 0, half)], (2,))
        passed(1, 2)
        beside[1].wait_recv()
        own_part((1,))
        met([(NEXT, 0, half)], (1,))
        passed(1, 3)
        for c in in_next[:PIECES // 2]:
            c.wait_recv()
        passed(1, 4)
        met([(LAST, 0, quarter)], (0, 1, 2))
        passed(1, 5)
        passed(1, 6)
        passed(1, 7)
        for c in in_next[PIECES // 2:]:
            c.wait_recv()
        met([(LAST, quarter, half)], (0, 1, 2))
        answer(1)
        for c in x_on[1]:
            c.wait_recv()
        final()
        give(LAST)
        answer(3)
        answer(2)
        answer(0)
        give(NEXT)

    @pl.when(outer)
    def _():
        def settle(c):
            to_mate[c].wait_recv()
            x_out[1][c].start()

        for c in range(PIECES):
            passed(0, c)
            settle(c)
        beside[1].start()
        beside[0].wait_recv()
        own_part((0,))
        for c in x_on[0]:
            c.wait_recv()
        own_part((2,))
        beside[1].wait_recv()
        own_part((1,))
        for c in range(PIECES):
            passed(1, c)
        for c in x_on[1]:
            c.wait_recv()
        own_part((3,))
        for j in (3, 2, 1, 0):
            answer(j)

    @pl.when(outer)
    def _():
        for c in pq_out[0] + pq_out[1]:
            c.wait_send()

    @pl.when(inner)
    def _():
        for c in [t_in_away, t_in_next] + in_away[AHEAD:] + in_next + to_mate + z_ahead[0] + z_ahead[1]:
            c.wait_send()

    @pl.when(w == 1)
    def _():
        for c in sums:
            c.wait_send()

    @pl.when(w >= SIDE // 2)
    def _():
        for k in far_side:
            votes[k].wait_send()

    for c in [votes[k] for k in same_side] + list(tells.values()) + x_ahead[0] + x_ahead[1] + x_out[0][AHEAD:] + x_out[1] + x_on[0] + x_on[1] + beside:
        c.wait_send()

    for c in answers.values():
        c.wait_recv()
    hub_best = jnp.maximum(jnp.maximum(gave[0], res[1]), jnp.maximum(res[2], res[3]))
    other_best = jnp.maximum(jnp.maximum(res[4], res[5]), jnp.maximum(res[6], res[7]))
    backs[0].wait_recv()
    cfull[:, :half] = jnp.maximum(jnp.where(inner, other_best, hub_best), cres[...])
    cfull[:, half:] = jnp.where(inner, hub_best, other_best)
    spread = jnp.broadcast_to(cfull[...], (128, rows)).T
    mine = jnp.where(deep.astype(f32) == target[...], jnp.concatenate([spread] * (rows // 128), axis=1), -1.0)
    out[...] = jnp.max(mine, axis=0, keepdims=True)


    @pl.when(inner)
    def _():
        for c in backs:
            c.wait_send()

    for c in answers.values():
        c.wait_send()


def per_device_meet(embeddings, cluster_id, order_index):
    rows, width = embeddings.shape
    half = rows // 2
    dma = pltpu.SemaphoreType.DMA
    vmem = pl.BlockSpec(memory_space=pltpu.VMEM)
    line = lambda k, m: pltpu.VMEM((k, 1, m), jnp.float32)
    block = lambda k, m: pltpu.VMEM((k, m, width), jnp.bfloat16)
    found = pl.pallas_call(
        meet_kernel,
        out_shape=jax.ShapeDtypeStruct((1, rows), jnp.float32),
        in_specs=[pl.BlockSpec(memory_space=pl.ANY)] * 3,
        out_specs=vmem,
        scratch_shapes=[
            pltpu.VMEM((rows, width), jnp.bfloat16), pltpu.VMEM((1, rows), jnp.int32), pltpu.VMEM((1, rows), jnp.int32),
            dma((3,)), pltpu.VMEM((rows, width), jnp.bfloat16), block(4, rows),
            pltpu.VMEM((2 * SIDE, 2, rows), jnp.float32), line(SIDE * SIDE + 3, 128),
            block(2, half), pltpu.VMEM((half, width), jnp.bfloat16), block(2, half), block(2, AHEAD * half // PIECES), block(2, AHEAD * half // PIECES),
            block(3, half), pltpu.VMEM((4, 3, half), jnp.float32), pltpu.VMEM((4, 2, rows), jnp.float32),
            pltpu.VMEM((4, 2, half, 128), jnp.float32), pltpu.VMEM((2, half, 128), jnp.float32),
            pltpu.VMEM((1, rows), jnp.float32),
            line(4, rows), line(2 * SIDE, half), line(2 * SIDE, half), line(2, half), pltpu.VMEM((1, half), jnp.float32),
            pltpu.VMEM((1, rows), jnp.float32), pltpu.SemaphoreType.REGULAR((3,)),
            dma((SIDE * SIDE,)), dma((SIDE * SIDE,)), dma((2,)), dma, dma((2 * SIDE,)), dma((2 * SIDE,)),
            dma((2, PIECES)), dma((2, PIECES)), dma((2, AHEAD)), dma((2, AHEAD)), dma((2, AHEAD)), dma((2, AHEAD)),
            dma((2, PIECES)), dma((2, PIECES)), dma((2,)), dma((2,)),
            dma((PIECES,)), dma((PIECES,)), dma((2, PIECES)), dma((2, PIECES)), dma((2, PIECES)), dma((2, PIECES)),
            dma((2,)), dma((2,)), dma((2 * SIDE,)), dma((2 * SIDE,)), dma((2,)), dma,
        ],
        compiler_params=pltpu.CompilerParams(collective_id=0, has_side_effects=True, vmem_limit_bytes=56500000),
    )(embeddings, cluster_id.reshape(1, rows), order_index.reshape(1, rows))
    return jnp.maximum(found.reshape(rows), -1.0)


def solution(mesh):
    meet = mesh.shape["wide"] == SIDE and mesh.shape["narrow"] == SIDE
    return jax.shard_map(
        per_device_meet if meet else per_device,
        mesh=mesh,
        in_specs=(
            P(("parts", "wide", "narrow"), None),
            P(("parts", "wide", "narrow")),
            P(("parts", "wide", "narrow")),
        ),
        out_specs=P(("parts", "wide", "narrow")),
        check_vma=False,
    )
```

```python
import jax
import jax.numpy as jnp
from jax import lax
from jax.experimental import pallas as pl
from jax.experimental.pallas import tpu as pltpu
from jax.sharding import PartitionSpec as P

CPO = 16


def shifted(shard, axis, by):
    count = lax.axis_size(axis)
    return lax.ppermute(shard, axis, [(i, (i + by) % count) for i in range(count)])


def pair_inner(left, right):
    return lax.dot_general(
        left, right, (((1,), (1,)), ((), ())), preferred_element_type=jnp.float32
    )


def per_device(embeddings, cluster_id, order_index):
    wide_size = lax.axis_size("wide")
    rows = embeddings.shape[0]
    width = embeddings.shape[1]
    bucket = 2 * rows // wide_size
    values = embeddings.astype(jnp.float32)
    unit = (values * lax.rsqrt(jnp.sum(values * values, axis=1, keepdims=True) + 1e-06)).astype(
        jnp.bfloat16
    )
    owner = cluster_id // CPO
    here = jnp.arange(rows, dtype=jnp.int32)
    earlier = (owner[:, None] == owner[None, :]) & (here[None, :] < here[:, None])
    slot = jnp.sum(jnp.where(earlier, 1, 0), axis=1)
    target = owner * bucket + slot
    send_rows = jnp.zeros((wide_size * bucket, width), jnp.bfloat16).at[target].set(unit)
    meta_rows = jnp.stack([cluster_id, order_index], axis=1)
    send_meta = jnp.full((wide_size * bucket, 2), -1, jnp.int32).at[target].set(meta_rows)
    held, held_meta = (
        lax.all_to_all(send_rows, "wide", split_axis=0, concat_axis=0, tiled=True),
        lax.all_to_all(send_meta, "wide", split_axis=0, concat_axis=0, tiled=True),
    )
    held_cl = held_meta[:, 0]
    held_or = held_meta[:, 1]
    live = held_cl >= 0
    start_best = jnp.full((held.shape[0],), -1.0, jnp.float32)

    def row_best(inner, other_cl, other_or):
        allowed = (
            (other_cl[None, :] == held_cl[:, None])
            & (other_or[None, :] < held_or[:, None])
            & live[:, None]
        )
        return jnp.max(jnp.where(allowed, inner, -1.0), axis=1)

    narrow_size = lax.axis_size("narrow")
    best = jnp.maximum(start_best, row_best(pair_inner(held, held), held_cl, held_or))
    for distance in range(1, narrow_size // 2 + 1):
        other_rows, other_meta = shifted((held, held_meta), "narrow", distance)
        other_cl = other_meta[:, 0]
        other_or = other_meta[:, 1]
        inner = pair_inner(held, other_rows)
        best = jnp.maximum(best, row_best(inner, other_cl, other_or))
        column_ok = (
            (held_cl[:, None] == other_cl[None, :])
            & (held_or[:, None] < other_or[None, :])
            & (other_cl[None, :] >= 0)
        )
        column_best = jnp.max(jnp.where(column_ok, inner, -1.0), axis=0)
        returned = shifted(column_best, "narrow", -distance)
        best = jnp.maximum(best, returned)
    answers = lax.all_to_all(best, "wide", split_axis=0, concat_axis=0, tiled=True)
    return answers[target]


PIECES = 8
AHEAD = 1
SIDE = 4
MESH = pl.DeviceIdType.MESH
NEXT, LAST, RELAY = range(3)


def meet_kernel(emb_far, cl, od, out, emb, got, own, uq, marks, cand, pq, pk, gotpq, gotx, gotz, kbuf, kmeta, asked, ktall,
                colacc, target, racc, gave, res, cacc, cres, cfull, late,
                cas, car, ps, pr, mks, mkr, qs, qr, axs, axr, azs, azr, zs, zr, zms, zmr, ms, mr, xs, xr, fs, fr, ns, nr, rs, rr, ts, tr):
    w = lax.axis_index("wide")
    n = lax.axis_index("narrow")

    def flipped(v, k):
        return (v, v + 1 - 2 * lax.rem(v, 2), lax.rem(v + 2, SIDE), SIDE - 1 - v)[k]

    near, cross, far = (flipped(n, k) for k in (1, 2, 3))
    peers = (near, cross, far)
    mate, over_mate, over = (flipped(w, k) for k in (1, 2, 3))
    early = w < SIDE // 2
    outer = (w == 0) | (w == SIDE - 1)
    inner = (w > 0) & (w < SIDE - 1)
    rows = emb.shape[0]
    half = rows // 2
    f32 = jnp.float32

    def send(s, d, ss, rs_, **who):
        return pltpu.make_async_remote_copy(s, d, ss, rs_, device_id=who, device_id_type=MESH)

    take = pltpu.make_async_copy(emb_far, emb, got)
    take.start()
    same_side = [(0, b) for b in range(1, SIDE)] + [(1, b) for b in range(SIDE)]
    far_side = [(a, b) for a in (2, 3) for b in range(SIDE)]
    barrier = pltpu.get_barrier_semaphore()

    def greet(a, b):
        pl.semaphore_signal(barrier, inc=1, device_id={"wide": flipped(w, a), "narrow": flipped(n, b)}, device_id_type=MESH)

    for a, b in same_side:
        if a == 0:
            greet(a, b)

    @pl.when(w != SIDE - 1)
    def _():
        for b in range(SIDE):
            greet(1, b)

    @pl.when(early)
    def _():
        for a, b in far_side:
            greet(a, b)

    id_row = cl[...].astype(f32)
    od_row = od[...].astype(f32)
    spot = lax.broadcasted_iota(jnp.int32, (1, 128), 1).astype(f32)
    fits = jnp.zeros((1, 128), f32)
    for o in range(SIDE):
        mine = jnp.where((id_row >= o * CPO) & (id_row < (o + 1) * CPO), 1.0, 0.0)
        fits = jnp.where((spot == o) & (jnp.sum(mine, axis=1, keepdims=True) == half), 1.0, fits)
    cand[0] = fits

    def lowest(mask):
        return jnp.min(jnp.where(mask > 0.5, spot, jnp.float32(SIDE)), axis=1, keepdims=True)

    @pl.when(early)
    def _():
        pl.semaphore_wait(barrier, len(same_side))

    @pl.when(w == SIDE // 2)
    def _():
        pl.semaphore_wait(barrier, len(same_side) + len(far_side) - SIDE)
        pl.semaphore_signal(late.at[0], inc=1, device_id={"wide": 1}, device_id_type=MESH)

    @pl.when(w == SIDE - 1)
    def _():
        pl.semaphore_wait(barrier, len(same_side) + len(far_side))
        pl.semaphore_signal(late.at[1], inc=1, device_id={"wide": 1}, device_id_type=MESH)
        for b in range(SIDE):
            pl.semaphore_signal(late.at[2], inc=1, device_id={"wide": 2, "narrow": b}, device_id_type=MESH)

    z_part = [pl.ds(c * (half // PIECES), half // PIECES) for c in range(PIECES)]
    votes = {
        (a, b): send(cand.at[0], cand.at[a * SIDE + b], cas.at[a * SIDE + b], car.at[a * SIDE + b],
                     wide=flipped(w, a), narrow=flipped(n, b))
        for a, b in same_side + far_side
    }
    sums = [send(cand.at[SIDE * SIDE], cand.at[SIDE * SIDE + 1], ps.at[k], pr, wide=who) for k, who in enumerate((over, over_mate))]
    @pl.when(w >= SIDE // 2)
    def _():
        for k in far_side:
            votes[k].start()

    for k in same_side:
        if k[0] == 0:
            votes[k].start()

    @pl.when(w != SIDE // 2)
    def _():
        for b in range(SIDE):
            votes[1, b].start()

    take.wait()

    def normed(values):
        values = values.astype(f32)
        return (values * lax.rsqrt(jnp.sum(values * values, axis=1, keepdims=True) + 1e-06)).astype(jnp.bfloat16)

    own[...] = normed(emb[...])
    local = lowest(fits)
    first = jnp.where((id_row >= local * CPO) & (id_row < (local + 1.0) * CPO), 1.0, 0.0)
    deep = lax.broadcasted_iota(jnp.int32, (rows, rows), 0)
    long = lax.broadcasted_iota(jnp.int32, (rows, rows), 1)
    tri = jnp.where(deep < long, 1.0, 0.0).astype(jnp.bfloat16)
    rank = jnp.dot(jnp.broadcast_to(first, (16, rows)).astype(jnp.bfloat16), tri, preferred_element_type=f32)[0:1]
    lane = lax.broadcasted_iota(jnp.int32, (1, rows), 1).astype(f32)
    place = jnp.where(first > 0.5, rank, half + lane - rank)
    pick = jnp.where(deep.astype(f32) == place, 1.0, 0.0).astype(jnp.bfloat16)
    pq_out = [[send(pq.at[k, p], gotpq.at[k, p], qs.at[k, c], qr.at[k, c], wide=mate) for c, p in enumerate(z_part)] for k in range(2)]
    ahead = 2
    pq[0] = jnp.dot(pick[:half], own[...], preferred_element_type=f32).astype(jnp.bfloat16)

    @pl.when(outer)
    def _():
        for c in pq_out[0][:ahead]:
            c.start()

    od_high = jnp.floor(od_row * (1.0 / 128))
    od_low = od_row - od_high * 128
    digits = [jnp.broadcast_to(r, (16, rows)).astype(jnp.bfloat16) for r in (id_row, od_high, od_low)]
    marked = [pair_inner(t, pick)[0:1] for t in digits]
    marks[0] = jnp.concatenate([marked[0], marked[1] * 128 + marked[2]], axis=0)
    tells = {
        (a, b): send(marks.at[0], marks.at[a * SIDE + b], mks.at[a * SIDE + b], mkr.at[a * SIDE + b],
                     wide=flipped(w, a), narrow=flipped(n, b))
        for a, b in same_side
    }

    @pl.when(w == SIDE // 2)
    def _():
        pl.semaphore_wait(late.at[2], SIDE)
        for b in range(SIDE):
            votes[1, b].start()

    for c in tells.values():
        c.start()

    @pl.when(outer)
    def _():
        for c in pq_out[0][ahead:]:
            c.start()

    pq[1] = jnp.dot(pick[half:], own[...], preferred_element_type=f32).astype(jnp.bfloat16)

    @pl.when(outer)
    def _():
        for c in pq_out[1]:
            c.start()

    def both(dst, ss, sr, **who):
        return [[send(pq.at[k, p], dst.at[k, p], ss.at[k, c], sr.at[k, c], **who) for c, p in enumerate(z_part[:AHEAD])] for k in range(2)]

    x_ahead = both(gotx, axs, axr, narrow=cross)
    z_ahead = both(gotz, azs, azr, wide=over)
    for c in x_ahead[0] + x_ahead[1]:
        c.start()

    @pl.when(w == SIDE // 2)
    def _():
        for c in z_ahead[0] + z_ahead[1]:
            c.start()

    for k in same_side:
        votes[k].wait_recv()
    cand[SIDE * SIDE] = jnp.min(cand[0:2 * SIDE], axis=0)

    @pl.when(w == 1)
    def _():
        for k, c in enumerate(sums):
            pl.semaphore_wait(late.at[k], 1)
            c.start()
        for c in z_ahead[0] + z_ahead[1]:
            c.start()

    @pl.when(early)
    def _():
        for k in far_side:
            votes[k].wait_recv()
        cand[SIDE * SIDE + 2] = jnp.min(cand[2 * SIDE:4 * SIDE], axis=0)

    @pl.when(w >= SIDE // 2)
    def _():
        sums[0].wait_recv()
        cand[SIDE * SIDE + 2] = cand[SIDE * SIDE + 1]

    shared = jnp.minimum(cand[SIDE * SIDE], cand[SIDE * SIDE + 2])

    def turn(fit):
        agreed = jnp.where(lowest(shared) == lowest(fit), 1.0, 0.0)
        return jnp.where(early, 1.0 - agreed, agreed)

    swap = turn(fits)
    mate_swap = turn(cand[SIDE])

    def choose(flag, a, b):
        return jnp.where(flag > 0.5, b.astype(f32), a.astype(f32)).astype(jnp.bfloat16)

    def way(src, msrc, dst, ss):
        row = [send(src.at[p], kbuf.at[dst, p], zs.at[ss, c], zr.at[dst, c], wide=over) for c, p in enumerate(z_part)]
        return send(msrc, kmeta.at[dst], zms.at[ss], zmr.at[dst], wide=over), row

    t_in_away, in_away = way(pk, kmeta.at[2], NEXT, 0)
    t_in_next, in_next = way(kbuf.at[RELAY], kmeta.at[3], LAST, 1)
    to_mate = [send(pk.at[p], uq.at[1, p], ms.at[c], mr.at[c], wide=mate) for c, p in enumerate(z_part)]
    behind = [pl.ds(half + c * (half // PIECES), half // PIECES) for c in range(PIECES)]
    x_out = [[send(uq.at[k, p], uq.at[2 + k, p], xs.at[k, c], xr.at[k, c], narrow=cross) for c, p in enumerate(z_part)] for k in range(2)]
    x_on = [
        [send(uq.at[2 + k, p], uq.at[2 + k, behind[c]], fs.at[k, c], fr.at[k, c], narrow=near) for c, p in enumerate(z_part)]
        for k in range(2)
    ]
    beside = [send(uq.at[k, pl.ds(0, half)], uq.at[k, pl.ds(half, half)], ns.at[k], nr.at[k], narrow=near) for k in range(2)]

    def tag_half(slot, flag):
        return jnp.where(flag > 0.5, marks[slot, :, half:], marks[slot, :, :half])

    @pl.when(inner)
    def _():
        kmeta[2, 0:2] = tag_half(0, swap)
        kmeta[2, 2:3] = jnp.broadcast_to(swap, (1, half))
        t_in_away.start()

    hub = jnp.where(inner, 1.0 - swap, swap)
    for c, p in list(enumerate(z_part))[AHEAD:] + list(enumerate(z_part))[:AHEAD]:
        @pl.when(inner)
        def _():
            pk[p] = choose(swap, pq[0, p], pq[1, p])
            if c >= AHEAD:
                in_away[c].start()

        uq[0, p] = choose(hub, pq[0, p], pq[1, p])
        if c >= AHEAD:
            x_out[0][c].start()
    beside[0].start()

    @pl.when(inner)
    def _():
        for c in to_mate:
            c.start()
        tells[1, 0].wait_recv()
        kmeta[3, 0:2] = tag_half(SIDE, mate_swap)
        kmeta[3, 2:3] = jnp.broadcast_to(mate_swap, (1, half))
        t_in_next.start()

    @pl.when(outer)
    def _():
        tells[1, 0].wait_recv()

    target[...] = jnp.where(swap > 0.5, jnp.where(place < half, place + half, place - half), place)
    for k in same_side:
        if k != (1, 0):
            tells[k].wait_recv()
    for j in range(4):
        for k in range(2):
            slot = (j % 2) * SIDE + (j // 2) * 2 + k
            flag = turn(cand[slot])
            asked[j, :, k * half:(k + 1) * half] = tag_half(slot, jnp.where(inner, 1.0 - flag, flag))

    def tall(row):
        return jnp.broadcast_to(row, (128, row.shape[1])).T

    for k in range(2):
        for r in range(2):
            ktall[k, r] = tall(asked[k, r:r + 1, :half])

    def stack(parts):
        return parts[0] if len(parts) == 1 else jnp.concatenate(parts, axis=0)

    def tag_of(pieces, r):
        return stack([jnp.concatenate([ktall[s, r, lo:hi]] * (rows // 128), axis=1) for s, lo, hi in pieces])

    def own_part(js):
        pieces = [(0, 0, half), (1, 0, half)]
        keys = stack([uq[0, :half], uq[1, :half]])
        k_cl, k_od = tag_of(pieces, 0), tag_of(pieces, 1)
        for j in js:
            ok = (k_cl == asked[j, 0:1]) & (k_od < asked[j, 1:2])
            racc[j] = jnp.maximum(racc[j], jnp.max(jnp.where(ok, pair_inner(keys, uq[j]), -1.0), axis=0, keepdims=True))

    started = set()

    def met(pieces, js):
        keys = stack([kbuf[s, lo:hi] for s, lo, hi in pieces])
        slots = [(s + 2, lo, hi) for s, lo, hi in pieces]
        k_cl, k_od = tag_of(slots, 0), tag_of(slots, 1)
        col = jnp.full((keys.shape[0], 128), -1.0, f32)
        for j in js:
            same = jnp.where(k_cl == asked[j, 0:1], pair_inner(keys, uq[j]), -1.0)
            before = k_od < asked[j, 1:2]
            racc[j] = jnp.maximum(racc[j], jnp.max(jnp.where(before, same, -1.0), axis=0, keepdims=True))
            after = jnp.where(before, -1.0, same)
            for k in range(rows // 128):
                col = jnp.maximum(col, after[:, k * 128:(k + 1) * 128])
        at = 0
        for s, lo, hi in pieces:
            part = col[at:at + hi - lo]
            at += hi - lo
            if (s, lo) in started:
                part = jnp.maximum(part, colacc[s, lo:hi])
            started.add((s, lo))
            colacc[s, lo:hi] = part

    def final():
        pieces = [(s, 0, half) for s in (2 + LAST, 2 + NEXT, 0, 1)]
        keys = stack([kbuf[LAST], kbuf[NEXT], uq[0, :half], uq[1, :half]])
        k_cl, k_od = tag_of(pieces, 0), tag_of(pieces, 1)
        same = jnp.where(k_cl == asked[3, 0:1], pair_inner(keys, uq[3]), -1.0)
        before = k_od < asked[3, 1:2]
        after = jnp.where(before[:rows], -1.0, same[:rows])
        for k in range(rows // 128):
            for s, lo in ((LAST, 0), (NEXT, half)):
                colacc[s] = jnp.maximum(colacc[s], after[lo:lo + half, k * 128:(k + 1) * 128])
        racc[3] = jnp.max(jnp.where(before, same, -1.0), axis=0, keepdims=True)

    for j in range(4):
        racc[j] = jnp.full((1, rows), -1.0, f32)
    answers = {
        (a, b): send(gave.at[a * SIDE + b], res.at[a * SIDE + b], rs.at[a * SIDE + b], rr.at[a * SIDE + b],
                     wide=flipped(w, a), narrow=flipped(n, b))
        for a, b in same_side
    }
    backs = [send(cacc.at[s], cres, ts.at[s], tr, wide=who) for s, who in enumerate((over, over_mate))]

    def give(slot):
        cacc[slot] = jnp.max(colacc[slot].T, axis=0, keepdims=True)
        backs[slot].start()

    def answer(j):
        for k in range(2)[::-1]:
            key = (j % 2, (j // 2) * 2 + k)
            gave[key[0] * SIDE + key[1]] = racc[j, :, k * half:(k + 1) * half]
            if key in answers:
                answers[key].start()

    cross_flag = turn(cand[2])
    cross_hub = jnp.where(inner, 1.0 - cross_flag, cross_flag)

    def passed(k, c):
        if k == 0 and c < AHEAD:
            p = part(c)
            x_ahead[0][c].wait_recv()
            x_ahead[1][c].wait_recv()
            uq[2, p] = choose(cross_hub, gotx[0, p], gotx[1, p])
        else:
            x_out[k][c].wait_recv()
        x_on[k][c].start()

    def part(c):
        return slice(c * (half // PIECES), (c + 1) * (half // PIECES))

    quarter = half // 2

    @pl.when(inner)
    def _():
        def settle(c):
            pq_out[0][c].wait_recv()
            pq_out[1][c].wait_recv()
            p = part(c)
            kbuf[RELAY, p] = choose(mate_swap, gotpq[0, p], gotpq[1, p])
            in_next[c].start()
            uq[1, p] = choose(mate_swap, gotpq[1, p], gotpq[0, p])
            x_out[1][c].start()

        for c in range(PIECES):
            settle(c)
            passed(0, c)
        beside[1].start()
        passed(1, 0)
        passed(1, 1)
        t_in_away.wait_recv()
        t_in_next.wait_recv()
        for s in range(2):
            for r in range(2):
                ktall[s + 2, r] = tall(kmeta[s, r:r + 1])
        beside[0].wait_recv()
        own_part((0,))
        over_flag = kmeta[NEXT, 2:3, 0:1]
        for c in range(AHEAD):
            z_ahead[0][c].wait_recv()
            z_ahead[1][c].wait_recv()
            kbuf[NEXT, part(c)] = choose(over_flag, gotz[0, part(c)], gotz[1, part(c)])
        for c in in_away[AHEAD:]:
            c.wait_recv()
        met([(NEXT, 0, half)], (0,))
        for c in x_on[0]:
            c.wait_recv()
        own_part((2,))
        met([(NEXT, 0, half)], (2,))
        passed(1, 2)
        beside[1].wait_recv()
        own_part((1,))
        met([(NEXT, 0, half)], (1,))
        passed(1, 3)
        for c in in_next[:PIECES // 2]:
            c.wait_recv()
        passed(1, 4)
        met([(LAST, 0, quarter)], (0, 1, 2))
        passed(1, 5)
        passed(1, 6)
        passed(1, 7)
        for c in in_next[PIECES // 2:]:
            c.wait_recv()
        met([(LAST, quarter, half)], (0, 1, 2))
        answer(1)
        for c in x_on[1]:
            c.wait_recv()
        final()
        give(LAST)
        answer(3)
        answer(2)
        answer(0)
        give(NEXT)

    @pl.when(outer)
    def _():
        def settle(c):
            to_mate[c].wait_recv()
            x_out[1][c].start()

        for c in range(PIECES):
            passed(0, c)
            settle(c)
        beside[1].start()
        beside[0].wait_recv()
        own_part((0,))
        for c in x_on[0]:
            c.wait_recv()
        own_part((2,))
        beside[1].wait_recv()
        own_part((1,))
        for c in range(PIECES):
            passed(1, c)
        for c in x_on[1]:
            c.wait_recv()
        own_part((3,))
        for j in (3, 2, 1, 0):
            answer(j)

    @pl.when(outer)
    def _():
        for c in pq_out[0] + pq_out[1]:
            c.wait_send()

    @pl.when(inner)
    def _():
        for c in [t_in_away, t_in_next] + in_away[AHEAD:] + in_next + to_mate + z_ahead[0] + z_ahead[1]:
            c.wait_send()

    @pl.when(w == 1)
    def _():
        for c in sums:
            c.wait_send()

    @pl.when(w >= SIDE // 2)
    def _():
        for k in far_side:
            votes[k].wait_send()

    for c in [votes[k] for k in same_side] + list(tells.values()) + x_ahead[0] + x_ahead[1] + x_out[0][AHEAD:] + x_out[1] + x_on[0] + x_on[1] + beside:
        c.wait_send()

    for c in answers.values():
        c.wait_recv()
    hub_best = jnp.maximum(jnp.maximum(gave[0], res[1]), jnp.maximum(res[2], res[3]))
    other_best = jnp.maximum(jnp.maximum(res[4], res[5]), jnp.maximum(res[6], res[7]))
    backs[0].wait_recv()
    cfull[:, :half] = jnp.maximum(jnp.where(inner, other_best, hub_best), cres[...])
    cfull[:, half:] = jnp.where(inner, hub_best, other_best)
    spread = jnp.broadcast_to(cfull[...], (128, rows)).T
    mine = jnp.where(deep.astype(f32) == target[...], jnp.concatenate([spread] * (rows // 128), axis=1), -1.0)
    out[...] = jnp.max(mine, axis=0, keepdims=True)


    @pl.when(inner)
    def _():
        for c in backs:
            c.wait_send()

    for c in answers.values():
        c.wait_send()


def per_device_meet(embeddings, cluster_id, order_index):
    rows, width = embeddings.shape
    half = rows // 2
    dma = pltpu.SemaphoreType.DMA
    vmem = pl.BlockSpec(memory_space=pltpu.VMEM)
    line = lambda k, m: pltpu.VMEM((k, 1, m), jnp.float32)
    block = lambda k, m: pltpu.VMEM((k, m, width), jnp.bfloat16)
    found = pl.pallas_call(
        meet_kernel,
        out_shape=jax.ShapeDtypeStruct((1, rows), jnp.float32),
        in_specs=[pl.BlockSpec(memory_space=pl.ANY), vmem, vmem],
        out_specs=vmem,
        scratch_shapes=[
            pltpu.VMEM((rows, width), jnp.bfloat16), dma, pltpu.VMEM((rows, width), jnp.bfloat16), block(4, rows),
            pltpu.VMEM((2 * SIDE, 2, rows), jnp.float32), line(SIDE * SIDE + 3, 128),
            block(2, half), pltpu.VMEM((half, width), jnp.bfloat16), block(2, half), block(2, AHEAD * half // PIECES), block(2, AHEAD * half // PIECES),
            block(3, half), pltpu.VMEM((4, 3, half), jnp.float32), pltpu.VMEM((4, 2, rows), jnp.float32),
            pltpu.VMEM((4, 2, half, 128), jnp.float32), pltpu.VMEM((2, half, 128), jnp.float32),
            pltpu.VMEM((1, rows), jnp.float32),
            line(4, rows), line(2 * SIDE, half), line(2 * SIDE, half), line(2, half), pltpu.VMEM((1, half), jnp.float32),
            pltpu.VMEM((1, rows), jnp.float32), pltpu.SemaphoreType.REGULAR((3,)),
            dma((SIDE * SIDE,)), dma((SIDE * SIDE,)), dma((2,)), dma, dma((2 * SIDE,)), dma((2 * SIDE,)),
            dma((2, PIECES)), dma((2, PIECES)), dma((2, AHEAD)), dma((2, AHEAD)), dma((2, AHEAD)), dma((2, AHEAD)),
            dma((2, PIECES)), dma((2, PIECES)), dma((2,)), dma((2,)),
            dma((PIECES,)), dma((PIECES,)), dma((2, PIECES)), dma((2, PIECES)), dma((2, PIECES)), dma((2, PIECES)),
            dma((2,)), dma((2,)), dma((2 * SIDE,)), dma((2 * SIDE,)), dma((2,)), dma,
        ],
        compiler_params=pltpu.CompilerParams(collective_id=0, has_side_effects=True, vmem_limit_bytes=56500000),
    )(embeddings, cluster_id.reshape(1, rows), order_index.reshape(1, rows))
    return jnp.maximum(found.reshape(rows), -1.0)


def solution(mesh):
    meet = mesh.shape["wide"] == SIDE and mesh.shape["narrow"] == SIDE
    return jax.shard_map(
        per_device_meet if meet else per_device,
        mesh=mesh,
        in_specs=(
            P(("parts", "wide", "narrow"), None),
            P(("parts", "wide", "narrow")),
            P(("parts", "wide", "narrow")),
        ),
        out_specs=P(("parts", "wide", "narrow")),
        check_vma=False,
    )
```

```python
import jax
import jax.numpy as jnp
from jax import lax
from jax.experimental import pallas as pl
from jax.experimental.pallas import tpu as pltpu
from jax.sharding import PartitionSpec as P

CPO = 16


def shifted(shard, axis, by):
    count = lax.axis_size(axis)
    return lax.ppermute(shard, axis, [(i, (i + by) % count) for i in range(count)])


def pair_inner(left, right):
    return lax.dot_general(
        left, right, (((1,), (1,)), ((), ())), preferred_element_type=jnp.float32
    )


def per_device(embeddings, cluster_id, order_index):
    wide_size = lax.axis_size("wide")
    rows = embeddings.shape[0]
    width = embeddings.shape[1]
    bucket = 2 * rows // wide_size
    values = embeddings.astype(jnp.float32)
    unit = (values * lax.rsqrt(jnp.sum(values * values, axis=1, keepdims=True) + 1e-06)).astype(
        jnp.bfloat16
    )
    owner = cluster_id // CPO
    here = jnp.arange(rows, dtype=jnp.int32)
    earlier = (owner[:, None] == owner[None, :]) & (here[None, :] < here[:, None])
    slot = jnp.sum(jnp.where(earlier, 1, 0), axis=1)
    target = owner * bucket + slot
    send_rows = jnp.zeros((wide_size * bucket, width), jnp.bfloat16).at[target].set(unit)
    meta_rows = jnp.stack([cluster_id, order_index], axis=1)
    send_meta = jnp.full((wide_size * bucket, 2), -1, jnp.int32).at[target].set(meta_rows)
    held, held_meta = (
        lax.all_to_all(send_rows, "wide", split_axis=0, concat_axis=0, tiled=True),
        lax.all_to_all(send_meta, "wide", split_axis=0, concat_axis=0, tiled=True),
    )
    held_cl = held_meta[:, 0]
    held_or = held_meta[:, 1]
    live = held_cl >= 0
    start_best = jnp.full((held.shape[0],), -1.0, jnp.float32)

    def row_best(inner, other_cl, other_or):
        allowed = (
            (other_cl[None, :] == held_cl[:, None])
            & (other_or[None, :] < held_or[:, None])
            & live[:, None]
        )
        return jnp.max(jnp.where(allowed, inner, -1.0), axis=1)

    narrow_size = lax.axis_size("narrow")
    best = jnp.maximum(start_best, row_best(pair_inner(held, held), held_cl, held_or))
    for distance in range(1, narrow_size // 2 + 1):
        other_rows, other_meta = shifted((held, held_meta), "narrow", distance)
        other_cl = other_meta[:, 0]
        other_or = other_meta[:, 1]
        inner = pair_inner(held, other_rows)
        best = jnp.maximum(best, row_best(inner, other_cl, other_or))
        column_ok = (
            (held_cl[:, None] == other_cl[None, :])
            & (held_or[:, None] < other_or[None, :])
            & (other_cl[None, :] >= 0)
        )
        column_best = jnp.max(jnp.where(column_ok, inner, -1.0), axis=0)
        returned = shifted(column_best, "narrow", -distance)
        best = jnp.maximum(best, returned)
    answers = lax.all_to_all(best, "wide", split_axis=0, concat_axis=0, tiled=True)
    return answers[target]


PIECES = 8
AHEAD = 1
SIDE = 4
MESH = pl.DeviceIdType.MESH
NEXT, LAST, RELAY = range(3)


def meet_kernel(emb_far, cl, od, out, emb, got, own, uq, marks, cand, pq, pk, gotpq, gotx, gotz, kbuf, kmeta, asked, ktall,
                colacc, target, racc, gave, res, cacc, cres, cfull, late,
                cas, car, ps, pr, mks, mkr, qs, qr, axs, axr, azs, azr, zs, zr, zms, zmr, ms, mr, xs, xr, fs, fr, ns, nr, rs, rr, ts, tr):
    w = lax.axis_index("wide")
    n = lax.axis_index("narrow")

    def flipped(v, k):
        return (v, v + 1 - 2 * lax.rem(v, 2), lax.rem(v + 2, SIDE), SIDE - 1 - v)[k]

    near, cross, far = (flipped(n, k) for k in (1, 2, 3))
    peers = (near, cross, far)
    mate, over_mate, over = (flipped(w, k) for k in (1, 2, 3))
    early = w < SIDE // 2
    outer = (w == 0) | (w == SIDE - 1)
    inner = (w > 0) & (w < SIDE - 1)
    rows = emb.shape[0]
    half = rows // 2
    f32 = jnp.float32

    def send(s, d, ss, rs_, **who):
        return pltpu.make_async_remote_copy(s, d, ss, rs_, device_id=who, device_id_type=MESH)

    take = pltpu.make_async_copy(emb_far, emb, got)
    take.start()
    same_side = [(0, b) for b in range(1, SIDE)] + [(1, b) for b in range(SIDE)]
    far_side = [(a, b) for a in (2, 3) for b in range(SIDE)]
    barrier = pltpu.get_barrier_semaphore()

    def greet(a, b):
        pl.semaphore_signal(barrier, inc=1, device_id={"wide": flipped(w, a), "narrow": flipped(n, b)}, device_id_type=MESH)

    for a, b in same_side:
        if a == 0:
            greet(a, b)

    @pl.when(w != SIDE - 1)
    def _():
        for b in range(SIDE):
            greet(1, b)

    @pl.when(early)
    def _():
        for a, b in far_side:
            greet(a, b)

    id_row = cl[...].astype(f32)
    od_row = od[...].astype(f32)
    spot = lax.broadcasted_iota(jnp.int32, (1, 128), 1).astype(f32)
    fits = jnp.zeros((1, 128), f32)
    for o in range(SIDE):
        mine = jnp.where((id_row >= o * CPO) & (id_row < (o + 1) * CPO), 1.0, 0.0)
        fits = jnp.where((spot == o) & (jnp.sum(mine, axis=1, keepdims=True) == half), 1.0, fits)
    cand[0] = fits

    def lowest(mask):
        return jnp.min(jnp.where(mask > 0.5, spot, jnp.float32(SIDE)), axis=1, keepdims=True)

    @pl.when(early)
    def _():
        pl.semaphore_wait(barrier, len(same_side))

    @pl.when(w == SIDE // 2)
    def _():
        pl.semaphore_wait(barrier, len(same_side) + len(far_side) - SIDE)
        pl.semaphore_signal(late.at[0], inc=1, device_id={"wide": 1}, device_id_type=MESH)

    @pl.when(w == SIDE - 1)
    def _():
        pl.semaphore_wait(barrier, len(same_side) + len(far_side))
        pl.semaphore_signal(late.at[1], inc=1, device_id={"wide": 1}, device_id_type=MESH)
        for b in range(SIDE):
            pl.semaphore_signal(late.at[2], inc=1, device_id={"wide": 2, "narrow": b}, device_id_type=MESH)

    z_part = [pl.ds(c * (half // PIECES), half // PIECES) for c in range(PIECES)]
    votes = {
        (a, b): send(cand.at[0], cand.at[a * SIDE + b], cas.at[a * SIDE + b], car.at[a * SIDE + b],
                     wide=flipped(w, a), narrow=flipped(n, b))
        for a, b in same_side + far_side
    }
    sums = [send(cand.at[SIDE * SIDE], cand.at[SIDE * SIDE + 1], ps.at[k], pr, wide=who) for k, who in enumerate((over, over_mate))]
    @pl.when(w >= SIDE // 2)
    def _():
        for k in far_side:
            votes[k].start()

    for k in same_side:
        if k[0] == 0:
            votes[k].start()

    @pl.when(w != SIDE // 2)
    def _():
        for b in range(SIDE):
            votes[1, b].start()

    take.wait()

    def normed(values):
        values = values.astype(f32)
        return (values * lax.rsqrt(jnp.sum(values * values, axis=1, keepdims=True) + 1e-06)).astype(jnp.bfloat16)

    own[...] = normed(emb[...])
    local = lowest(fits)
    first = jnp.where((id_row >= local * CPO) & (id_row < (local + 1.0) * CPO), 1.0, 0.0)
    deep = lax.broadcasted_iota(jnp.int32, (rows, rows), 0)
    long = lax.broadcasted_iota(jnp.int32, (rows, rows), 1)
    tri = jnp.where(deep < long, 1.0, 0.0).astype(jnp.bfloat16)
    rank = jnp.dot(jnp.broadcast_to(first, (16, rows)).astype(jnp.bfloat16), tri, preferred_element_type=f32)[0:1]
    lane = lax.broadcasted_iota(jnp.int32, (1, rows), 1).astype(f32)
    place = jnp.where(first > 0.5, rank, half + lane - rank)
    pick = jnp.where(deep.astype(f32) == place, 1.0, 0.0).astype(jnp.bfloat16)
    pq_out = [[send(pq.at[k, p], gotpq.at[k, p], qs.at[k, c], qr.at[k, c], wide=mate) for c, p in enumerate(z_part)] for k in range(2)]
    ahead = 2
    pq[0] = jnp.dot(pick[:half], own[...], preferred_element_type=f32).astype(jnp.bfloat16)

    @pl.when(outer)
    def _():
        for c in pq_out[0][:ahead]:
            c.start()

    od_high = jnp.floor(od_row * (1.0 / 128))
    od_low = od_row - od_high * 128
    digits = [jnp.broadcast_to(r, (16, rows)).astype(jnp.bfloat16) for r in (id_row, od_high, od_low)]
    marked = [pair_inner(t, pick)[0:1] for t in digits]
    marks[0] = jnp.concatenate([marked[0], marked[1] * 128 + marked[2]], axis=0)
    tells = {
        (a, b): send(marks.at[0], marks.at[a * SIDE + b], mks.at[a * SIDE + b], mkr.at[a * SIDE + b],
                     wide=flipped(w, a), narrow=flipped(n, b))
        for a, b in same_side
    }

    @pl.when(w == SIDE // 2)
    def _():
        pl.semaphore_wait(late.at[2], SIDE)
        for b in range(SIDE):
            votes[1, b].start()

    for c in tells.values():
        c.start()

    @pl.when(outer)
    def _():
        for c in pq_out[0][ahead:]:
            c.start()

    pq[1] = jnp.dot(pick[half:], own[...], preferred_element_type=f32).astype(jnp.bfloat16)

    @pl.when(outer)
    def _():
        for c in pq_out[1]:
            c.start()

    def both(dst, ss, sr, **who):
        return [[send(pq.at[k, p], dst.at[k, p], ss.at[k, c], sr.at[k, c], **who) for c, p in enumerate(z_part[:AHEAD])] for k in range(2)]

    x_ahead = both(gotx, axs, axr, narrow=cross)
    z_ahead = both(gotz, azs, azr, wide=over)
    for c in x_ahead[0] + x_ahead[1]:
        c.start()

    @pl.when(w == SIDE // 2)
    def _():
        for c in z_ahead[0] + z_ahead[1]:
            c.start()

    for k in same_side:
        votes[k].wait_recv()
    cand[SIDE * SIDE] = jnp.min(cand[0:2 * SIDE], axis=0)

    @pl.when(w == 1)
    def _():
        for k, c in enumerate(sums):
            pl.semaphore_wait(late.at[k], 1)
            c.start()
        for c in z_ahead[0] + z_ahead[1]:
            c.start()

    @pl.when(early)
    def _():
        for k in far_side:
            votes[k].wait_recv()
        cand[SIDE * SIDE + 2] = jnp.min(cand[2 * SIDE:4 * SIDE], axis=0)

    @pl.when(w >= SIDE // 2)
    def _():
        sums[0].wait_recv()
        cand[SIDE * SIDE + 2] = cand[SIDE * SIDE + 1]

    shared = jnp.minimum(cand[SIDE * SIDE], cand[SIDE * SIDE + 2])

    def turn(fit):
        agreed = jnp.where(lowest(shared) == lowest(fit), 1.0, 0.0)
        return jnp.where(early, 1.0 - agreed, agreed)

    swap = turn(fits)
    mate_swap = turn(cand[SIDE])

    def choose(flag, a, b):
        return jnp.where(flag > 0.5, b.astype(f32), a.astype(f32)).astype(jnp.bfloat16)

    def way(src, msrc, dst, ss):
        row = [send(src.at[p], kbuf.at[dst, p], zs.at[ss, c], zr.at[dst, c], wide=over) for c, p in enumerate(z_part)]
        return send(msrc, kmeta.at[dst], zms.at[ss], zmr.at[dst], wide=over), row

    t_in_away, in_away = way(pk, kmeta.at[2], NEXT, 0)
    t_in_next, in_next = way(kbuf.at[RELAY], kmeta.at[3], LAST, 1)
    to_mate = [send(pk.at[p], uq.at[1, p], ms.at[c], mr.at[c], wide=mate) for c, p in enumerate(z_part)]
    behind = [pl.ds(half + c * (half // PIECES), half // PIECES) for c in range(PIECES)]
    x_out = [[send(uq.at[k, p], uq.at[2 + k, p], xs.at[k, c], xr.at[k, c], narrow=cross) for c, p in enumerate(z_part)] for k in range(2)]
    x_on = [
        [send(uq.at[2 + k, p], uq.at[2 + k, behind[c]], fs.at[k, c], fr.at[k, c], narrow=near) for c, p in enumerate(z_part)]
        for k in range(2)
    ]
    beside = [send(uq.at[k, pl.ds(0, half)], uq.at[k, pl.ds(half, half)], ns.at[k], nr.at[k], narrow=near) for k in range(2)]

    def tag_half(slot, flag):
        return jnp.where(flag > 0.5, marks[slot, :, half:], marks[slot, :, :half])

    @pl.when(inner)
    def _():
        kmeta[2, 0:2] = tag_half(0, swap)
        kmeta[2, 2:3] = jnp.broadcast_to(swap, (1, half))
        t_in_away.start()

    hub = jnp.where(inner, 1.0 - swap, swap)
    for c, p in list(enumerate(z_part))[AHEAD:] + list(enumerate(z_part))[:AHEAD]:
        @pl.when(inner)
        def _():
            pk[p] = choose(swap, pq[0, p], pq[1, p])
            if c >= AHEAD:
                in_away[c].start()

        uq[0, p] = choose(hub, pq[0, p], pq[1, p])
        if c >= AHEAD:
            x_out[0][c].start()
    beside[0].start()

    @pl.when(inner)
    def _():
        for c in to_mate:
            c.start()
        tells[1, 0].wait_recv()
        kmeta[3, 0:2] = tag_half(SIDE, mate_swap)
        kmeta[3, 2:3] = jnp.broadcast_to(mate_swap, (1, half))
        t_in_next.start()

    @pl.when(outer)
    def _():
        tells[1, 0].wait_recv()

    target[...] = jnp.where(swap > 0.5, jnp.where(place < half, place + half, place - half), place)
    for k in same_side:
        if k != (1, 0):
            tells[k].wait_recv()
    for j in range(4):
        for k in range(2):
            slot = (j % 2) * SIDE + (j // 2) * 2 + k
            flag = turn(cand[slot])
            asked[j, :, k * half:(k + 1) * half] = tag_half(slot, jnp.where(inner, 1.0 - flag, flag))

    def tall(row):
        return jnp.broadcast_to(row, (128, row.shape[1])).T

    for k in range(2):
        for r in range(2):
            ktall[k, r] = tall(asked[k, r:r + 1, :half])

    def stack(parts):
        return parts[0] if len(parts) == 1 else jnp.concatenate(parts, axis=0)

    def tag_of(pieces, r):
        return stack([jnp.concatenate([ktall[s, r, lo:hi]] * (rows // 128), axis=1) for s, lo, hi in pieces])

    def own_part(js):
        pieces = [(0, 0, half), (1, 0, half)]
        keys = stack([uq[0, :half], uq[1, :half]])
        k_cl, k_od = tag_of(pieces, 0), tag_of(pieces, 1)
        for j in js:
            ok = (k_cl == asked[j, 0:1]) & (k_od < asked[j, 1:2])
            racc[j] = jnp.maximum(racc[j], jnp.max(jnp.where(ok, pair_inner(keys, uq[j]), -1.0), axis=0, keepdims=True))

    started = set()

    def met(pieces, js):
        keys = stack([kbuf[s, lo:hi] for s, lo, hi in pieces])
        slots = [(s + 2, lo, hi) for s, lo, hi in pieces]
        k_cl, k_od = tag_of(slots, 0), tag_of(slots, 1)
        col = jnp.full((keys.shape[0], 128), -1.0, f32)
        for j in js:
            same = jnp.where(k_cl == asked[j, 0:1], pair_inner(keys, uq[j]), -1.0)
            before = k_od < asked[j, 1:2]
            racc[j] = jnp.maximum(racc[j], jnp.max(jnp.where(before, same, -1.0), axis=0, keepdims=True))
            after = jnp.where(before, -1.0, same)
            for k in range(rows // 128):
                col = jnp.maximum(col, after[:, k * 128:(k + 1) * 128])
        at = 0
        for s, lo, hi in pieces:
            part = col[at:at + hi - lo]
            at += hi - lo
            if (s, lo) in started:
                part = jnp.maximum(part, colacc[s, lo:hi])
            started.add((s, lo))
            colacc[s, lo:hi] = part

    def final():
        pieces = [(s, 0, half) for s in (2 + LAST, 2 + NEXT, 0, 1)]
        keys = stack([kbuf[LAST], kbuf[NEXT], uq[0, :half], uq[1, :half]])
        k_cl, k_od = tag_of(pieces, 0), tag_of(pieces, 1)
        same = jnp.where(k_cl == asked[3, 0:1], pair_inner(keys, uq[3]), -1.0)
        before = k_od < asked[3, 1:2]
        after = jnp.where(before[:rows], -1.0, same[:rows])
        for k in range(rows // 128):
            for s, lo in ((LAST, 0), (NEXT, half)):
                colacc[s] = jnp.maximum(colacc[s], after[lo:lo + half, k * 128:(k + 1) * 128])
        racc[3] = jnp.max(jnp.where(before, same, -1.0), axis=0, keepdims=True)

    for j in range(4):
        racc[j] = jnp.full((1, rows), -1.0, f32)
    answers = {
        (a, b): send(gave.at[a * SIDE + b], res.at[a * SIDE + b], rs.at[a * SIDE + b], rr.at[a * SIDE + b],
                     wide=flipped(w, a), narrow=flipped(n, b))
        for a, b in same_side
    }
    backs = [send(cacc.at[s], cres, ts.at[s], tr, wide=who) for s, who in enumerate((over, over_mate))]

    def give(slot):
        cacc[slot] = jnp.max(colacc[slot].T, axis=0, keepdims=True)
        backs[slot].start()

    def answer(j):
        for k in range(2)[::-1]:
            key = (j % 2, (j // 2) * 2 + k)
            gave[key[0] * SIDE + key[1]] = racc[j, :, k * half:(k + 1) * half]
            if key in answers:
                answers[key].start()

    cross_flag = turn(cand[2])
    cross_hub = jnp.where(inner, 1.0 - cross_flag, cross_flag)

    def passed(k, c):
        if k == 0 and c < AHEAD:
            p = part(c)
            x_ahead[0][c].wait_recv()
            x_ahead[1][c].wait_recv()
            uq[2, p] = choose(cross_hub, gotx[0, p], gotx[1, p])
        else:
            x_out[k][c].wait_recv()
        x_on[k][c].start()

    def part(c):
        return slice(c * (half // PIECES), (c + 1) * (half // PIECES))

    quarter = half // 2

    @pl.when(inner)
    def _():
        def settle(c):
            pq_out[0][c].wait_recv()
            pq_out[1][c].wait_recv()
            p = part(c)
            kbuf[RELAY, p] = choose(mate_swap, gotpq[0, p], gotpq[1, p])
            in_next[c].start()
            uq[1, p] = choose(mate_swap, gotpq[1, p], gotpq[0, p])
            x_out[1][c].start()

        for c in range(PIECES):
            settle(c)
            passed(0, c)
        beside[1].start()
        passed(1, 0)
        passed(1, 1)
        t_in_away.wait_recv()
        t_in_next.wait_recv()
        for s in range(2):
            for r in range(2):
                ktall[s + 2, r] = tall(kmeta[s, r:r + 1])
        beside[0].wait_recv()
        own_part((0,))
        over_flag = kmeta[NEXT, 2:3, 0:1]
        for c in range(AHEAD):
            z_ahead[0][c].wait_recv()
            z_ahead[1][c].wait_recv()
            kbuf[NEXT, part(c)] = choose(over_flag, gotz[0, part(c)], gotz[1, part(c)])
        for c in in_away[AHEAD:]:
            c.wait_recv()
        met([(NEXT, 0, half)], (0,))
        for c in x_on[0]:
            c.wait_recv()
        own_part((2,))
        met([(NEXT, 0, half)], (2,))
        passed(1, 2)
        beside[1].wait_recv()
        own_part((1,))
        met([(NEXT, 0, half)], (1,))
        passed(1, 3)
        passed(1, 4)
        passed(1, 5)
        passed(1, 6)
        passed(1, 7)
        for c in in_next:
            c.wait_recv()
        met([(LAST, 0, half)], (1, 0, 2))
        answer(1)
        for c in x_on[1]:
            c.wait_recv()
        final()
        give(LAST)
        answer(3)
        answer(2)
        answer(0)
        give(NEXT)

    @pl.when(outer)
    def _():
        def settle(c):
            to_mate[c].wait_recv()
            x_out[1][c].start()

        for c in range(PIECES):
            passed(0, c)
            settle(c)
        beside[1].start()
        beside[0].wait_recv()
        own_part((0,))
        for c in x_on[0]:
            c.wait_recv()
        own_part((2,))
        beside[1].wait_recv()
        own_part((1,))
        for c in range(PIECES):
            passed(1, c)
        for c in x_on[1]:
            c.wait_recv()
        own_part((3,))
        for j in (3, 2, 1, 0):
            answer(j)

    @pl.when(outer)
    def _():
        for c in pq_out[0] + pq_out[1]:
            c.wait_send()

    @pl.when(inner)
    def _():
        for c in [t_in_away, t_in_next] + in_away[AHEAD:] + in_next + to_mate + z_ahead[0] + z_ahead[1]:
            c.wait_send()

    @pl.when(w == 1)
    def _():
        for c in sums:
            c.wait_send()

    @pl.when(w >= SIDE // 2)
    def _():
        for k in far_side:
            votes[k].wait_send()

    for c in [votes[k] for k in same_side] + list(tells.values()) + x_ahead[0] + x_ahead[1] + x_out[0][AHEAD:] + x_out[1] + x_on[0] + x_on[1] + beside:
        c.wait_send()

    for c in answers.values():
        c.wait_recv()
    hub_best = jnp.maximum(jnp.maximum(gave[0], res[1]), jnp.maximum(res[2], res[3]))
    other_best = jnp.maximum(jnp.maximum(res[4], res[5]), jnp.maximum(res[6], res[7]))
    backs[0].wait_recv()
    cfull[:, :half] = jnp.maximum(jnp.where(inner, other_best, hub_best), cres[...])
    cfull[:, half:] = jnp.where(inner, hub_best, other_best)
    spread = jnp.broadcast_to(cfull[...], (128, rows)).T
    mine = jnp.where(deep.astype(f32) == target[...], jnp.concatenate([spread] * (rows // 128), axis=1), -1.0)
    out[...] = jnp.max(mine, axis=0, keepdims=True)


    @pl.when(inner)
    def _():
        for c in backs:
            c.wait_send()

    for c in answers.values():
        c.wait_send()


def per_device_meet(embeddings, cluster_id, order_index):
    rows, width = embeddings.shape
    half = rows // 2
    dma = pltpu.SemaphoreType.DMA
    vmem = pl.BlockSpec(memory_space=pltpu.VMEM)
    line = lambda k, m: pltpu.VMEM((k, 1, m), jnp.float32)
    block = lambda k, m: pltpu.VMEM((k, m, width), jnp.bfloat16)
    found = pl.pallas_call(
        meet_kernel,
        out_shape=jax.ShapeDtypeStruct((1, rows), jnp.float32),
        in_specs=[pl.BlockSpec(memory_space=pl.ANY), vmem, vmem],
        out_specs=vmem,
        scratch_shapes=[
            pltpu.VMEM((rows, width), jnp.bfloat16), dma, pltpu.VMEM((rows, width), jnp.bfloat16), block(4, rows),
            pltpu.VMEM((2 * SIDE, 2, rows), jnp.float32), line(SIDE * SIDE + 3, 128),
            block(2, half), pltpu.VMEM((half, width), jnp.bfloat16), block(2, half), block(2, AHEAD * half // PIECES), block(2, AHEAD * half // PIECES),
            block(3, half), pltpu.VMEM((4, 3, half), jnp.float32), pltpu.VMEM((4, 2, rows), jnp.float32),
            pltpu.VMEM((4, 2, half, 128), jnp.float32), pltpu.VMEM((2, half, 128), jnp.float32),
            pltpu.VMEM((1, rows), jnp.float32),
            line(4, rows), line(2 * SIDE, half), line(2 * SIDE, half), line(2, half), pltpu.VMEM((1, half), jnp.float32),
            pltpu.VMEM((1, rows), jnp.float32), pltpu.SemaphoreType.REGULAR((3,)),
            dma((SIDE * SIDE,)), dma((SIDE * SIDE,)), dma((2,)), dma, dma((2 * SIDE,)), dma((2 * SIDE,)),
            dma((2, PIECES)), dma((2, PIECES)), dma((2, AHEAD)), dma((2, AHEAD)), dma((2, AHEAD)), dma((2, AHEAD)),
            dma((2, PIECES)), dma((2, PIECES)), dma((2,)), dma((2,)),
            dma((PIECES,)), dma((PIECES,)), dma((2, PIECES)), dma((2, PIECES)), dma((2, PIECES)), dma((2, PIECES)),
            dma((2,)), dma((2,)), dma((2 * SIDE,)), dma((2 * SIDE,)), dma((2,)), dma,
        ],
        compiler_params=pltpu.CompilerParams(collective_id=0, has_side_effects=True, vmem_limit_bytes=56500000),
    )(embeddings, cluster_id.reshape(1, rows), order_index.reshape(1, rows))
    return jnp.maximum(found.reshape(rows), -1.0)


def solution(mesh):
    meet = mesh.shape["wide"] == SIDE and mesh.shape["narrow"] == SIDE
    return jax.shard_map(
        per_device_meet if meet else per_device,
        mesh=mesh,
        in_specs=(
            P(("parts", "wide", "narrow"), None),
            P(("parts", "wide", "narrow")),
            P(("parts", "wide", "narrow")),
        ),
        out_specs=P(("parts", "wide", "narrow")),
        check_vma=False,
    )
```

```python
import jax
import jax.numpy as jnp
from jax import lax
from jax.experimental import pallas as pl
from jax.experimental.pallas import tpu as pltpu
from jax.sharding import PartitionSpec as P

CPO = 16


def shifted(shard, axis, by):
    count = lax.axis_size(axis)
    return lax.ppermute(shard, axis, [(i, (i + by) % count) for i in range(count)])


def pair_inner(left, right):
    return lax.dot_general(
        left, right, (((1,), (1,)), ((), ())), preferred_element_type=jnp.float32
    )


def per_device(embeddings, cluster_id, order_index):
    wide_size = lax.axis_size("wide")
    rows = embeddings.shape[0]
    width = embeddings.shape[1]
    bucket = 2 * rows // wide_size
    values = embeddings.astype(jnp.float32)
    unit = (values * lax.rsqrt(jnp.sum(values * values, axis=1, keepdims=True) + 1e-06)).astype(
        jnp.bfloat16
    )
    owner = cluster_id // CPO
    here = jnp.arange(rows, dtype=jnp.int32)
    earlier = (owner[:, None] == owner[None, :]) & (here[None, :] < here[:, None])
    slot = jnp.sum(jnp.where(earlier, 1, 0), axis=1)
    target = owner * bucket + slot
    send_rows = jnp.zeros((wide_size * bucket, width), jnp.bfloat16).at[target].set(unit)
    meta_rows = jnp.stack([cluster_id, order_index], axis=1)
    send_meta = jnp.full((wide_size * bucket, 2), -1, jnp.int32).at[target].set(meta_rows)
    held, held_meta = (
        lax.all_to_all(send_rows, "wide", split_axis=0, concat_axis=0, tiled=True),
        lax.all_to_all(send_meta, "wide", split_axis=0, concat_axis=0, tiled=True),
    )
    held_cl = held_meta[:, 0]
    held_or = held_meta[:, 1]
    live = held_cl >= 0
    start_best = jnp.full((held.shape[0],), -1.0, jnp.float32)

    def row_best(inner, other_cl, other_or):
        allowed = (
            (other_cl[None, :] == held_cl[:, None])
            & (other_or[None, :] < held_or[:, None])
            & live[:, None]
        )
        return jnp.max(jnp.where(allowed, inner, -1.0), axis=1)

    narrow_size = lax.axis_size("narrow")
    best = jnp.maximum(start_best, row_best(pair_inner(held, held), held_cl, held_or))
    for distance in range(1, narrow_size // 2 + 1):
        other_rows, other_meta = shifted((held, held_meta), "narrow", distance)
        other_cl = other_meta[:, 0]
        other_or = other_meta[:, 1]
        inner = pair_inner(held, other_rows)
        best = jnp.maximum(best, row_best(inner, other_cl, other_or))
        column_ok = (
            (held_cl[:, None] == other_cl[None, :])
            & (held_or[:, None] < other_or[None, :])
            & (other_cl[None, :] >= 0)
        )
        column_best = jnp.max(jnp.where(column_ok, inner, -1.0), axis=0)
        returned = shifted(column_best, "narrow", -distance)
        best = jnp.maximum(best, returned)
    answers = lax.all_to_all(best, "wide", split_axis=0, concat_axis=0, tiled=True)
    return answers[target]


PIECES = 8
AHEAD = 1
SIDE = 4
MESH = pl.DeviceIdType.MESH
NEXT, LAST, RELAY = range(3)


def meet_kernel(emb_far, cl, od, out, emb, got, own, uq, marks, cand, pq, pk, gotpq, gotx, gotz, kbuf, kmeta, asked, ktall,
                colacc, target, racc, gave, res, cacc, cres, cfull, late,
                cas, car, ps, pr, mks, mkr, qs, qr, axs, axr, azs, azr, zs, zr, zms, zmr, ms, mr, xs, xr, fs, fr, ns, nr, rs, rr, ts, tr):
    w = lax.axis_index("wide")
    n = lax.axis_index("narrow")

    def flipped(v, k):
        return (v, v + 1 - 2 * lax.rem(v, 2), lax.rem(v + 2, SIDE), SIDE - 1 - v)[k]

    near, cross, far = (flipped(n, k) for k in (1, 2, 3))
    peers = (near, cross, far)
    mate, over_mate, over = (flipped(w, k) for k in (1, 2, 3))
    early = w < SIDE // 2
    outer = (w == 0) | (w == SIDE - 1)
    inner = (w > 0) & (w < SIDE - 1)
    rows = emb.shape[0]
    half = rows // 2
    f32 = jnp.float32

    def send(s, d, ss, rs_, **who):
        return pltpu.make_async_remote_copy(s, d, ss, rs_, device_id=who, device_id_type=MESH)

    take = pltpu.make_async_copy(emb_far, emb, got)
    take.start()
    same_side = [(0, b) for b in range(1, SIDE)] + [(1, b) for b in range(SIDE)]
    far_side = [(a, b) for a in (2, 3) for b in range(SIDE)]
    barrier = pltpu.get_barrier_semaphore()

    def greet(a, b):
        pl.semaphore_signal(barrier, inc=1, device_id={"wide": flipped(w, a), "narrow": flipped(n, b)}, device_id_type=MESH)

    for a, b in same_side:
        if a == 0:
            greet(a, b)

    @pl.when(w != SIDE - 1)
    def _():
        for b in range(SIDE):
            greet(1, b)

    @pl.when(early)
    def _():
        for a, b in far_side:
            greet(a, b)

    id_row = cl[...].astype(f32)
    od_row = od[...].astype(f32)
    spot = lax.broadcasted_iota(jnp.int32, (1, 128), 1).astype(f32)
    fits = jnp.zeros((1, 128), f32)
    for o in range(SIDE):
        mine = jnp.where((id_row >= o * CPO) & (id_row < (o + 1) * CPO), 1.0, 0.0)
        fits = jnp.where((spot == o) & (jnp.sum(mine, axis=1, keepdims=True) == half), 1.0, fits)
    cand[0] = fits

    def lowest(mask):
        return jnp.min(jnp.where(mask > 0.5, spot, jnp.float32(SIDE)), axis=1, keepdims=True)

    @pl.when(early)
    def _():
        pl.semaphore_wait(barrier, len(same_side))

    @pl.when(w == SIDE // 2)
    def _():
        pl.semaphore_wait(barrier, len(same_side) + len(far_side) - SIDE)
        pl.semaphore_signal(late.at[0], inc=1, device_id={"wide": 1}, device_id_type=MESH)

    @pl.when(w == SIDE - 1)
    def _():
        pl.semaphore_wait(barrier, len(same_side) + len(far_side))
        pl.semaphore_signal(late.at[1], inc=1, device_id={"wide": 1}, device_id_type=MESH)
        for b in range(SIDE):
            pl.semaphore_signal(late.at[2], inc=1, device_id={"wide": 2, "narrow": b}, device_id_type=MESH)

    z_part = [pl.ds(c * (half // PIECES), half // PIECES) for c in range(PIECES)]
    votes = {
        (a, b): send(cand.at[0], cand.at[a * SIDE + b], cas.at[a * SIDE + b], car.at[a * SIDE + b],
                     wide=flipped(w, a), narrow=flipped(n, b))
        for a, b in same_side + far_side
    }
    sums = [send(cand.at[SIDE * SIDE], cand.at[SIDE * SIDE + 1], ps.at[k], pr, wide=who) for k, who in enumerate((over, over_mate))]
    @pl.when(w >= SIDE // 2)
    def _():
        for k in far_side:
            votes[k].start()

    for k in same_side:
        if k[0] == 0:
            votes[k].start()

    @pl.when(w != SIDE // 2)
    def _():
        for b in range(SIDE):
            votes[1, b].start()

    take.wait()

    def normed(values):
        values = values.astype(f32)
        return (values * lax.rsqrt(jnp.sum(values * values, axis=1, keepdims=True) + 1e-06)).astype(jnp.bfloat16)

    own[...] = normed(emb[...])
    local = lowest(fits)
    first = jnp.where((id_row >= local * CPO) & (id_row < (local + 1.0) * CPO), 1.0, 0.0)
    deep = lax.broadcasted_iota(jnp.int32, (rows, rows), 0)
    long = lax.broadcasted_iota(jnp.int32, (rows, rows), 1)
    tri = jnp.where(deep < long, 1.0, 0.0).astype(jnp.bfloat16)
    rank = jnp.dot(jnp.broadcast_to(first, (16, rows)).astype(jnp.bfloat16), tri, preferred_element_type=f32)[0:1]
    lane = lax.broadcasted_iota(jnp.int32, (1, rows), 1).astype(f32)
    place = jnp.where(first > 0.5, rank, half + lane - rank)
    pick = jnp.where(deep.astype(f32) == place, 1.0, 0.0).astype(jnp.bfloat16)
    pq_out = [[send(pq.at[k, p], gotpq.at[k, p], qs.at[k, c], qr.at[k, c], wide=mate) for c, p in enumerate(z_part)] for k in range(2)]
    ahead = 2
    pq[0] = jnp.dot(pick[:half], own[...], preferred_element_type=f32).astype(jnp.bfloat16)

    @pl.when(outer)
    def _():
        for c in pq_out[0][:ahead]:
            c.start()

    od_high = jnp.floor(od_row * (1.0 / 128))
    od_low = od_row - od_high * 128
    digits = [jnp.broadcast_to(r, (16, rows)).astype(jnp.bfloat16) for r in (id_row, od_high, od_low)]
    marked = [pair_inner(t, pick)[0:1] for t in digits]
    marks[0] = jnp.concatenate([marked[0], marked[1] * 128 + marked[2]], axis=0)
    tells = {
        (a, b): send(marks.at[0], marks.at[a * SIDE + b], mks.at[a * SIDE + b], mkr.at[a * SIDE + b],
                     wide=flipped(w, a), narrow=flipped(n, b))
        for a, b in same_side
    }

    @pl.when(w == SIDE // 2)
    def _():
        pl.semaphore_wait(late.at[2], SIDE)
        for b in range(SIDE):
            votes[1, b].start()

    for c in tells.values():
        c.start()

    @pl.when(outer)
    def _():
        for c in pq_out[0][ahead:]:
            c.start()

    pq[1] = jnp.dot(pick[half:], own[...], preferred_element_type=f32).astype(jnp.bfloat16)

    @pl.when(outer)
    def _():
        for c in pq_out[1]:
            c.start()

    def both(dst, ss, sr, **who):
        return [[send(pq.at[k, p], dst.at[k, p], ss.at[k, c], sr.at[k, c], **who) for c, p in enumerate(z_part[:AHEAD])] for k in range(2)]

    x_ahead = both(gotx, axs, axr, narrow=cross)
    z_ahead = both(gotz, azs, azr, wide=over)
    for c in x_ahead[0] + x_ahead[1]:
        c.start()

    @pl.when(w == SIDE // 2)
    def _():
        for c in z_ahead[0] + z_ahead[1]:
            c.start()

    for k in same_side:
        votes[k].wait_recv()
    cand[SIDE * SIDE] = jnp.min(cand[0:2 * SIDE], axis=0)

    @pl.when(w == 1)
    def _():
        for k, c in enumerate(sums):
            pl.semaphore_wait(late.at[k], 1)
            c.start()
        for c in z_ahead[0] + z_ahead[1]:
            c.start()

    @pl.when(early)
    def _():
        for k in far_side:
            votes[k].wait_recv()
        cand[SIDE * SIDE + 2] = jnp.min(cand[2 * SIDE:4 * SIDE], axis=0)

    @pl.when(w >= SIDE // 2)
    def _():
        sums[0].wait_recv()
        cand[SIDE * SIDE + 2] = cand[SIDE * SIDE + 1]

    shared = jnp.minimum(cand[SIDE * SIDE], cand[SIDE * SIDE + 2])

    def turn(fit):
        agreed = jnp.where(lowest(shared) == lowest(fit), 1.0, 0.0)
        return jnp.where(early, 1.0 - agreed, agreed)

    swap = turn(fits)
    mate_swap = turn(cand[SIDE])

    def choose(flag, a, b):
        return jnp.where(flag > 0.5, b.astype(f32), a.astype(f32)).astype(jnp.bfloat16)

    def way(src, msrc, dst, ss):
        row = [send(src.at[p], kbuf.at[dst, p], zs.at[ss, c], zr.at[dst, c], wide=over) for c, p in enumerate(z_part)]
        return send(msrc, kmeta.at[dst], zms.at[ss], zmr.at[dst], wide=over), row

    t_in_away, in_away = way(pk, kmeta.at[2], NEXT, 0)
    t_in_next, in_next = way(kbuf.at[RELAY], kmeta.at[3], LAST, 1)
    to_mate = [send(pk.at[p], uq.at[1, p], ms.at[c], mr.at[c], wide=mate) for c, p in enumerate(z_part)]
    behind = [pl.ds(half + c * (half // PIECES), half // PIECES) for c in range(PIECES)]
    x_out = [[send(uq.at[k, p], uq.at[2 + k, p], xs.at[k, c], xr.at[k, c], narrow=cross) for c, p in enumerate(z_part)] for k in range(2)]
    x_on = [
        [send(uq.at[2 + k, p], uq.at[2 + k, behind[c]], fs.at[k, c], fr.at[k, c], narrow=near) for c, p in enumerate(z_part)]
        for k in range(2)
    ]
    beside = [send(uq.at[k, pl.ds(0, half)], uq.at[k, pl.ds(half, half)], ns.at[k], nr.at[k], narrow=near) for k in range(2)]

    def tag_half(slot, flag):
        return jnp.where(flag > 0.5, marks[slot, :, half:], marks[slot, :, :half])

    @pl.when(inner)
    def _():
        kmeta[2, 0:2] = tag_half(0, swap)
        kmeta[2, 2:3] = jnp.broadcast_to(swap, (1, half))
        t_in_away.start()

    hub = jnp.where(inner, 1.0 - swap, swap)
    for c, p in list(enumerate(z_part))[AHEAD:] + list(enumerate(z_part))[:AHEAD]:
        @pl.when(inner)
        def _():
            pk[p] = choose(swap, pq[0, p], pq[1, p])
            if c >= AHEAD:
                in_away[c].start()

        uq[0, p] = choose(hub, pq[0, p], pq[1, p])
        if c >= AHEAD:
            x_out[0][c].start()
    beside[0].start()

    @pl.when(inner)
    def _():
        for c in to_mate:
            c.start()
        tells[1, 0].wait_recv()
        kmeta[3, 0:2] = tag_half(SIDE, mate_swap)
        kmeta[3, 2:3] = jnp.broadcast_to(mate_swap, (1, half))
        t_in_next.start()

    @pl.when(outer)
    def _():
        tells[1, 0].wait_recv()

    target[...] = jnp.where(swap > 0.5, jnp.where(place < half, place + half, place - half), place)
    for k in same_side:
        if k != (1, 0):
            tells[k].wait_recv()
    for j in range(4):
        for k in range(2):
            slot = (j % 2) * SIDE + (j // 2) * 2 + k
            flag = turn(cand[slot])
            asked[j, :, k * half:(k + 1) * half] = tag_half(slot, jnp.where(inner, 1.0 - flag, flag))

    def tall(row):
        return jnp.broadcast_to(row, (128, row.shape[1])).T

    for k in range(2):
        for r in range(2):
            ktall[k, r] = tall(asked[k, r:r + 1, :half])

    def stack(parts):
        return parts[0] if len(parts) == 1 else jnp.concatenate(parts, axis=0)

    def tag_of(pieces, r):
        return stack([jnp.concatenate([ktall[s, r, lo:hi]] * (rows // 128), axis=1) for s, lo, hi in pieces])

    def own_part(js):
        pieces = [(0, 0, half), (1, 0, half)]
        keys = stack([uq[0, :half], uq[1, :half]])
        k_cl, k_od = tag_of(pieces, 0), tag_of(pieces, 1)
        for j in js:
            ok = (k_cl == asked[j, 0:1]) & (k_od < asked[j, 1:2])
            racc[j] = jnp.maximum(racc[j], jnp.max(jnp.where(ok, pair_inner(keys, uq[j]), -1.0), axis=0, keepdims=True))

    started = set()

    def met(pieces, js):
        keys = stack([kbuf[s, lo:hi] for s, lo, hi in pieces])
        slots = [(s + 2, lo, hi) for s, lo, hi in pieces]
        k_cl, k_od = tag_of(slots, 0), tag_of(slots, 1)
        col = jnp.full((keys.shape[0], 128), -1.0, f32)
        for j in js:
            same = jnp.where(k_cl == asked[j, 0:1], pair_inner(keys, uq[j]), -1.0)
            before = k_od < asked[j, 1:2]
            racc[j] = jnp.maximum(racc[j], jnp.max(jnp.where(before, same, -1.0), axis=0, keepdims=True))
            after = jnp.where(before, -1.0, same)
            for k in range(rows // 128):
                col = jnp.maximum(col, after[:, k * 128:(k + 1) * 128])
        at = 0
        for s, lo, hi in pieces:
            part = col[at:at + hi - lo]
            at += hi - lo
            if (s, lo) in started:
                part = jnp.maximum(part, colacc[s, lo:hi])
            started.add((s, lo))
            colacc[s, lo:hi] = part

    def final():
        pieces = [(s, 0, half) for s in (2 + LAST, 2 + NEXT, 0, 1)]
        keys = stack([kbuf[LAST], kbuf[NEXT], uq[0, :half], uq[1, :half]])
        k_cl, k_od = tag_of(pieces, 0), tag_of(pieces, 1)
        same = jnp.where(k_cl == asked[3, 0:1], pair_inner(keys, uq[3]), -1.0)
        before = k_od < asked[3, 1:2]
        after = jnp.where(before[:rows], -1.0, same[:rows])
        for k in range(rows // 128):
            for s, lo in ((LAST, 0), (NEXT, half)):
                colacc[s] = jnp.maximum(colacc[s], after[lo:lo + half, k * 128:(k + 1) * 128])
        racc[3] = jnp.max(jnp.where(before, same, -1.0), axis=0, keepdims=True)

    for j in range(4):
        racc[j] = jnp.full((1, rows), -1.0, f32)
    answers = {
        (a, b): send(gave.at[a * SIDE + b], res.at[a * SIDE + b], rs.at[a * SIDE + b], rr.at[a * SIDE + b],
                     wide=flipped(w, a), narrow=flipped(n, b))
        for a, b in same_side
    }
    backs = [send(cacc.at[s], cres, ts.at[s], tr, wide=who) for s, who in enumerate((over, over_mate))]

    def give(slot):
        cacc[slot] = jnp.max(colacc[slot].T, axis=0, keepdims=True)
        backs[slot].start()

    def answer(j):
        for k in range(2)[::-1]:
            key = (j % 2, (j // 2) * 2 + k)
            gave[key[0] * SIDE + key[1]] = racc[j, :, k * half:(k + 1) * half]
            if key in answers:
                answers[key].start()

    cross_flag = turn(cand[2])
    cross_hub = jnp.where(inner, 1.0 - cross_flag, cross_flag)

    def passed(k, c):
        if k == 0 and c < AHEAD:
            p = part(c)
            x_ahead[0][c].wait_recv()
            x_ahead[1][c].wait_recv()
            uq[2, p] = choose(cross_hub, gotx[0, p], gotx[1, p])
        else:
            x_out[k][c].wait_recv()
        x_on[k][c].start()

    def part(c):
        return slice(c * (half // PIECES), (c + 1) * (half // PIECES))

    quarter = half // 2

    @pl.when(inner)
    def _():
        def settle(c):
            pq_out[0][c].wait_recv()
            pq_out[1][c].wait_recv()
            p = part(c)
            kbuf[RELAY, p] = choose(mate_swap, gotpq[0, p], gotpq[1, p])
            in_next[c].start()
            uq[1, p] = choose(mate_swap, gotpq[1, p], gotpq[0, p])
            x_out[1][c].start()

        for c in range(PIECES):
            settle(c)
            passed(0, c)
        beside[1].start()
        passed(1, 0)
        passed(1, 1)
        t_in_away.wait_recv()
        t_in_next.wait_recv()
        for s in range(2):
            for r in range(2):
                ktall[s + 2, r] = tall(kmeta[s, r:r + 1])
        beside[0].wait_recv()
        own_part((0,))
        over_flag = kmeta[NEXT, 2:3, 0:1]
        for c in range(AHEAD):
            z_ahead[0][c].wait_recv()
            z_ahead[1][c].wait_recv()
            kbuf[NEXT, part(c)] = choose(over_flag, gotz[0, part(c)], gotz[1, part(c)])
        for c in in_away[AHEAD:]:
            c.wait_recv()
        met([(NEXT, 0, half)], (0,))
        for c in x_on[0]:
            c.wait_recv()
        own_part((2,))
        met([(NEXT, 0, half)], (2,))
        passed(1, 2)
        beside[1].wait_recv()
        own_part((1,))
        met([(NEXT, 0, half)], (1,))
        passed(1, 3)
        for c in in_next[:PIECES // 2]:
            c.wait_recv()
        passed(1, 4)
        met([(LAST, 0, quarter)], (0, 1, 2))
        passed(1, 5)
        passed(1, 6)
        passed(1, 7)
        for c in in_next[PIECES // 2:]:
            c.wait_recv()
        met([(LAST, quarter, half)], (0, 1, 2))
        answer(1)
        for c in x_on[1]:
            c.wait_recv()
        final()

        @pl.when(early)
        def _():
            answer(3)
            give(LAST)

        @pl.when(w >= SIDE // 2)
        def _():
            give(LAST)
            answer(3)

        answer(2)
        answer(0)
        give(NEXT)

    @pl.when(outer)
    def _():
        def settle(c):
            to_mate[c].wait_recv()
            x_out[1][c].start()

        for c in range(PIECES):
            passed(0, c)
            settle(c)
        beside[1].start()
        beside[0].wait_recv()
        own_part((0,))
        for c in x_on[0]:
            c.wait_recv()
        own_part((2,))
        beside[1].wait_recv()
        own_part((1,))
        for c in range(PIECES):
            passed(1, c)
        for c in x_on[1]:
            c.wait_recv()
        own_part((3,))
        for j in (3, 2, 1, 0):
            answer(j)

    @pl.when(outer)
    def _():
        for c in pq_out[0] + pq_out[1]:
            c.wait_send()

    @pl.when(inner)
    def _():
        for c in [t_in_away, t_in_next] + in_away[AHEAD:] + in_next + to_mate + z_ahead[0] + z_ahead[1]:
            c.wait_send()

    @pl.when(w == 1)
    def _():
        for c in sums:
            c.wait_send()

    @pl.when(w >= SIDE // 2)
    def _():
        for k in far_side:
            votes[k].wait_send()

    for c in [votes[k] for k in same_side] + list(tells.values()) + x_ahead[0] + x_ahead[1] + x_out[0][AHEAD:] + x_out[1] + x_on[0] + x_on[1] + beside:
        c.wait_send()

    for c in answers.values():
        c.wait_recv()
    hub_best = jnp.maximum(jnp.maximum(gave[0], res[1]), jnp.maximum(res[2], res[3]))
    other_best = jnp.maximum(jnp.maximum(res[4], res[5]), jnp.maximum(res[6], res[7]))
    backs[0].wait_recv()
    cfull[:, :half] = jnp.maximum(jnp.where(inner, other_best, hub_best), cres[...])
    cfull[:, half:] = jnp.where(inner, hub_best, other_best)
    spread = jnp.broadcast_to(cfull[...], (128, rows)).T
    mine = jnp.where(deep.astype(f32) == target[...], jnp.concatenate([spread] * (rows // 128), axis=1), -1.0)
    out[...] = jnp.max(mine, axis=0, keepdims=True)


    @pl.when(inner)
    def _():
        for c in backs:
            c.wait_send()

    for c in answers.values():
        c.wait_send()


def per_device_meet(embeddings, cluster_id, order_index):
    rows, width = embeddings.shape
    half = rows // 2
    dma = pltpu.SemaphoreType.DMA
    vmem = pl.BlockSpec(memory_space=pltpu.VMEM)
    line = lambda k, m: pltpu.VMEM((k, 1, m), jnp.float32)
    block = lambda k, m: pltpu.VMEM((k, m, width), jnp.bfloat16)
    found = pl.pallas_call(
        meet_kernel,
        out_shape=jax.ShapeDtypeStruct((1, rows), jnp.float32),
        in_specs=[pl.BlockSpec(memory_space=pl.ANY), vmem, vmem],
        out_specs=vmem,
        scratch_shapes=[
            pltpu.VMEM((rows, width), jnp.bfloat16), dma, pltpu.VMEM((rows, width), jnp.bfloat16), block(4, rows),
            pltpu.VMEM((2 * SIDE, 2, rows), jnp.float32), line(SIDE * SIDE + 3, 128),
            block(2, half), pltpu.VMEM((half, width), jnp.bfloat16), block(2, half), block(2, AHEAD * half // PIECES), block(2, AHEAD * half // PIECES),
            block(3, half), pltpu.VMEM((4, 3, half), jnp.float32), pltpu.VMEM((4, 2, rows), jnp.float32),
            pltpu.VMEM((4, 2, half, 128), jnp.float32), pltpu.VMEM((2, half, 128), jnp.float32),
            pltpu.VMEM((1, rows), jnp.float32),
            line(4, rows), line(2 * SIDE, half), line(2 * SIDE, half), line(2, half), pltpu.VMEM((1, half), jnp.float32),
            pltpu.VMEM((1, rows), jnp.float32), pltpu.SemaphoreType.REGULAR((3,)),
            dma((SIDE * SIDE,)), dma((SIDE * SIDE,)), dma((2,)), dma, dma((2 * SIDE,)), dma((2 * SIDE,)),
            dma((2, PIECES)), dma((2, PIECES)), dma((2, AHEAD)), dma((2, AHEAD)), dma((2, AHEAD)), dma((2, AHEAD)),
            dma((2, PIECES)), dma((2, PIECES)), dma((2,)), dma((2,)),
            dma((PIECES,)), dma((PIECES,)), dma((2, PIECES)), dma((2, PIECES)), dma((2, PIECES)), dma((2, PIECES)),
            dma((2,)), dma((2,)), dma((2 * SIDE,)), dma((2 * SIDE,)), dma((2,)), dma,
        ],
        compiler_params=pltpu.CompilerParams(collective_id=0, has_side_effects=True, vmem_limit_bytes=56500000),
    )(embeddings, cluster_id.reshape(1, rows), order_index.reshape(1, rows))
    return jnp.maximum(found.reshape(rows), -1.0)


def solution(mesh):
    meet = mesh.shape["wide"] == SIDE and mesh.shape["narrow"] == SIDE
    return jax.shard_map(
        per_device_meet if meet else per_device,
        mesh=mesh,
        in_specs=(
            P(("parts", "wide", "narrow"), None),
            P(("parts", "wide", "narrow")),
            P(("parts", "wide", "narrow")),
        ),
        out_specs=P(("parts", "wide", "narrow")),
        check_vma=False,
    )
```
